32 devices in a mesh: lat: 2 (over y), lon: 16 (over z, x, core).
Axes of the slice: x: 2, y: 2, z: 4, core: 2. Of those that a mesh axis runs over, the one named last changes fastest.
Arguments:
- species_amounts: float32 [8, 64, 16, 128], P('lat', 'lon'), may hold values from 0.1 to 3
- thermal_anomaly: float32 [8, 64, 16], P('lat', 'lon'), may hold values from -1 to 1
- solar_flux_factor: float32 [8, 64], P('lat', 'lon'), may hold values from 0 to 1
- inner_iterations: int32 [8, 64], P('lat', 'lon'), may hold values from 4 to 36
- reference_speed: float32 [512], replicated, may hold values from 0.01 to 3
- thermal_response: float32 [512], replicated, may hold values from -1 to 1
- photo_breakup: float32 [512], replicated, may hold values from 0.03 to 3
- reaction_recipe: int32 [4, 512], replicated, may hold values from 0 to 127
- eastward_wind_ratio: float32 [16, 8, 64], P('lon', 'lat'), may hold values from -0.95 to 0.95
- northward_wind_ratio: float32 [16, 8, 64], P('lon', 'lat'), may hold values from -0.95 to 0.95
Outputs:
- transported: float32 [8, 64, 16, 128], P('lat', 'lon')
The draws below stay inside these ranges and needn't reach their ends.
Inputs may be any that keep to these rules, and one draw needn't show every extreme that they name: `reaction_recipe`: row 0 and row 1 name the two reactants of each reaction, rows 2 and 3 its two products.
All inputs are finite; a program needn't handle non-finite values.
Results may differ from the reference program's by a relative error of at most 0.0003.
Values sent between devices are 32-bit elements; how exact they have to be, the bound alone decides.
A program may use at most 64 MiB of HBM per device.

```python
import math
import jax
import jax.numpy as jnp
from jax import lax

S = 128
R = 512
MINSUB = 4
MAXSUB = 36
ADV_STEPS = 2
PARALLEL_TOTAL = 8
MERIDIAN_TOTAL = 64
ALTITUDE_LAYERS = 16


def draw_inner_iterations(key, part):
    dawn_key = jax.random.fold_in(key, 11)
    day_key = jax.random.fold_in(key, 12)
    night_key = jax.random.fold_in(key, 13)
    dawn_lon = jax.random.randint(dawn_key, (), 0, MERIDIAN_TOTAL)
    longitude = lax.broadcasted_iota(jnp.int32, (PARALLEL_TOTAL, MERIDIAN_TOTAL), 1)
    distance = (longitude - dawn_lon) % MERIDIAN_TOTAL
    sunlit = distance < MERIDIAN_TOTAL // 2
    day_count = jax.random.randint(day_key, (PARALLEL_TOTAL, MERIDIAN_TOTAL), 24, MAXSUB + 1)
    night_count = jax.random.randint(night_key, (PARALLEL_TOTAL, MERIDIAN_TOTAL), MINSUB, MINSUB + 3)
    counts = jnp.where(sunlit, day_count, night_count)
    counts = counts.at[0, dawn_lon].set(MAXSUB)
    counts = counts.at[0, (dawn_lon + MERIDIAN_TOTAL // 2) % MERIDIAN_TOTAL].set(MINSUB)
    return counts.astype(jnp.int32)


def place_ends(values, own_key, least, top_value):
    spot = [jax.random.randint(jax.random.fold_in(own_key, axis), (), 0, length) for axis, length in enumerate(values.shape)]
    longest = values.shape.index(max(values.shape))
    beside = spot[:longest] + [(spot[longest] + 1) % values.shape[longest]] + spot[longest + 1:]
    return values.at[tuple(spot)].set(least).at[tuple(beside)].set(top_value)


def block_levels(rng, dims, pieces, low, largest):
    loudness = 1.0
    for position, shards_of in pieces:
        steps = jax.random.uniform(jax.random.fold_in(jax.random.fold_in(rng, 6), position), (shards_of,), jnp.float32, low / len(pieces), largest / len(pieces))
        loudness = loudness * jnp.repeat(jnp.exp(steps), dims[position] // shards_of).reshape((-1,) + (1,) * (len(dims) - 1 - position))
    return loudness


def setup_inputs(seed: int = 0) -> dict:
    streams_of = jax.random.split(jax.random.key(seed), 11)
    species_amounts = jnp.clip(jnp.exp(math.log(3.0) - 3.4011974 * jax.random.uniform(streams_of[0], (PARALLEL_TOTAL, MERIDIAN_TOTAL, ALTITUDE_LAYERS, S), jnp.float32) ** block_levels(streams_of[0], (PARALLEL_TOTAL, MERIDIAN_TOTAL, ALTITUDE_LAYERS, S), ((0, 2), (1, 16)), -0.2, 0.2)), 0.1, 3.0)
    thermal_anomaly = jnp.clip(jax.random.uniform(streams_of[1], (PARALLEL_TOTAL, MERIDIAN_TOTAL, ALTITUDE_LAYERS), jnp.float32, -1.0, 1.0) * block_levels(streams_of[1], (PARALLEL_TOTAL, MERIDIAN_TOTAL, ALTITUDE_LAYERS), ((0, 2), (1, 16)), -0.4, 0.0), -1.0, 1.0)
    solar_flux_factor = jnp.clip(1.0 * jax.random.uniform(streams_of[2], (PARALLEL_TOTAL, MERIDIAN_TOTAL), jnp.float32) ** block_levels(streams_of[2], (PARALLEL_TOTAL, MERIDIAN_TOTAL), ((0, 2), (1, 16)), -0.2, 0.2), 0.0, 1.0)
    inner_iterations = draw_inner_iterations(jax.random.fold_in(streams_of[10], 71), 0)
    reference_speed = jnp.clip(jnp.exp(jax.random.uniform(streams_of[4], (R,), jnp.float32, math.log(0.01), math.log(3.0))), 0.01, 3.0)
    thermal_response = jnp.clip(jax.random.uniform(streams_of[5], (R,), jnp.float32, -1.0, 1.0), -1.0, 1.0)
    photo_breakup = jnp.clip(jnp.exp(jax.random.uniform(streams_of[6], (R,), jnp.float32, math.log(0.03), math.log(3.0))), 0.03, 3.0)
    reaction_recipe = place_ends(jax.random.randint(streams_of[7], (4, R), 0, S), jax.random.fold_in(streams_of[7], 1), 0, S - 1).astype(jnp.int32)
    eastward_wind_ratio = jnp.clip(jax.random.uniform(streams_of[8], (ALTITUDE_LAYERS, PARALLEL_TOTAL, MERIDIAN_TOTAL), jnp.float32, -0.95, 0.95) * block_levels(streams_of[8], (ALTITUDE_LAYERS, PARALLEL_TOTAL, MERIDIAN_TOTAL), ((0, 16), (1, 2)), -0.4, 0.0), -0.95, 0.95)
    northward_wind_ratio = jnp.clip(jax.random.uniform(streams_of[9], (ALTITUDE_LAYERS, PARALLEL_TOTAL, MERIDIAN_TOTAL), jnp.float32, -0.95, 0.95) * block_levels(streams_of[9], (ALTITUDE_LAYERS, PARALLEL_TOTAL, MERIDIAN_TOTAL), ((0, 16), (1, 2)), -0.4, 0.0), -0.95, 0.95)
    return {"species_amounts": species_amounts, "thermal_anomaly": thermal_anomaly, "solar_flux_factor": solar_flux_factor, "inner_iterations": inner_iterations, "reference_speed": reference_speed, "thermal_response": thermal_response, "photo_breakup": photo_breakup, "reaction_recipe": reaction_recipe, "eastward_wind_ratio": eastward_wind_ratio, "northward_wind_ratio": northward_wind_ratio}


def slice_axis(array, start, count, along):
    return lax.slice_in_dim(array, start, start + count, axis=along)


def flux_sweep(padded, courant_pad, along, length):
    far_left = slice_axis(padded, 0, length + 3, along)
    near_left = slice_axis(padded, 1, length + 3, along)
    near_right = slice_axis(padded, 2, length + 3, along)
    far_right = slice_axis(padded, 3, length + 3, along)
    edges = (7.0 / 12.0) * (near_left + near_right) - (1.0 / 12.0) * (far_left + far_right)
    edges = jnp.minimum(jnp.maximum(edges, jnp.minimum(near_left, near_right)), jnp.maximum(near_left, near_right))
    cell_means = slice_axis(padded, 2, length + 2, along)
    left_edge = slice_axis(edges, 0, length + 2, along)
    right_edge = slice_axis(edges, 1, length + 2, along)
    edge_jump = right_edge - left_edge
    curvature = 6.0 * cell_means - 3.0 * (left_edge + right_edge)
    courant = slice_axis(courant_pad, 3, length + 1, along)
    magnitude = jnp.abs(courant)
    from_left = slice_axis(right_edge, 0, length + 1, along) - 0.5 * courant * (
        slice_axis(edge_jump, 0, length + 1, along)
        - (1.0 - (2.0 / 3.0) * courant) * slice_axis(curvature, 0, length + 1, along))
    from_right = slice_axis(left_edge, 1, length + 1, along) + 0.5 * magnitude * (
        slice_axis(edge_jump, 1, length + 1, along)
        + (1.0 - (2.0 / 3.0) * magnitude) * slice_axis(curvature, 1, length + 1, along))
    face_flux = courant * jnp.where(courant >= 0.0, from_left, from_right)
    interior = slice_axis(padded, 3, length, along)
    return interior - (slice_axis(face_flux, 1, length, along) - slice_axis(face_flux, 0, length, along))


def wrap_pad(array, along):
    extent = array.shape[along]
    return jnp.concatenate([slice_axis(array, extent - 3, 3, along), array, slice_axis(array, 0, 3, along)], axis=along)


def zero_pad(array, along):
    widths = [(0, 0)] * array.ndim
    widths[along] = (3, 3)
    return jnp.pad(array, widths)


def reference(species_amounts, thermal_anomaly, solar_flux_factor, inner_iterations, reference_speed, thermal_response, photo_breakup, reaction_recipe, eastward_wind_ratio, northward_wind_ratio):
    species = species_amounts.shape[-1]

    def lone_parallel(inputs):
        conc_row, warmth_strip, sun_row, count_row = inputs
        local_warmth = warmth_strip.reshape(1, -1)
        local_irradiance = jnp.broadcast_to(sun_row[:, None], warmth_strip.shape).reshape(1, -1)
        speed_coefficient = reference_speed[:, None] * jnp.exp(thermal_response[:, None] * local_warmth) + photo_breakup[:, None] * local_irradiance
        mesh_box_total = jnp.broadcast_to(count_row[:, None], warmth_strip.shape).reshape(1, -1)
        substep = 1.0 / mesh_box_total.astype(jnp.float32)
        start = conc_row.reshape(-1, species).T

        def advance(step_index, current):
            first_conc = current[reaction_recipe[0]]
            second_conc = current[reaction_recipe[1]]
            reaction_flow = speed_coefficient * first_conc * second_conc
            produced = jax.ops.segment_sum(reaction_flow, reaction_recipe[2], species) + jax.ops.segment_sum(reaction_flow, reaction_recipe[3], species)
            lost_rate = jax.ops.segment_sum(speed_coefficient * second_conc, reaction_recipe[0], species) + jax.ops.segment_sum(speed_coefficient * first_conc, reaction_recipe[1], species)
            updated = (current + substep * produced) / (1.0 + substep * lost_rate)
            return jnp.where(step_index < mesh_box_total, updated, current)

        result = lax.fori_loop(0, MAXSUB, advance, start)
        return result.T.reshape(conc_row.shape)

    carried_quantity = lax.map(lone_parallel, (species_amounts, thermal_anomaly, solar_flux_factor, inner_iterations))
    east_faces = jnp.transpose(eastward_wind_ratio, (1, 2, 0))[..., None]
    row_ids = lax.broadcasted_iota(jnp.int32, (carried_quantity.shape[0], 1, 1, 1), 0)
    south_faces = jnp.where(row_ids > 0, jnp.transpose(northward_wind_ratio, (1, 2, 0))[..., None], 0.0)
    east_pad = wrap_pad(east_faces, 1)
    south_pad = zero_pad(south_faces, 0)
    for sweep_index in range(ADV_STEPS):
        carried_quantity = flux_sweep(wrap_pad(carried_quantity, 1), east_pad, 1, carried_quantity.shape[1])
        carried_quantity = flux_sweep(zero_pad(carried_quantity, 0), south_pad, 0, carried_quantity.shape[0])
    return carried_quantity
```

```python
import functools
import jax
import jax.numpy as jnp
from jax import lax
from jax.experimental import pallas as pl
from jax.experimental.pallas import tpu as pltpu
from jax.sharding import PartitionSpec as P

ADV_STEPS = 2
FAST_LEAST = 1e-12
FAST_MOST = 1e8
HIGHEST = lax.Precision.HIGHEST
MOST_SUBSTEPS = 36
FLOOR = 1e-20
FLOOR_LOG = -66.43856


def with_halo(block, sides, width):
    for axis, dim in sides:
        count = lax.axis_size(axis)
        forward = [(i, i + 1) for i in range(count - 1)]
        backward = [(target, source) for source, target in forward]
        low = lax.ppermute(
            lax.slice_in_dim(block, block.shape[dim] - width, None, axis=dim), axis, forward
        )
        high = lax.ppermute(lax.slice_in_dim(block, 0, width, axis=dim), axis, backward)
        block = jnp.concatenate([low, block, high], axis=dim)
    return block


def slice_axis(array, start, count, along):
    return lax.slice_in_dim(array, start, start + count, axis=along)


def flux_sweep(padded, courant_pad, along, length):
    far_left = slice_axis(padded, 0, length + 3, along)
    near_left = slice_axis(padded, 1, length + 3, along)
    near_right = slice_axis(padded, 2, length + 3, along)
    far_right = slice_axis(padded, 3, length + 3, along)
    edges = 7.0 / 12.0 * (near_left + near_right) - 1.0 / 12.0 * (far_left + far_right)
    edges = jnp.minimum(
        jnp.maximum(edges, jnp.minimum(near_left, near_right)), jnp.maximum(near_left, near_right)
    )
    cell_means = slice_axis(padded, 2, length + 2, along)
    left_edge = slice_axis(edges, 0, length + 2, along)
    right_edge = slice_axis(edges, 1, length + 2, along)
    edge_jump = right_edge - left_edge
    curvature = 6.0 * cell_means - 3.0 * (left_edge + right_edge)
    courant = slice_axis(courant_pad, 3, length + 1, along)
    magnitude = jnp.abs(courant)
    from_left = slice_axis(right_edge, 0, length + 1, along) - 0.5 * courant * (
        slice_axis(edge_jump, 0, length + 1, along)
        - (1.0 - 2.0 / 3.0 * courant) * slice_axis(curvature, 0, length + 1, along)
    )
    from_right = slice_axis(left_edge, 1, length + 1, along) + 0.5 * magnitude * (
        slice_axis(edge_jump, 1, length + 1, along)
        + (1.0 - 2.0 / 3.0 * magnitude) * slice_axis(curvature, 1, length + 1, along)
    )
    face_flux = courant * jnp.where(courant >= 0.0, from_left, from_right)
    interior = slice_axis(padded, 3, length, along)
    return interior - (
        slice_axis(face_flux, 1, length, along) - slice_axis(face_flux, 0, length, along)
    )


def wrap_pad(array, along):
    extent = array.shape[along]
    return jnp.concatenate(
        [slice_axis(array, extent - 3, 3, along), array, slice_axis(array, 0, 3, along)], axis=along
    )


def two_halves(values):
    high = values.astype(jnp.bfloat16)
    low = (values - high.astype(jnp.float32)).astype(jnp.bfloat16)
    return jnp.concatenate([high, low], axis=1)


def dot32(left, right, dims=((1,), (0,)), precision=None):
    return lax.dot_general(
        left, right, (dims, ((), ())), precision=precision, preferred_element_type=jnp.float32
    )


def chem_kernel(*refs):
    sources, (out, rates, pick, spread, state, least, most, warmth) = refs[:8], refs[8:16]
    amounts, anomaly, solar, counts, speed, response, photo, recipe = held = refs[16:24]
    copies = [
        pltpu.make_async_copy(source, here, refs[24].at[index])
        for index, (source, here) in enumerate(zip(sources, held))
    ]
    for copy in copies:
        copy.start()
    for copy in copies:
        copy.wait()
    rows, columns, levels = anomaly.shape
    cells, species = state.shape
    width = rows * columns
    chunks = rates.shape[0]
    for row in range(rows):
        warmth[row * columns : (row + 1) * columns, :] = anomaly[row]
    place = lax.broadcasted_iota(jnp.int32, (width, species), 0)
    sunlight = jnp.zeros((width, species), jnp.float32)
    count = jnp.zeros((width, species), jnp.int32)
    longest = jnp.int32(0)
    for column in range(width):
        here = place == column
        spot = (column // columns, column % columns)
        sunlight = jnp.where(here, solar[spot], sunlight)
        count = jnp.where(here, counts[spot], count)
        longest = jnp.maximum(longest, counts[spot])
    ids = lax.broadcasted_iota(jnp.int32, (species, species), 0)
    for chunk in range(chunks):
        part = pl.ds(chunk * species, species)
        hits = [
            (recipe[row : row + 1, part] == ids).astype(jnp.float32) for row in range(4)
        ]
        taking = jnp.concatenate([hits[0], hits[1]], axis=1).astype(jnp.bfloat16)
        pick[chunk] = jnp.concatenate([taking, taking], axis=0)
        giving = jnp.concatenate(
            [jnp.transpose(hits[2] + hits[3]), jnp.transpose(hits[0] + hits[1])], axis=1
        ).astype(jnp.bfloat16)
        spread[chunk] = jnp.concatenate([giving, giving], axis=0)
    for level in range(levels):
        block = pl.ds(level * width, width)
        heat = jnp.broadcast_to(warmth[:, level : level + 1], (width, species))
        for chunk in range(chunks):
            part = pl.ds(chunk * species, species)
            rates[chunk, block, :] = (
                speed[:, part] * jnp.exp(response[:, part] * heat) + photo[:, part] * sunlight
            )

    def start():
        for level in range(levels):
            state[pl.ds(level * width, width), :] = amounts[pl.ds(level, width, stride=levels), :]

    def tiled(values):
        return jnp.concatenate([values] * levels, axis=0)

    start()
    substep = 1.0 / count.astype(jnp.float32)
    least[...] = state[...]
    most[...] = state[...]

    def advance(step, carry):
        current = state[...]
        least[...] = jnp.minimum(least[...], current)
        most[...] = jnp.maximum(most[...], current)
        pair = two_halves(current)
        flows = []
        for chunk in range(chunks):
            taken = dot32(pair, pick[chunk])
            flows.append(two_halves(rates[chunk] * taken[:, :species] * taken[:, species:]))
        total = dot32(jnp.concatenate(flows, axis=1), spread[...].reshape(-1, 2 * species))
        produced = total[:, :species]
        consumed = total[:, species:]
        size = tiled(substep)
        updated = (current + size * produced) / (current + size * consumed) * current
        state[...] = jnp.where(tiled(count) > step, updated, current)
        return carry

    lax.fori_loop(0, longest, advance, 0)
    usual = (jnp.min(least[...]) >= FAST_LEAST) & (jnp.max(most[...]) <= FAST_MOST)

    @pl.when(jnp.logical_not(usual))
    def _():
        start()

        def advance_fully(step, carry):
            current = state[...]
            produced = jnp.zeros((cells, species), jnp.float32)
            lost = jnp.zeros((cells, species), jnp.float32)
            for chunk in range(chunks):
                first_hit = pick[chunk, :species, :species].astype(jnp.float32)
                second_hit = pick[chunk, :species, species:].astype(jnp.float32)
                making = spread[chunk, :species, :species].astype(jnp.float32)
                first = dot32(current, first_hit, precision=HIGHEST)
                second = dot32(current, second_hit, precision=HIGHEST)
                rate = rates[chunk]
                produced += dot32(rate * first * second, making, precision=HIGHEST)
                lost += dot32(rate * second, first_hit, ((1,), (1,)), HIGHEST)
                lost += dot32(rate * first, second_hit, ((1,), (1,)), HIGHEST)
            size = tiled(substep)
            updated = (current + size * produced) / (1.0 + size * lost)
            state[...] = jnp.where(tiled(count) > step, updated, current)
            return carry

        lax.fori_loop(0, longest, advance_fully, 0)

    for level in range(levels):
        out[pl.ds(level, width, stride=levels), :] = state[pl.ds(level * width, width), :]


def react(operands):
    cells, species = operands[0].shape
    rows, columns, levels = operands[1].shape
    chunks = operands[7].shape[1] // species
    in_vmem = pl.BlockSpec(memory_space=pltpu.VMEM)
    held = [
        (pltpu.SMEM if index in (2, 3) else pltpu.VMEM)(operand.shape, operand.dtype)
        for index, operand in enumerate(operands)
    ]
    table = pltpu.VMEM((chunks, 2 * species, 2 * species), jnp.bfloat16)
    field = pltpu.VMEM((cells, species), jnp.float32)
    return pl.pallas_call(
        chem_kernel,
        out_shape=jax.ShapeDtypeStruct((cells, species), jnp.float32),
        in_specs=[pl.BlockSpec(memory_space=pltpu.HBM)] * len(operands),
        out_specs=in_vmem,
        scratch_shapes=[
            pltpu.VMEM((chunks, cells, species), jnp.float32), table, table,
            field, field, field, pltpu.VMEM((rows * columns, levels), jnp.float32),
            *held, pltpu.SemaphoreType.DMA((len(operands),)),
        ],
        compiler_params=pltpu.CompilerParams(vmem_limit_bytes=67043328),
    )(*operands)


def others(bands, devices):
    return [(dy, dl) for dl in range(devices) for dy in range(bands) if (dy, dl) != (0, 0)]


def peer(bands, devices, dy, dl):
    band, block = lax.axis_index("lat"), lax.axis_index("lon")
    return (lax.rem(band + dy, bands), lax.rem(block + dl, devices))


def signal_peers(bands, devices):
    barrier = pltpu.get_barrier_semaphore()
    for dy, dl in others(bands, devices):
        pl.semaphore_signal(
            barrier, inc=1, device_id=peer(bands, devices, dy, dl),
            device_id_type=pl.DeviceIdType.MESH,
        )


def wrap_rows(buffer, slot, values, half):
    extent = values.shape[0]
    buffer[slot, 8 : 8 + extent, :] = values
    buffer[slot, 0:8, :] = pltpu.roll(values[extent - 8 :], half, 1)
    buffer[slot, 8 + extent : 16 + extent, :] = pltpu.roll(values[:8], half, 1)


def clipped_edge(far_left, near_left, near_right, far_right):
    edge = 7.0 / 12.0 * (near_left + near_right) - 1.0 / 12.0 * (far_left + far_right)
    return jnp.minimum(
        jnp.maximum(edge, jnp.minimum(near_left, near_right)), jnp.maximum(near_left, near_right)
    )


def face_flow(courant, before, edge, after, left_mean, right_mean):
    magnitude = jnp.abs(courant)
    rightward = courant >= 0.0
    other = jnp.where(rightward, before, after)
    mean = jnp.where(rightward, left_mean, right_mean)
    bend = 6.0 * mean - 3.0 * (other + edge)
    return courant * (
        edge + 0.5 * magnitude * ((other - edge) + (1.0 - 2.0 / 3.0 * magnitude) * bend)
    )


def move_kernel(
    bands, devices, packed, east, north, out,
    inbox, outbox, back, wind_out, wind_in, courants, grid, edges,
    send_there, recv_there, send_wind, recv_wind, send_back, recv_back,
):
    band, block = lax.axis_index("lat"), lax.axis_index("lon")
    _, rows, longitudes = east.shape
    levels, _, _, species = packed.shape
    half = species // 2
    columns = longitudes // devices
    extent = longitudes // 2
    lats = bands * rows
    low_rows = rows // 2
    offsets = others(bands, devices)

    def remote(source, target, send_sem, recv_sem, device):
        return pltpu.make_async_remote_copy(
            src_ref=source, dst_ref=target, send_sem=send_sem, recv_sem=recv_sem,
            device_id=device, device_id_type=pl.DeviceIdType.MESH,
        )

    wind_out[...] = jnp.zeros_like(wind_out)
    wind_out[0:rows, 0:longitudes] = east[0]
    wind_out[rows : 2 * rows, 0:longitudes] = north[0]
    wind_in[band] = wind_out[...]
    inbox[band, block] = packed[block, band]
    pl.semaphore_wait(pltpu.get_barrier_semaphore(), len(offsets))

    winds = []
    for dy in range(1, bands):
        copy = remote(
            wind_out, wind_in.at[band], send_wind.at[dy], recv_wind.at[dy],
            peer(bands, devices, dy, 0),
        )
        copy.start()
        winds.append(copy)
    moves = []
    for index, (dy, dl) in enumerate(offsets):
        device = peer(bands, devices, dy, dl)
        copy = remote(
            packed.at[device[1], device[0]], inbox.at[band, block],
            send_there.at[index], recv_there.at[index], device,
        )
        copy.start()
        moves.append(copy)

    for copy in winds:
        copy.wait()
    near_tall = lax.broadcasted_iota(jnp.int32, (extent, species), 1) < half
    wide = wind_out.shape[1]
    tall = [wind_in[y] for y in range(bands)]
    tall.append(jnp.zeros((wide - bands * 2 * rows, wide), jnp.float32))
    turned = jnp.transpose(jnp.concatenate(tall, axis=0))
    for lat in range(lats):
        for kind in range(2):
            lane = lat // rows * 2 * rows + kind * rows + lat % rows
            courants[kind, lat] = jnp.where(
                near_tall,
                jnp.broadcast_to(turned[0:extent, lane : lane + 1], (extent, species)),
                jnp.broadcast_to(turned[extent : 2 * extent, lane : lane + 1], (extent, species)),
            )
    for copy in moves:
        copy.wait()

    near = lax.broadcasted_iota(jnp.int32, (low_rows * columns, species), 1) < half

    def swap_pair(first, second):
        return (
            jnp.where(near, first, pltpu.roll(second, half, 1)),
            jnp.where(near, pltpu.roll(first, half, 1), second),
        )

    for y in range(bands):
        for spot in range(devices // 2):
            pair = swap_pair(inbox[y, spot], inbox[y, spot + devices // 2])
            for high in range(2):
                for low in range(low_rows):
                    lat = y * rows + high * low_rows + low
                    grid[lat, 8 + spot * columns : 8 + (spot + 1) * columns, :] = pair[high][
                        low * columns : (low + 1) * columns
                    ]
    planes = [grid[lat, 8 : 8 + extent, :] for lat in range(lats)]
    empty = jnp.zeros((extent, species), jnp.float32)
    for sweep_index in range(ADV_STEPS):
        swept = []
        for lat in range(lats):
            mean = planes[lat]
            wrap_rows(grid, lat, mean, half)

            def shifted(buffer, shift):
                return buffer[lat, 8 + shift : 8 + shift + extent, :]

            left_mean = shifted(grid, -1)
            edge = clipped_edge(shifted(grid, -2), left_mean, mean, shifted(grid, 1))
            wrap_rows(edges, lat, edge, half)
            flow = face_flow(
                courants[0, lat], shifted(edges, -1), edge, shifted(edges, 1), left_mean, mean
            )
            wrap_rows(grid, lat, flow, half)
            swept.append(mean - (shifted(grid, 1) - flow))
        padded = [empty, empty] + swept + [empty, empty]
        rims = [clipped_edge(*padded[lat : lat + 4]) for lat in range(lats + 1)]
        flows = [
            face_flow(
                courants[1, lat], rims[lat - 1], rims[lat], rims[lat + 1],
                swept[lat - 1], swept[lat],
            )
            for lat in range(1, lats)
        ]
        flows = [empty] + flows + [empty]
        planes = [swept[lat] - (flows[lat + 1] - flows[lat]) for lat in range(lats)]
    for lat in range(lats):
        grid[lat, 8 : 8 + extent, :] = planes[lat]
    for y in range(bands):
        for spot in range(devices // 2):
            sides = [
                jnp.concatenate(
                    [
                        grid[
                            y * rows + high * low_rows + low,
                            8 + spot * columns : 8 + (spot + 1) * columns,
                            :,
                        ]
                        for low in range(low_rows)
                    ],
                    axis=0,
                )
                for high in range(2)
            ]
            outbox[y, spot], outbox[y, spot + devices // 2] = swap_pair(*sides)
    back[block, band] = outbox[band, block]
    moves = []
    for index, (dy, dl) in enumerate(offsets):
        device = peer(bands, devices, dy, dl)
        copy = remote(
            outbox.at[device[0], device[1]], back.at[block, band],
            send_back.at[index], recv_back.at[index], device,
        )
        copy.start()
        moves.append(copy)
    for copy in moves:
        copy.wait()
    count = low_rows * columns
    for level in range(levels):
        front, behind = swap_pair(back[level, 0], back[level, 1])
        out[pl.ds(level, count, stride=levels), :] = front
        out[pl.ds(count * levels + level, count, stride=levels), :] = behind


def halves(values):
    high = values.astype(jnp.bfloat16)
    return high, (values - high.astype(jnp.float32)).astype(jnp.bfloat16)


def substeps(groups, state, number, log_rates, pick, spread, *results):
    sides = range(2)
    gathered = [results[side * groups : (side + 1) * groups] for side in sides]
    scattered = [results[(2 + side) * groups : (3 + side) * groups] for side in sides]
    tall = state.shape[0] // groups
    species = state.shape[1]

    def load_pick():
        for side in sides:
            pltpu.matmul_push_rhs(pick[side], 0, side)

    def load_spread():
        for side in sides:
            pltpu.matmul_push_rhs(spread[side], 1, side)

    def gather(group, logs):
        pair = jnp.concatenate(halves(jnp.maximum(logs, FLOOR_LOG)), axis=1)
        for side in sides:
            pltpu.matmul_acc_lhs(
                gathered[side][group], pair, load_staged_rhs=None if group else 0
            )

    load_pick()
    for group in range(groups):
        gather(group, jnp.log2(state[group * tall : (group + 1) * tall, :]))
    load_spread()

    def advance(step, carry):
        for group in range(groups):
            block = slice(group * tall, (group + 1) * tall)
            for side in sides:
                logs = pltpu.matmul_pop(gathered[side][group]) + log_rates[side, block, :]
                high, low = halves(jnp.exp2(logs))
                pltpu.matmul_acc_lhs(
                    scattered[side][group], high, load_staged_rhs=None if group else 1
                )
                pltpu.matmul_acc_lhs(scattered[side][group], low)
        load_pick()
        load_spread()
        for group in range(groups):
            block = slice(group * tall, (group + 1) * tall)
            total = pltpu.matmul_pop(scattered[0][group]) + pltpu.matmul_pop(scattered[1][group])
            current, count = state[block, :], number[block, :]
            above = count * current + total[:, :species]
            below = count + total[:, species:] * (1.0 / jnp.maximum(current, FLOOR))
            gather(group, jnp.log2(above) - jnp.log2(below))
            state[block, :] = jnp.where(count > step.astype(jnp.float32), above / below, current)
        return carry

    lax.fori_loop(0, MOST_SUBSTEPS, advance, 0)
    for side in sides:
        for group in range(groups):
            pltpu.matmul_pop(gathered[side][group])
        pltpu.matmul_acc_lhs(
            scattered[side][0], jnp.zeros((tall, 2 * species), jnp.bfloat16), load_staged_rhs=1
        )
        pltpu.matmul_pop(scattered[side][0])


def whole_kernel(bands, devices, *refs):
    sources, out = refs[:10], refs[10]
    amounts, anomaly, solar, counts, speed, response, photo, recipe, east, north = held = refs[11:21]
    log_rates, pick, spread, state, number, warmth, arrived, packed = refs[21:29]
    move_refs = refs[29:]
    width = warmth.shape[0]
    cells, species = state.shape
    levels = cells // width

    signal_peers(bands, devices)
    copies = [
        pltpu.make_async_copy(source, here, arrived.at[index])
        for index, (source, here) in enumerate(zip(sources, held))
    ]
    for copy in copies:
        copy.start()
    for copy in copies:
        copy.wait()
    rows, columns, _ = anomaly.shape
    for row in range(rows):
        warmth[row * columns : (row + 1) * columns, :] = anomaly[row]
    place = lax.broadcasted_iota(jnp.int32, (width, species), 0)
    sunlight = jnp.zeros((width, species), jnp.float32)
    count = jnp.zeros((width, species), jnp.int32)
    for column in range(width):
        here = place == column
        spot = (column // columns, column % columns)
        sunlight = jnp.where(here, solar[spot], sunlight)
        count = jnp.where(here, counts[spot], count)
    count = count.astype(jnp.float32)
    ids = lax.broadcasted_iota(jnp.int32, (species, species), 0)
    for chunk in range(4):
        part = pl.ds(chunk * species, species)
        hits = [(recipe[row : row + 1, part] == ids).astype(jnp.float32) for row in range(4)]
        taking, giving = hits[0] + hits[1], hits[2] + hits[3]
        side, spot = chunk // 2, chunk % 2 * species
        for copy in range(2):
            pick[side, copy * species : (copy + 1) * species, spot : spot + species] = (
                taking.astype(jnp.bfloat16)
            )
        spread[side, spot : spot + species, :] = jnp.concatenate(
            [jnp.transpose(giving), jnp.transpose(taking)], axis=1
        ).astype(jnp.bfloat16)
    for level in range(levels):
        block = pl.ds(level * width, width)
        heat = jnp.broadcast_to(warmth[:, level : level + 1], (width, species))
        for chunk in range(4):
            part = pl.ds(chunk * species, species)
            log_rates[chunk // 2, block, chunk % 2 * species : (chunk % 2 + 1) * species] = jnp.log2(
                speed[:, part] * jnp.exp(response[:, part] * heat) + photo[:, part] * sunlight
            )
        state[block, :] = amounts[pl.ds(level, width, stride=levels), :]
        number[block, :] = count

    groups = cells // 32
    pl.run_scoped(
        functools.partial(substeps, groups, state, number, log_rates, pick, spread),
        *[
            pltpu.ACC(side)((32, 2 * species), jnp.float32)
            for use in range(2)
            for side in range(2)
            for group in range(groups)
        ],
    )

    half = species // 2
    near = lax.broadcasted_iota(jnp.int32, (width // 2, species), 1) < half
    for level in range(levels):
        front = state[pl.ds(level * width, width // 2), :]
        behind = state[pl.ds(level * width + width // 2, width // 2), :]
        packed[level, 0] = jnp.where(near, front, pltpu.roll(behind, half, 1))
        packed[level, 1] = jnp.where(near, pltpu.roll(front, half, 1), behind)
    move_kernel(bands, devices, packed, east, north, out, *move_refs)


def react_and_advect(operands):
    bands, devices = lax.axis_size("lat"), lax.axis_size("lon")
    cells, species = operands[0].shape
    rows, columns, levels = operands[1].shape
    longitudes = operands[8].shape[2]
    lats, extent, count = bands * rows, longitudes // 2, rows * columns // 2
    wide = -(-longitudes // 128) * 128
    held = [
        (pltpu.SMEM if index in (2, 3) else pltpu.VMEM)(operand.shape, operand.dtype)
        for index, operand in enumerate(operands)
    ]
    semaphores = pltpu.SemaphoreType.DMA((bands * devices - 1,))
    wind_semaphores = pltpu.SemaphoreType.DMA((bands,))
    box = pltpu.VMEM((bands, devices, count, species), jnp.float32)
    exchanged = pltpu.VMEM((levels, bands, count, species), jnp.float32)
    wrapped = pltpu.VMEM((lats, extent + 16, species), jnp.float32)
    table = pltpu.VMEM((2, 2 * species, 2 * species), jnp.bfloat16)
    field = pltpu.VMEM((cells, species), jnp.float32)
    return pl.pallas_call(
        functools.partial(whole_kernel, bands, devices),
        out_shape=jax.ShapeDtypeStruct((cells, species), jnp.float32),
        in_specs=[pl.BlockSpec(memory_space=pltpu.HBM)] * len(operands),
        out_specs=pl.BlockSpec(memory_space=pltpu.VMEM),
        scratch_shapes=[
            *held,
            pltpu.VMEM((2, cells, 2 * species), jnp.float32), table, table, field, field,
            pltpu.VMEM((rows * columns, levels), jnp.float32),
            pltpu.SemaphoreType.DMA((len(operands),)), exchanged,
            box, box, exchanged,
            pltpu.VMEM((2 * rows, wide), jnp.float32),
            pltpu.VMEM((bands, 2 * rows, wide), jnp.float32),
            pltpu.VMEM((2, lats, extent, species), jnp.float32), wrapped, wrapped,
            semaphores, semaphores, wind_semaphores, wind_semaphores, semaphores, semaphores,
        ],
        compiler_params=pltpu.CompilerParams(
            collective_id=0, has_side_effects=True, vmem_limit_bytes=32 << 20
        ),
    )(*operands)


def per_device(
    species_amounts,
    thermal_anomaly,
    solar_flux_factor,
    inner_iterations,
    reference_speed,
    thermal_response,
    photo_breakup,
    reaction_recipe,
    eastward_wind_ratio,
    northward_wind_ratio,
):
    rows, columns, levels, species = species_amounts.shape
    devices = lax.axis_size("lon")
    longitudes = eastward_wind_ratio.shape[2]
    reactions = reaction_recipe.shape[1]
    operands = (
        species_amounts.reshape(-1, species), thermal_anomaly, solar_flux_factor,
        inner_iterations, reference_speed.reshape(1, -1), thermal_response.reshape(1, -1),
        photo_breakup.reshape(1, -1), reaction_recipe,
    )
    paired = lax.axis_size("lat") == 2 and levels == devices and rows % 2 == 0
    tabled = species == 128 and reactions == 4 * species and rows * columns % 16 == 0
    if paired and tabled and devices % 2 == 0 and longitudes <= 128:
        moved = react_and_advect((*operands, eastward_wind_ratio, northward_wind_ratio))
        return moved.reshape(species_amounts.shape)
    settled_columns = react(operands).reshape(species_amounts.shape)
    lat_rows = species_amounts.shape[0]
    row_ids = lax.axis_index("lat") * lat_rows + lax.broadcasted_iota(
        jnp.int32, (lat_rows, 1, 1, 1), 0
    )
    carried_quantity = lax.all_to_all(
        settled_columns, "lon", split_axis=2, concat_axis=1, tiled=True
    )
    east_faces = jnp.transpose(eastward_wind_ratio, (1, 2, 0))[..., None]
    south_faces = jnp.where(
        row_ids > 0, jnp.transpose(northward_wind_ratio, (1, 2, 0))[..., None], 0.0
    )
    east_pad = wrap_pad(east_faces, 1)
    for sweep_index in range(ADV_STEPS):
        carried_quantity = flux_sweep(
            wrap_pad(carried_quantity, 1), east_pad, 1, carried_quantity.shape[1]
        )
        rimmed, south_pad = (
            with_halo(carried_quantity, (("lat", 0),), 3),
            with_halo(south_faces, (("lat", 0),), 3),
        )
        carried_quantity = flux_sweep(rimmed, south_pad, 0, lat_rows)
    return lax.all_to_all(carried_quantity, "lon", split_axis=1, concat_axis=2, tiled=True)


def solution(mesh):
    return jax.shard_map(
        per_device,
        mesh=mesh,
        in_specs=(
            P("lat", "lon", None, None),
            P("lat", "lon", None),
            P("lat", "lon"),
            P("lat", "lon"),
            P(),
            P(),
            P(),
            P(),
            P("lon", "lat", None),
            P("lon", "lat", None),
        ),
        out_specs=P("lat", "lon", None, None),
        check_vma=False,
    )
```

```python
import functools
import jax
import jax.numpy as jnp
from jax import lax
from jax.experimental import pallas as pl
from jax.experimental.pallas import tpu as pltpu
from jax.sharding import PartitionSpec as P

ADV_STEPS = 2
FAST_LEAST = 1e-12
FAST_MOST = 1e8
HIGHEST = lax.Precision.HIGHEST
MOST_SUBSTEPS = 36
FLOOR = 1e-20
FLOOR_LOG = -66.43856


def with_halo(block, sides, width):
    for axis, dim in sides:
        count = lax.axis_size(axis)
        forward = [(i, i + 1) for i in range(count - 1)]
        backward = [(target, source) for source, target in forward]
        low = lax.ppermute(
            lax.slice_in_dim(block, block.shape[dim] - width, None, axis=dim), axis, forward
        )
        high = lax.ppermute(lax.slice_in_dim(block, 0, width, axis=dim), axis, backward)
        block = jnp.concatenate([low, block, high], axis=dim)
    return block


def slice_axis(array, start, count, along):
    return lax.slice_in_dim(array, start, start + count, axis=along)


def flux_sweep(padded, courant_pad, along, length):
    far_left = slice_axis(padded, 0, length + 3, along)
    near_left = slice_axis(padded, 1, length + 3, along)
    near_right = slice_axis(padded, 2, length + 3, along)
    far_right = slice_axis(padded, 3, length + 3, along)
    edges = 7.0 / 12.0 * (near_left + near_right) - 1.0 / 12.0 * (far_left + far_right)
    edges = jnp.minimum(
        jnp.maximum(edges, jnp.minimum(near_left, near_right)), jnp.maximum(near_left, near_right)
    )
    cell_means = slice_axis(padded, 2, length + 2, along)
    left_edge = slice_axis(edges, 0, length + 2, along)
    right_edge = slice_axis(edges, 1, length + 2, along)
    edge_jump = right_edge - left_edge
    curvature = 6.0 * cell_means - 3.0 * (left_edge + right_edge)
    courant = slice_axis(courant_pad, 3, length + 1, along)
    magnitude = jnp.abs(courant)
    from_left = slice_axis(right_edge, 0, length + 1, along) - 0.5 * courant * (
        slice_axis(edge_jump, 0, length + 1, along)
        - (1.0 - 2.0 / 3.0 * courant) * slice_axis(curvature, 0, length + 1, along)
    )
    from_right = slice_axis(left_edge, 1, length + 1, along) + 0.5 * magnitude * (
        slice_axis(edge_jump, 1, length + 1, along)
        + (1.0 - 2.0 / 3.0 * magnitude) * slice_axis(curvature, 1, length + 1, along)
    )
    face_flux = courant * jnp.where(courant >= 0.0, from_left, from_right)
    interior = slice_axis(padded, 3, length, along)
    return interior - (
        slice_axis(face_flux, 1, length, along) - slice_axis(face_flux, 0, length, along)
    )


def wrap_pad(array, along):
    extent = array.shape[along]
    return jnp.concatenate(
        [slice_axis(array, extent - 3, 3, along), array, slice_axis(array, 0, 3, along)], axis=along
    )


def two_halves(values):
    high = values.astype(jnp.bfloat16)
    low = (values - high.astype(jnp.float32)).astype(jnp.bfloat16)
    return jnp.concatenate([high, low], axis=1)


def dot32(left, right, dims=((1,), (0,)), precision=None):
    return lax.dot_general(
        left, right, (dims, ((), ())), precision=precision, preferred_element_type=jnp.float32
    )


def chem_kernel(*refs):
    sources, (out, rates, pick, spread, state, least, most, warmth) = refs[:8], refs[8:16]
    amounts, anomaly, solar, counts, speed, response, photo, recipe = held = refs[16:24]
    copies = [
        pltpu.make_async_copy(source, here, refs[24].at[index])
        for index, (source, here) in enumerate(zip(sources, held))
    ]
    for copy in copies:
        copy.start()
    for copy in copies:
        copy.wait()
    rows, columns, levels = anomaly.shape
    cells, species = state.shape
    width = rows * columns
    chunks = rates.shape[0]
    for row in range(rows):
        warmth[row * columns : (row + 1) * columns, :] = anomaly[row]
    place = lax.broadcasted_iota(jnp.int32, (width, species), 0)
    sunlight = jnp.zeros((width, species), jnp.float32)
    count = jnp.zeros((width, species), jnp.int32)
    longest = jnp.int32(0)
    for column in range(width):
        here = place == column
        spot = (column // columns, column % columns)
        sunlight = jnp.where(here, solar[spot], sunlight)
        count = jnp.where(here, counts[spot], count)
        longest = jnp.maximum(longest, counts[spot])
    ids = lax.broadcasted_iota(jnp.int32, (species, species), 0)
    for chunk in range(chunks):
        part = pl.ds(chunk * species, species)
        hits = [
            (recipe[row : row + 1, part] == ids).astype(jnp.float32) for row in range(4)
        ]
        taking = jnp.concatenate([hits[0], hits[1]], axis=1).astype(jnp.bfloat16)
        pick[chunk] = jnp.concatenate([taking, taking], axis=0)
        giving = jnp.concatenate(
            [jnp.transpose(hits[2] + hits[3]), jnp.transpose(hits[0] + hits[1])], axis=1
        ).astype(jnp.bfloat16)
        spread[chunk] = jnp.concatenate([giving, giving], axis=0)
    for level in range(levels):
        block = pl.ds(level * width, width)
        heat = jnp.broadcast_to(warmth[:, level : level + 1], (width, species))
        for chunk in range(chunks):
            part = pl.ds(chunk * species, species)
            rates[chunk, block, :] = (
                speed[:, part] * jnp.exp(response[:, part] * heat) + photo[:, part] * sunlight
            )

    def start():
        for level in range(levels):
            state[pl.ds(level * width, width), :] = amounts[pl.ds(level, width, stride=levels), :]

    def tiled(values):
        return jnp.concatenate([values] * levels, axis=0)

    start()
    substep = 1.0 / count.astype(jnp.float32)
    least[...] = state[...]
    most[...] = state[...]

    def advance(step, carry):
        current = state[...]
        least[...] = jnp.minimum(least[...], current)
        most[...] = jnp.maximum(most[...], current)
        pair = two_halves(current)
        flows = []
        for chunk in range(chunks):
            taken = dot32(pair, pick[chunk])
            flows.append(two_halves(rates[chunk] * taken[:, :species] * taken[:, species:]))
        total = dot32(jnp.concatenate(flows, axis=1), spread[...].reshape(-1, 2 * species))
        produced = total[:, :species]
        consumed = total[:, species:]
        size = tiled(substep)
        updated = (current + size * produced) / (current + size * consumed) * current
        state[...] = jnp.where(tiled(count) > step, updated, current)
        return carry

    lax.fori_loop(0, longest, advance, 0)
    usual = (jnp.min(least[...]) >= FAST_LEAST) & (jnp.max(most[...]) <= FAST_MOST)

    @pl.when(jnp.logical_not(usual))
    def _():
        start()

        def advance_fully(step, carry):
            current = state[...]
            produced = jnp.zeros((cells, species), jnp.float32)
            lost = jnp.zeros((cells, species), jnp.float32)
            for chunk in range(chunks):
                first_hit = pick[chunk, :species, :species].astype(jnp.float32)
                second_hit = pick[chunk, :species, species:].astype(jnp.float32)
                making = spread[chunk, :species, :species].astype(jnp.float32)
                first = dot32(current, first_hit, precision=HIGHEST)
                second = dot32(current, second_hit, precision=HIGHEST)
                rate = rates[chunk]
                produced += dot32(rate * first * second, making, precision=HIGHEST)
                lost += dot32(rate * second, first_hit, ((1,), (1,)), HIGHEST)
                lost += dot32(rate * first, second_hit, ((1,), (1,)), HIGHEST)
            size = tiled(substep)
            updated = (current + size * produced) / (1.0 + size * lost)
            state[...] = jnp.where(tiled(count) > step, updated, current)
            return carry

        lax.fori_loop(0, longest, advance_fully, 0)

    for level in range(levels):
        out[pl.ds(level, width, stride=levels), :] = state[pl.ds(level * width, width), :]


def react(operands):
    cells, species = operands[0].shape
    rows, columns, levels = operands[1].shape
    chunks = operands[7].shape[1] // species
    in_vmem = pl.BlockSpec(memory_space=pltpu.VMEM)
    held = [
        (pltpu.SMEM if index in (2, 3) else pltpu.VMEM)(operand.shape, operand.dtype)
        for index, operand in enumerate(operands)
    ]
    table = pltpu.VMEM((chunks, 2 * species, 2 * species), jnp.bfloat16)
    field = pltpu.VMEM((cells, species), jnp.float32)
    return pl.pallas_call(
        chem_kernel,
        out_shape=jax.ShapeDtypeStruct((cells, species), jnp.float32),
        in_specs=[pl.BlockSpec(memory_space=pltpu.HBM)] * len(operands),
        out_specs=in_vmem,
        scratch_shapes=[
            pltpu.VMEM((chunks, cells, species), jnp.float32), table, table,
            field, field, field, pltpu.VMEM((rows * columns, levels), jnp.float32),
            *held, pltpu.SemaphoreType.DMA((len(operands),)),
        ],
        compiler_params=pltpu.CompilerParams(vmem_limit_bytes=67043328),
    )(*operands)


def others(bands, devices):
    return [(dy, dl) for dl in range(devices) for dy in range(bands) if (dy, dl) != (0, 0)]


def peer(bands, devices, dy, dl):
    band, block = lax.axis_index("lat"), lax.axis_index("lon")
    return (lax.rem(band + dy, bands), lax.rem(block + dl, devices))


def signal_peers(bands, devices):
    barrier = pltpu.get_barrier_semaphore()
    for dy, dl in others(bands, devices):
        pl.semaphore_signal(
            barrier, inc=1, device_id=peer(bands, devices, dy, dl),
            device_id_type=pl.DeviceIdType.MESH,
        )


def wrap_rows(buffer, slot, values, half):
    extent = values.shape[0]
    buffer[slot, 8 : 8 + extent, :] = values
    buffer[slot, 0:8, :] = pltpu.roll(values[extent - 8 :], half, 1)
    buffer[slot, 8 + extent : 16 + extent, :] = pltpu.roll(values[:8], half, 1)


def clipped_edge(far_left, near_left, near_right, far_right):
    edge = 7.0 / 12.0 * (near_left + near_right) - 1.0 / 12.0 * (far_left + far_right)
    return jnp.minimum(
        jnp.maximum(edge, jnp.minimum(near_left, near_right)), jnp.maximum(near_left, near_right)
    )


def face_flow(courant, before, edge, after, left_mean, right_mean):
    magnitude = jnp.abs(courant)
    rightward = courant >= 0.0
    other = jnp.where(rightward, before, after)
    mean = jnp.where(rightward, left_mean, right_mean)
    bend = 6.0 * mean - 3.0 * (other + edge)
    return courant * (
        edge + 0.5 * magnitude * ((other - edge) + (1.0 - 2.0 / 3.0 * magnitude) * bend)
    )


def move_kernel(
    bands, devices, packed, east, north, out,
    inbox, outbox, back, wind_out, wind_in, courants, grid, edges,
    send_there, recv_there, send_wind, recv_wind, send_back, recv_back,
):
    band, block = lax.axis_index("lat"), lax.axis_index("lon")
    _, rows, longitudes = east.shape
    levels, _, _, species = packed.shape
    half = species // 2
    columns = longitudes // devices
    extent = longitudes // 2
    lats = bands * rows
    low_rows = rows // 2
    offsets = others(bands, devices)

    def remote(source, target, send_sem, recv_sem, device):
        return pltpu.make_async_remote_copy(
            src_ref=source, dst_ref=target, send_sem=send_sem, recv_sem=recv_sem,
            device_id=device, device_id_type=pl.DeviceIdType.MESH,
        )

    wind_out[...] = jnp.zeros_like(wind_out)
    wind_out[0:rows, 0:longitudes] = east[0]
    wind_out[rows : 2 * rows, 0:longitudes] = north[0]
    wind_in[band] = wind_out[...]
    inbox[band, block] = packed[block, band]
    pl.semaphore_wait(pltpu.get_barrier_semaphore(), len(offsets))

    winds = []
    for dy in range(1, bands):
        copy = remote(
            wind_out, wind_in.at[band], send_wind.at[dy], recv_wind.at[dy],
            peer(bands, devices, dy, 0),
        )
        copy.start()
        winds.append(copy)
    moves = []
    for index, (dy, dl) in enumerate(offsets):
        device = peer(bands, devices, dy, dl)
        copy = remote(
            packed.at[device[1], device[0]], inbox.at[band, block],
            send_there.at[index], recv_there.at[index], device,
        )
        copy.start()
        moves.append(copy)

    for copy in winds:
        copy.wait()
    near_tall = lax.broadcasted_iota(jnp.int32, (extent, species), 1) < half
    wide = wind_out.shape[1]
    tall = [wind_in[y] for y in range(bands)]
    tall.append(jnp.zeros((wide - bands * 2 * rows, wide), jnp.float32))
    turned = jnp.transpose(jnp.concatenate(tall, axis=0))
    for lat in range(lats):
        for kind in range(2):
            lane = lat // rows * 2 * rows + kind * rows + lat % rows
            courants[kind, lat] = jnp.where(
                near_tall,
                jnp.broadcast_to(turned[0:extent, lane : lane + 1], (extent, species)),
                jnp.broadcast_to(turned[extent : 2 * extent, lane : lane + 1], (extent, species)),
            )
    for copy in moves:
        copy.wait()

    near = lax.broadcasted_iota(jnp.int32, (low_rows * columns, species), 1) < half

    def swap_pair(first, second):
        return (
            jnp.where(near, first, pltpu.roll(second, half, 1)),
            jnp.where(near, pltpu.roll(first, half, 1), second),
        )

    for y in range(bands):
        for spot in range(devices // 2):
            pair = swap_pair(inbox[y, spot], inbox[y, spot + devices // 2])
            for high in range(2):
                for low in range(low_rows):
                    lat = y * rows + high * low_rows + low
                    grid[lat, 8 + spot * columns : 8 + (spot + 1) * columns, :] = pair[high][
                        low * columns : (low + 1) * columns
                    ]
    planes = [grid[lat, 8 : 8 + extent, :] for lat in range(lats)]
    empty = jnp.zeros((extent, species), jnp.float32)
    for sweep_index in range(ADV_STEPS):
        swept = []
        for lat in range(lats):
            mean = planes[lat]
            wrap_rows(grid, lat, mean, half)

            def shifted(buffer, shift):
                return buffer[lat, 8 + shift : 8 + shift + extent, :]

            left_mean = shifted(grid, -1)
            edge = clipped_edge(shifted(grid, -2), left_mean, mean, shifted(grid, 1))
            wrap_rows(edges, lat, edge, half)
            flow = face_flow(
                courants[0, lat], shifted(edges, -1), edge, shifted(edges, 1), left_mean, mean
            )
            wrap_rows(grid, lat, flow, half)
            swept.append(mean - (shifted(grid, 1) - flow))
        padded = [empty, empty] + swept + [empty, empty]
        rims = [clipped_edge(*padded[lat : lat + 4]) for lat in range(lats + 1)]
        flows = [
            face_flow(
                courants[1, lat], rims[lat - 1], rims[lat], rims[lat + 1],
                swept[lat - 1], swept[lat],
            )
            for lat in range(1, lats)
        ]
        flows = [empty] + flows + [empty]
        planes = [swept[lat] - (flows[lat + 1] - flows[lat]) for lat in range(lats)]
    for lat in range(lats):
        grid[lat, 8 : 8 + extent, :] = planes[lat]
    for y in range(bands):
        for spot in range(devices // 2):
            sides = [
                jnp.concatenate(
                    [
                        grid[
                            y * rows + high * low_rows + low,
                            8 + spot * columns : 8 + (spot + 1) * columns,
                            :,
                        ]
                        for low in range(low_rows)
                    ],
                    axis=0,
                )
                for high in range(2)
            ]
            outbox[y, spot], outbox[y, spot + devices // 2] = swap_pair(*sides)
    back[block, band] = outbox[band, block]
    moves = []
    for index, (dy, dl) in enumerate(offsets):
        device = peer(bands, devices, dy, dl)
        copy = remote(
            outbox.at[device[0], device[1]], back.at[block, band],
            send_back.at[index], recv_back.at[index], device,
        )
        copy.start()
        moves.append(copy)
    for copy in moves:
        copy.wait()
    count = low_rows * columns
    for level in range(levels):
        front, behind = swap_pair(back[level, 0], back[level, 1])
        out[pl.ds(level, count, stride=levels), :] = front
        out[pl.ds(count * levels + level, count, stride=levels), :] = behind


def halves(values):
    high = values.astype(jnp.bfloat16)
    return high, (values - high.astype(jnp.float32)).astype(jnp.bfloat16)


def substeps(groups, state, number, log_rates, pick, spread, *results):
    sides = range(2)
    gathered = [results[side * groups : (side + 1) * groups] for side in sides]
    scattered = [results[(2 + side) * groups : (3 + side) * groups] for side in sides]
    tall = state.shape[0] // groups
    species = state.shape[1]

    def load_pick():
        for side in sides:
            pltpu.matmul_push_rhs(pick[side], 0, side)

    def load_spread():
        for side in sides:
            pltpu.matmul_push_rhs(spread[side], 1, side)

    def gather(group, logs):
        pair = jnp.concatenate(halves(jnp.maximum(logs, FLOOR_LOG)), axis=1)
        for side in sides:
            pltpu.matmul_acc_lhs(
                gathered[side][group], pair, load_staged_rhs=None if group else 0
            )

    load_pick()
    for group in range(groups):
        gather(group, jnp.log2(state[group * tall : (group + 1) * tall, :]))
    load_spread()

    def advance(step, carry):
        for group in range(groups):
            block = slice(group * tall, (group + 1) * tall)
            for side in sides:
                logs = pltpu.matmul_pop(gathered[side][group]) + log_rates[side, block, :]
                high, low = halves(jnp.exp2(logs))
                pltpu.matmul_acc_lhs(
                    scattered[side][group], high, load_staged_rhs=None if group else 1
                )
                pltpu.matmul_acc_lhs(scattered[side][group], low)
        load_pick()
        load_spread()
        for group in range(groups):
            block = slice(group * tall, (group + 1) * tall)
            total = pltpu.matmul_pop(scattered[0][group]) + pltpu.matmul_pop(scattered[1][group])
            current, count = state[block, :], number[block, :]
            above = count * current + total[:, :species]
            below = count + total[:, species:] * (1.0 / jnp.maximum(current, FLOOR))
            gather(group, jnp.log2(above) - jnp.log2(below))
            state[block, :] = jnp.where(count > step.astype(jnp.float32), above / below, current)
        return carry

    lax.fori_loop(0, MOST_SUBSTEPS, advance, 0)
    for side in sides:
        for group in range(groups):
            pltpu.matmul_pop(gathered[side][group])
        pltpu.matmul_acc_lhs(
            scattered[side][0], jnp.zeros((tall, 2 * species), jnp.bfloat16), load_staged_rhs=1
        )
        pltpu.matmul_pop(scattered[side][0])


def whole_kernel(bands, devices, *refs):
    sources, out = refs[:10], refs[10]
    amounts, anomaly, solar, counts, speed, response, photo, recipe, east, north = held = refs[11:21]
    log_rates, pick, spread, state, number, warmth, arrived, packed = refs[21:29]
    move_refs = refs[29:]
    width = warmth.shape[0]
    cells, species = state.shape
    levels = cells // width

    signal_peers(bands, devices)
    copies = [
        pltpu.make_async_copy(source, here, arrived.at[index])
        for index, (source, here) in enumerate(zip(sources, held))
    ]
    for copy in copies:
        copy.start()
    for copy in copies:
        copy.wait()
    rows, columns, _ = anomaly.shape
    for row in range(rows):
        warmth[row * columns : (row + 1) * columns, :] = anomaly[row]
    place = lax.broadcasted_iota(jnp.int32, (width, species), 0)
    sunlight = jnp.zeros((width, species), jnp.float32)
    count = jnp.zeros((width, species), jnp.int32)
    for column in range(width):
        here = place == column
        spot = (column // columns, column % columns)
        sunlight = jnp.where(here, solar[spot], sunlight)
        count = jnp.where(here, counts[spot], count)
    count = count.astype(jnp.float32)
    ids = lax.broadcasted_iota(jnp.int32, (species, species), 0)
    for chunk in range(4):
        part = pl.ds(chunk * species, species)
        hits = [(recipe[row : row + 1, part] == ids).astype(jnp.float32) for row in range(4)]
        taking, giving = hits[0] + hits[1], hits[2] + hits[3]
        side, spot = chunk // 2, chunk % 2 * species
        for copy in range(2):
            pick[side, copy * species : (copy + 1) * species, spot : spot + species] = (
                taking.astype(jnp.bfloat16)
            )
        spread[side, spot : spot + species, :] = jnp.concatenate(
            [jnp.transpose(giving), jnp.transpose(taking)], axis=1
        ).astype(jnp.bfloat16)
    for level in range(levels):
        block = pl.ds(level * width, width)
        heat = jnp.broadcast_to(warmth[:, level : level + 1], (width, species))
        for chunk in range(4):
            part = pl.ds(chunk * species, species)
            log_rates[chunk // 2, block, chunk % 2 * species : (chunk % 2 + 1) * species] = jnp.log2(
                speed[:, part] * jnp.exp(response[:, part] * heat) + photo[:, part] * sunlight
            )
        state[block, :] = amounts[pl.ds(level, width, stride=levels), :]
        number[block, :] = count

    groups = cells // 32
    pl.run_scoped(
        functools.partial(substeps, groups, state, number, log_rates, pick, spread),
        *[
            pltpu.ACC(side)((32, 2 * species), jnp.float32)
            for use in range(2)
            for side in range(2)
            for group in range(groups)
        ],
    )

    half = species // 2
    near = lax.broadcasted_iota(jnp.int32, (width // 2, species), 1) < half
    for level in range(levels):
        front = state[pl.ds(level * width, width // 2), :]
        behind = state[pl.ds(level * width + width // 2, width // 2), :]
        packed[level, 0] = jnp.where(near, front, pltpu.roll(behind, half, 1))
        packed[level, 1] = jnp.where(near, pltpu.roll(front, half, 1), behind)
    move_kernel(bands, devices, packed, east, north, out, *move_refs)


def react_and_advect(operands):
    bands, devices = lax.axis_size("lat"), lax.axis_size("lon")
    cells, species = operands[0].shape
    rows, columns, levels = operands[1].shape
    longitudes = operands[8].shape[2]
    lats, extent, count = bands * rows, longitudes // 2, rows * columns // 2
    wide = -(-longitudes // 128) * 128
    held = [
        (pltpu.SMEM if index in (2, 3) else pltpu.VMEM)(operand.shape, operand.dtype)
        for index, operand in enumerate(operands)
    ]
    semaphores = pltpu.SemaphoreType.DMA((bands * devices - 1,))
    wind_semaphores = pltpu.SemaphoreType.DMA((bands,))
    box = pltpu.VMEM((bands, devices, count, species), jnp.float32)
    exchanged = pltpu.VMEM((levels, bands, count, species), jnp.float32)
    wrapped = pltpu.VMEM((lats, extent + 16, species), jnp.float32)
    table = pltpu.VMEM((2, 2 * species, 2 * species), jnp.bfloat16)
    field = pltpu.VMEM((cells, species), jnp.float32)
    return pl.pallas_call(
        functools.partial(whole_kernel, bands, devices),
        out_shape=jax.ShapeDtypeStruct((cells, species), jnp.float32),
        in_specs=[pl.BlockSpec(memory_space=pltpu.HBM)] * len(operands),
        out_specs=pl.BlockSpec(memory_space=pltpu.VMEM),
        scratch_shapes=[
            *held,
            pltpu.VMEM((2, cells, 2 * species), jnp.float32), table, table, field, field,
            pltpu.VMEM((rows * columns, levels), jnp.float32),
            pltpu.SemaphoreType.DMA((len(operands),)), exchanged,
            box, box, exchanged,
            pltpu.VMEM((2 * rows, wide), jnp.float32),
            pltpu.VMEM((bands, 2 * rows, wide), jnp.float32),
            pltpu.VMEM((2, lats, extent, species), jnp.float32), wrapped, wrapped,
            semaphores, semaphores, wind_semaphores, wind_semaphores, semaphores, semaphores,
        ],
        compiler_params=pltpu.CompilerParams(
            collective_id=0, has_side_effects=True, vmem_limit_bytes=67043328
        ),
    )(*operands)


def per_device(
    species_amounts,
    thermal_anomaly,
    solar_flux_factor,
    inner_iterations,
    reference_speed,
    thermal_response,
    photo_breakup,
    reaction_recipe,
    eastward_wind_ratio,
    northward_wind_ratio,
):
    rows, columns, levels, species = species_amounts.shape
    devices = lax.axis_size("lon")
    longitudes = eastward_wind_ratio.shape[2]
    reactions = reaction_recipe.shape[1]
    operands = (
        species_amounts.reshape(-1, species), thermal_anomaly, solar_flux_factor,
        inner_iterations, reference_speed.reshape(1, -1), thermal_response.reshape(1, -1),
        photo_breakup.reshape(1, -1), reaction_recipe,
    )
    paired = lax.axis_size("lat") == 2 and levels == devices and rows % 2 == 0
    tabled = species == 128 and reactions == 4 * species and rows * columns % 16 == 0
    if paired and tabled and devices % 2 == 0 and longitudes <= 128:
        moved = react_and_advect((*operands, eastward_wind_ratio, northward_wind_ratio))
        return moved.reshape(species_amounts.shape)
    settled_columns = react(operands).reshape(species_amounts.shape)
    lat_rows = species_amounts.shape[0]
    row_ids = lax.axis_index("lat") * lat_rows + lax.broadcasted_iota(
        jnp.int32, (lat_rows, 1, 1, 1), 0
    )
    carried_quantity = lax.all_to_all(
        settled_columns, "lon", split_axis=2, concat_axis=1, tiled=True
    )
    east_faces = jnp.transpose(eastward_wind_ratio, (1, 2, 0))[..., None]
    south_faces = jnp.where(
        row_ids > 0, jnp.transpose(northward_wind_ratio, (1, 2, 0))[..., None], 0.0
    )
    east_pad = wrap_pad(east_faces, 1)
    for sweep_index in range(ADV_STEPS):
        carried_quantity = flux_sweep(
            wrap_pad(carried_quantity, 1), east_pad, 1, carried_quantity.shape[1]
        )
        rimmed, south_pad = (
            with_halo(carried_quantity, (("lat", 0),), 3),
            with_halo(south_faces, (("lat", 0),), 3),
        )
        carried_quantity = flux_sweep(rimmed, south_pad, 0, lat_rows)
    return lax.all_to_all(carried_quantity, "lon", split_axis=1, concat_axis=2, tiled=True)


def solution(mesh):
    return jax.shard_map(
        per_device,
        mesh=mesh,
        in_specs=(
            P("lat", "lon", None, None),
            P("lat", "lon", None),
            P("lat", "lon"),
            P("lat", "lon"),
            P(),
            P(),
            P(),
            P(),
            P("lon", "lat", None),
            P("lon", "lat", None),
        ),
        out_specs=P("lat", "lon", None, None),
        check_vma=False,
    )
```

```python
import functools
import jax
import jax.numpy as jnp
from jax import lax
from jax.experimental import pallas as pl
from jax.experimental.pallas import tpu as pltpu
from jax.sharding import PartitionSpec as P

ADV_STEPS = 2
FAST_LEAST = 1e-12
FAST_MOST = 1e8
HIGHEST = lax.Precision.HIGHEST
MOST_SUBSTEPS = 36
FLOOR = 1e-20
FLOOR_LOG = -66.43856


def with_halo(block, sides, width):
    for axis, dim in sides:
        count = lax.axis_size(axis)
        forward = [(i, i + 1) for i in range(count - 1)]
        backward = [(target, source) for source, target in forward]
        low = lax.ppermute(
            lax.slice_in_dim(block, block.shape[dim] - width, None, axis=dim), axis, forward
        )
        high = lax.ppermute(lax.slice_in_dim(block, 0, width, axis=dim), axis, backward)
        block = jnp.concatenate([low, block, high], axis=dim)
    return block


def slice_axis(array, start, count, along):
    return lax.slice_in_dim(array, start, start + count, axis=along)


def flux_sweep(padded, courant_pad, along, length):
    far_left = slice_axis(padded, 0, length + 3, along)
    near_left = slice_axis(padded, 1, length + 3, along)
    near_right = slice_axis(padded, 2, length + 3, along)
    far_right = slice_axis(padded, 3, length + 3, along)
    edges = 7.0 / 12.0 * (near_left + near_right) - 1.0 / 12.0 * (far_left + far_right)
    edges = jnp.minimum(
        jnp.maximum(edges, jnp.minimum(near_left, near_right)), jnp.maximum(near_left, near_right)
    )
    cell_means = slice_axis(padded, 2, length + 2, along)
    left_edge = slice_axis(edges, 0, length + 2, along)
    right_edge = slice_axis(edges, 1, length + 2, along)
    edge_jump = right_edge - left_edge
    curvature = 6.0 * cell_means - 3.0 * (left_edge + right_edge)
    courant = slice_axis(courant_pad, 3, length + 1, along)
    magnitude = jnp.abs(courant)
    from_left = slice_axis(right_edge, 0, length + 1, along) - 0.5 * courant * (
        slice_axis(edge_jump, 0, length + 1, along)
        - (1.0 - 2.0 / 3.0 * courant) * slice_axis(curvature, 0, length + 1, along)
    )
    from_right = slice_axis(left_edge, 1, length + 1, along) + 0.5 * magnitude * (
        slice_axis(edge_jump, 1, length + 1, along)
        + (1.0 - 2.0 / 3.0 * magnitude) * slice_axis(curvature, 1, length + 1, along)
    )
    face_flux = courant * jnp.where(courant >= 0.0, from_left, from_right)
    interior = slice_axis(padded, 3, length, along)
    return interior - (
        slice_axis(face_flux, 1, length, along) - slice_axis(face_flux, 0, length, along)
    )


def wrap_pad(array, along):
    extent = array.shape[along]
    return jnp.concatenate(
        [slice_axis(array, extent - 3, 3, along), array, slice_axis(array, 0, 3, along)], axis=along
    )


def two_halves(values):
    high = values.astype(jnp.bfloat16)
    low = (values - high.astype(jnp.float32)).astype(jnp.bfloat16)
    return jnp.concatenate([high, low], axis=1)


def dot32(left, right, dims=((1,), (0,)), precision=None):
    return lax.dot_general(
        left, right, (dims, ((), ())), precision=precision, preferred_element_type=jnp.float32
    )


def chem_kernel(*refs):
    sources, (out, rates, pick, spread, state, least, most, warmth) = refs[:8], refs[8:16]
    amounts, anomaly, solar, counts, speed, response, photo, recipe = held = refs[16:24]
    copies = [
        pltpu.make_async_copy(source, here, refs[24].at[index])
        for index, (source, here) in enumerate(zip(sources, held))
    ]
    for copy in copies:
        copy.start()
    for copy in copies:
        copy.wait()
    rows, columns, levels = anomaly.shape
    cells, species = state.shape
    width = rows * columns
    chunks = rates.shape[0]
    for row in range(rows):
        warmth[row * columns : (row + 1) * columns, :] = anomaly[row]
    place = lax.broadcasted_iota(jnp.int32, (width, species), 0)
    sunlight = jnp.zeros((width, species), jnp.float32)
    count = jnp.zeros((width, species), jnp.int32)
    longest = jnp.int32(0)
    for column in range(width):
        here = place == column
        spot = (column // columns, column % columns)
        sunlight = jnp.where(here, solar[spot], sunlight)
        count = jnp.where(here, counts[spot], count)
        longest = jnp.maximum(longest, counts[spot])
    ids = lax.broadcasted_iota(jnp.int32, (species, species), 0)
    for chunk in range(chunks):
        part = pl.ds(chunk * species, species)
        hits = [
            (recipe[row : row + 1, part] == ids).astype(jnp.float32) for row in range(4)
        ]
        taking = jnp.concatenate([hits[0], hits[1]], axis=1).astype(jnp.bfloat16)
        pick[chunk] = jnp.concatenate([taking, taking], axis=0)
        giving = jnp.concatenate(
            [jnp.transpose(hits[2] + hits[3]), jnp.transpose(hits[0] + hits[1])], axis=1
        ).astype(jnp.bfloat16)
        spread[chunk] = jnp.concatenate([giving, giving], axis=0)
    for level in range(levels):
        block = pl.ds(level * width, width)
        heat = jnp.broadcast_to(warmth[:, level : level + 1], (width, species))
        for chunk in range(chunks):
            part = pl.ds(chunk * species, species)
            rates[chunk, block, :] = (
                speed[:, part] * jnp.exp(response[:, part] * heat) + photo[:, part] * sunlight
            )

    def start():
        for level in range(levels):
            state[pl.ds(level * width, width), :] = amounts[pl.ds(level, width, stride=levels), :]

    def tiled(values):
        return jnp.concatenate([values] * levels, axis=0)

    start()
    substep = 1.0 / count.astype(jnp.float32)
    least[...] = state[...]
    most[...] = state[...]

    def advance(step, carry):
        current = state[...]
        least[...] = jnp.minimum(least[...], current)
        most[...] = jnp.maximum(most[...], current)
        pair = two_halves(current)
        flows = []
        for chunk in range(chunks):
            taken = dot32(pair, pick[chunk])
            flows.append(two_halves(rates[chunk] * taken[:, :species] * taken[:, species:]))
        total = dot32(jnp.concatenate(flows, axis=1), spread[...].reshape(-1, 2 * species))
        produced = total[:, :species]
        consumed = total[:, species:]
        size = tiled(substep)
        updated = (current + size * produced) / (current + size * consumed) * current
        state[...] = jnp.where(tiled(count) > step, updated, current)
        return carry

    lax.fori_loop(0, longest, advance, 0)
    usual = (jnp.min(least[...]) >= FAST_LEAST) & (jnp.max(most[...]) <= FAST_MOST)

    @pl.when(jnp.logical_not(usual))
    def _():
        start()

        def advance_fully(step, carry):
            current = state[...]
            produced = jnp.zeros((cells, species), jnp.float32)
            lost = jnp.zeros((cells, species), jnp.float32)
            for chunk in range(chunks):
                first_hit = pick[chunk, :species, :species].astype(jnp.float32)
                second_hit = pick[chunk, :species, species:].astype(jnp.float32)
                making = spread[chunk, :species, :species].astype(jnp.float32)
                first = dot32(current, first_hit, precision=HIGHEST)
                second = dot32(current, second_hit, precision=HIGHEST)
                rate = rates[chunk]
                produced += dot32(rate * first * second, making, precision=HIGHEST)
                lost += dot32(rate * second, first_hit, ((1,), (1,)), HIGHEST)
                lost += dot32(rate * first, second_hit, ((1,), (1,)), HIGHEST)
            size = tiled(substep)
            updated = (current + size * produced) / (1.0 + size * lost)
            state[...] = jnp.where(tiled(count) > step, updated, current)
            return carry

        lax.fori_loop(0, longest, advance_fully, 0)

    for level in range(levels):
        out[pl.ds(level, width, stride=levels), :] = state[pl.ds(level * width, width), :]


def react(operands):
    cells, species = operands[0].shape
    rows, columns, levels = operands[1].shape
    chunks = operands[7].shape[1] // species
    in_vmem = pl.BlockSpec(memory_space=pltpu.VMEM)
    held = [
        (pltpu.SMEM if index in (2, 3) else pltpu.VMEM)(operand.shape, operand.dtype)
        for index, operand in enumerate(operands)
    ]
    table = pltpu.VMEM((chunks, 2 * species, 2 * species), jnp.bfloat16)
    field = pltpu.VMEM((cells, species), jnp.float32)
    return pl.pallas_call(
        chem_kernel,
        out_shape=jax.ShapeDtypeStruct((cells, species), jnp.float32),
        in_specs=[pl.BlockSpec(memory_space=pltpu.HBM)] * len(operands),
        out_specs=in_vmem,
        scratch_shapes=[
            pltpu.VMEM((chunks, cells, species), jnp.float32), table, table,
            field, field, field, pltpu.VMEM((rows * columns, levels), jnp.float32),
            *held, pltpu.SemaphoreType.DMA((len(operands),)),
        ],
        compiler_params=pltpu.CompilerParams(vmem_limit_bytes=67043328),
    )(*operands)


def others(bands, devices):
    return [(dy, dl) for dl in range(devices) for dy in range(bands) if (dy, dl) != (0, 0)]


def peer(bands, devices, dy, dl):
    band, block = lax.axis_index("lat"), lax.axis_index("lon")
    return (lax.rem(band + dy, bands), lax.rem(block + dl, devices))


def signal_peers(bands, devices):
    barrier = pltpu.get_barrier_semaphore()
    for dy, dl in others(bands, devices):
        pl.semaphore_signal(
            barrier, inc=1, device_id=peer(bands, devices, dy, dl),
            device_id_type=pl.DeviceIdType.MESH,
        )


def wrap_rows(buffer, slot, values, half):
    extent = values.shape[0]
    buffer[slot, 8 : 8 + extent, :] = values
    buffer[slot, 0:8, :] = pltpu.roll(values[extent - 8 :], half, 1)
    buffer[slot, 8 + extent : 16 + extent, :] = pltpu.roll(values[:8], half, 1)


def clipped_edge(far_left, near_left, near_right, far_right):
    edge = 7.0 / 12.0 * (near_left + near_right) - 1.0 / 12.0 * (far_left + far_right)
    return jnp.minimum(
        jnp.maximum(edge, jnp.minimum(near_left, near_right)), jnp.maximum(near_left, near_right)
    )


def face_flow(courant, before, edge, after, left_mean, right_mean):
    magnitude = jnp.abs(courant)
    rightward = courant >= 0.0
    other = jnp.where(rightward, before, after)
    mean = jnp.where(rightward, left_mean, right_mean)
    bend = 6.0 * mean - 3.0 * (other + edge)
    return courant * (
        edge + 0.5 * magnitude * ((other - edge) + (1.0 - 2.0 / 3.0 * magnitude) * bend)
    )


def move_kernel(
    bands, devices, packed, east, north, out,
    inbox, outbox, back, wind_out, wind_in, courants, grid, edges,
    send_there, recv_there, send_wind, recv_wind, send_back, recv_back,
):
    band, block = lax.axis_index("lat"), lax.axis_index("lon")
    _, rows, longitudes = east.shape
    species = packed.shape[2]
    levels = packed.shape[0] // bands
    half = species // 2
    columns = longitudes // devices
    extent = longitudes // 2
    lats = bands * rows
    low_rows = rows // 2
    offsets = others(bands, devices)

    def remote(source, target, send_sem, recv_sem, device):
        return pltpu.make_async_remote_copy(
            src_ref=source, dst_ref=target, send_sem=send_sem, recv_sem=recv_sem,
            device_id=device, device_id_type=pl.DeviceIdType.MESH,
        )

    wind_out[...] = jnp.zeros_like(wind_out)
    wind_out[0:rows, 0:longitudes] = east[0]
    wind_out[rows : 2 * rows, 0:longitudes] = north[0]
    wind_in[band] = wind_out[...]
    inbox[band * devices + block] = packed[block * bands + band]
    pl.semaphore_wait(pltpu.get_barrier_semaphore(), len(offsets))

    winds = []
    for dy in range(1, bands):
        copy = remote(
            wind_out, wind_in.at[band], send_wind.at[dy], recv_wind.at[dy],
            peer(bands, devices, dy, 0),
        )
        copy.start()
        winds.append(copy)
    def wait_for_all(box, semaphore):
        most = box.at[pl.ds(0, len(offsets))]
        pltpu.make_async_copy(most, most, semaphore.at[0]).wait()

    for dy, dl in offsets:
        device = peer(bands, devices, dy, dl)
        remote(
            packed.at[device[1] * bands + device[0]], inbox.at[band * devices + block],
            send_there.at[0], recv_there.at[0], device,
        ).start()

    for copy in winds:
        copy.wait()
    near_tall = lax.broadcasted_iota(jnp.int32, (extent, species), 1) < half
    wide = wind_out.shape[1]
    tall = [wind_in[y] for y in range(bands)]
    tall.append(jnp.zeros((wide - bands * 2 * rows, wide), jnp.float32))
    turned = jnp.transpose(jnp.concatenate(tall, axis=0))
    for lat in range(lats):
        for kind in range(2):
            lane = lat // rows * 2 * rows + kind * rows + lat % rows
            courants[kind, lat] = jnp.where(
                near_tall,
                jnp.broadcast_to(turned[0:extent, lane : lane + 1], (extent, species)),
                jnp.broadcast_to(turned[extent : 2 * extent, lane : lane + 1], (extent, species)),
            )
    wait_for_all(packed, send_there)
    wait_for_all(inbox, recv_there)

    near = lax.broadcasted_iota(jnp.int32, (low_rows * columns, species), 1) < half

    def swap_pair(first, second):
        return (
            jnp.where(near, first, pltpu.roll(second, half, 1)),
            jnp.where(near, pltpu.roll(first, half, 1), second),
        )

    for y in range(bands):
        for spot in range(devices // 2):
            pair = swap_pair(
                inbox[y * devices + spot], inbox[y * devices + spot + devices // 2]
            )
            for high in range(2):
                for low in range(low_rows):
                    lat = y * rows + high * low_rows + low
                    grid[lat, 8 + spot * columns : 8 + (spot + 1) * columns, :] = pair[high][
                        low * columns : (low + 1) * columns
                    ]
    planes = [grid[lat, 8 : 8 + extent, :] for lat in range(lats)]
    empty = jnp.zeros((extent, species), jnp.float32)
    for sweep_index in range(ADV_STEPS):
        swept = []
        for lat in range(lats):
            mean = planes[lat]
            wrap_rows(grid, lat, mean, half)

            def shifted(buffer, shift):
                return buffer[lat, 8 + shift : 8 + shift + extent, :]

            left_mean = shifted(grid, -1)
            edge = clipped_edge(shifted(grid, -2), left_mean, mean, shifted(grid, 1))
            wrap_rows(edges, lat, edge, half)
            flow = face_flow(
                courants[0, lat], shifted(edges, -1), edge, shifted(edges, 1), left_mean, mean
            )
            wrap_rows(grid, lat, flow, half)
            swept.append(mean - (shifted(grid, 1) - flow))
        padded = [empty, empty] + swept + [empty, empty]
        rims = [clipped_edge(*padded[lat : lat + 4]) for lat in range(lats + 1)]
        flows = [
            face_flow(
                courants[1, lat], rims[lat - 1], rims[lat], rims[lat + 1],
                swept[lat - 1], swept[lat],
            )
            for lat in range(1, lats)
        ]
        flows = [empty] + flows + [empty]
        planes = [swept[lat] - (flows[lat + 1] - flows[lat]) for lat in range(lats)]
    for lat in range(lats):
        grid[lat, 8 : 8 + extent, :] = planes[lat]
    for y in range(bands):
        for spot in range(devices // 2):
            sides = [
                jnp.concatenate(
                    [
                        grid[
                            y * rows + high * low_rows + low,
                            8 + spot * columns : 8 + (spot + 1) * columns,
                            :,
                        ]
                        for low in range(low_rows)
                    ],
                    axis=0,
                )
                for high in range(2)
            ]
            place = y * devices + spot
            outbox[place], outbox[place + devices // 2] = swap_pair(*sides)
    back[block * bands + band] = outbox[band * devices + block]
    for dy, dl in offsets:
        device = peer(bands, devices, dy, dl)
        remote(
            outbox.at[device[0] * devices + device[1]], back.at[block * bands + band],
            send_back.at[0], recv_back.at[0], device,
        ).start()
    wait_for_all(outbox, send_back)
    wait_for_all(back, recv_back)
    count = low_rows * columns
    for level in range(levels):
        front, behind = swap_pair(back[level * bands], back[level * bands + 1])
        out[pl.ds(level, count, stride=levels), :] = front
        out[pl.ds(count * levels + level, count, stride=levels), :] = behind


def halves(values):
    high = values.astype(jnp.bfloat16)
    return high, (values - high.astype(jnp.float32)).astype(jnp.bfloat16)


def substeps(groups, state, number, log_rates, pick, spread, *results):
    sides = range(2)
    gathered = [results[side * groups : (side + 1) * groups] for side in sides]
    scattered = [results[(2 + side) * groups : (3 + side) * groups] for side in sides]
    tall = state.shape[0] // groups
    species = state.shape[1]

    def load_pick():
        for side in sides:
            pltpu.matmul_push_rhs(pick[side], 0, side)

    def load_spread():
        for side in sides:
            pltpu.matmul_push_rhs(spread[side], 1, side)

    def gather(group, logs):
        pair = jnp.concatenate(halves(jnp.maximum(logs, FLOOR_LOG)), axis=1)
        for side in sides:
            pltpu.matmul_acc_lhs(
                gathered[side][group], pair, load_staged_rhs=None if group else 0
            )

    load_pick()
    for group in range(groups):
        gather(group, jnp.log2(state[group * tall : (group + 1) * tall, :]))
    load_spread()

    def advance(step, carry):
        for group in range(groups):
            block = slice(group * tall, (group + 1) * tall)
            for side in sides:
                logs = pltpu.matmul_pop(gathered[side][group]) + log_rates[side, block, :]
                high, low = halves(jnp.exp2(logs))
                pltpu.matmul_acc_lhs(
                    scattered[side][group], high, load_staged_rhs=None if group else 1
                )
                pltpu.matmul_acc_lhs(scattered[side][group], low)
            if group == 0:
                load_spread()
        load_pick()
        for group in range(groups):
            block = slice(group * tall, (group + 1) * tall)
            total = pltpu.matmul_pop(scattered[0][group]) + pltpu.matmul_pop(scattered[1][group])
            current, count = state[block, :], number[block, :]
            above = count * current + total[:, :species]
            below = count + total[:, species:] * (1.0 / jnp.maximum(current, FLOOR))
            gather(group, jnp.log2(above) - jnp.log2(below))
            state[block, :] = jnp.where(count > step.astype(jnp.float32), above / below, current)
        return carry

    lax.fori_loop(0, MOST_SUBSTEPS, advance, 0)
    for side in sides:
        for group in range(groups):
            pltpu.matmul_pop(gathered[side][group])
        pltpu.matmul_acc_lhs(
            scattered[side][0], jnp.zeros((tall, 2 * species), jnp.bfloat16), load_staged_rhs=1
        )
        pltpu.matmul_pop(scattered[side][0])


def whole_kernel(bands, devices, *refs):
    sources, out = refs[:10], refs[10]
    amounts, anomaly, solar, counts, speed, response, photo, recipe, east, north = held = refs[11:21]
    log_rates, pick, spread, state, number, warmth, arrived, packed = refs[21:29]
    move_refs = refs[29:]
    width = warmth.shape[0]
    cells, species = state.shape
    levels = cells // width

    copies = [
        pltpu.make_async_copy(source, here, arrived.at[index])
        for index, (source, here) in enumerate(zip(sources, held))
    ]
    for copy in copies:
        copy.start()
    signal_peers(bands, devices)
    for copy in copies:
        copy.wait()
    rows, columns, _ = anomaly.shape
    for row in range(rows):
        warmth[row * columns : (row + 1) * columns, :] = anomaly[row]
    place = lax.broadcasted_iota(jnp.int32, (width, species), 0)
    sunlight = jnp.zeros((width, species), jnp.float32)
    count = jnp.zeros((width, species), jnp.int32)
    for column in range(width):
        here = place == column
        spot = (column // columns, column % columns)
        sunlight = jnp.where(here, solar[spot], sunlight)
        count = jnp.where(here, counts[spot], count)
    count = count.astype(jnp.float32)
    ids = lax.broadcasted_iota(jnp.int32, (species, species), 0)
    for chunk in range(4):
        part = pl.ds(chunk * species, species)
        hits = [(recipe[row : row + 1, part] == ids).astype(jnp.float32) for row in range(4)]
        taking, giving = hits[0] + hits[1], hits[2] + hits[3]
        side, spot = chunk // 2, chunk % 2 * species
        for copy in range(2):
            pick[side, copy * species : (copy + 1) * species, spot : spot + species] = (
                taking.astype(jnp.bfloat16)
            )
        spread[side, spot : spot + species, :] = jnp.concatenate(
            [jnp.transpose(giving), jnp.transpose(taking)], axis=1
        ).astype(jnp.bfloat16)
    for level in range(levels):
        block = pl.ds(level * width, width)
        heat = jnp.broadcast_to(warmth[:, level : level + 1], (width, species))
        for chunk in range(4):
            part = pl.ds(chunk * species, species)
            log_rates[chunk // 2, block, chunk % 2 * species : (chunk % 2 + 1) * species] = jnp.log2(
                speed[:, part] * jnp.exp(response[:, part] * heat) + photo[:, part] * sunlight
            )
        state[block, :] = amounts[pl.ds(level, width, stride=levels), :]
        number[block, :] = count

    groups = cells // 32
    pl.run_scoped(
        functools.partial(substeps, groups, state, number, log_rates, pick, spread),
        *[
            pltpu.ACC(side)((32, 2 * species), jnp.float32)
            for use in range(2)
            for side in range(2)
            for group in range(groups)
        ],
    )

    half = species // 2
    near = lax.broadcasted_iota(jnp.int32, (width // 2, species), 1) < half
    for level in range(levels):
        front = state[pl.ds(level * width, width // 2), :]
        behind = state[pl.ds(level * width + width // 2, width // 2), :]
        packed[2 * level] = jnp.where(near, front, pltpu.roll(behind, half, 1))
        packed[2 * level + 1] = jnp.where(near, pltpu.roll(front, half, 1), behind)
    move_kernel(bands, devices, packed, east, north, out, *move_refs)


def react_and_advect(operands):
    bands, devices = lax.axis_size("lat"), lax.axis_size("lon")
    cells, species = operands[0].shape
    rows, columns, levels = operands[1].shape
    longitudes = operands[8].shape[2]
    lats, extent, count = bands * rows, longitudes // 2, rows * columns // 2
    wide = -(-longitudes // 128) * 128
    held = [
        (pltpu.SMEM if index in (2, 3) else pltpu.VMEM)(operand.shape, operand.dtype)
        for index, operand in enumerate(operands)
    ]
    semaphores = pltpu.SemaphoreType.DMA((1,))
    wind_semaphores = pltpu.SemaphoreType.DMA((bands,))
    box = pltpu.VMEM((bands * devices, count, species), jnp.float32)
    exchanged = pltpu.VMEM((levels * bands, count, species), jnp.float32)
    wrapped = pltpu.VMEM((lats, extent + 16, species), jnp.float32)
    table = pltpu.VMEM((2, 2 * species, 2 * species), jnp.bfloat16)
    field = pltpu.VMEM((cells, species), jnp.float32)
    return pl.pallas_call(
        functools.partial(whole_kernel, bands, devices),
        out_shape=jax.ShapeDtypeStruct((cells, species), jnp.float32),
        in_specs=[pl.BlockSpec(memory_space=pltpu.HBM)] * len(operands),
        out_specs=pl.BlockSpec(memory_space=pltpu.VMEM),
        scratch_shapes=[
            *held,
            pltpu.VMEM((2, cells, 2 * species), jnp.float32), table, table, field, field,
            pltpu.VMEM((rows * columns, levels), jnp.float32),
            pltpu.SemaphoreType.DMA((len(operands),)), exchanged,
            box, box, exchanged,
            pltpu.VMEM((2 * rows, wide), jnp.float32),
            pltpu.VMEM((bands, 2 * rows, wide), jnp.float32),
            pltpu.VMEM((2, lats, extent, species), jnp.float32), wrapped, wrapped,
            semaphores, semaphores, wind_semaphores, wind_semaphores, semaphores, semaphores,
        ],
        compiler_params=pltpu.CompilerParams(
            collective_id=0, has_side_effects=True, vmem_limit_bytes=32 << 20,
        ),
    )(*[pltpu.with_memory_space_constraint(operand, pltpu.HBM) for operand in operands])


def per_device(
    species_amounts,
    thermal_anomaly,
    solar_flux_factor,
    inner_iterations,
    reference_speed,
    thermal_response,
    photo_breakup,
    reaction_recipe,
    eastward_wind_ratio,
    northward_wind_ratio,
):
    rows, columns, levels, species = species_amounts.shape
    devices = lax.axis_size("lon")
    longitudes = eastward_wind_ratio.shape[2]
    reactions = reaction_recipe.shape[1]
    operands = (
        species_amounts.reshape(-1, species), thermal_anomaly, solar_flux_factor,
        inner_iterations, reference_speed.reshape(1, -1), thermal_response.reshape(1, -1),
        photo_breakup.reshape(1, -1), reaction_recipe,
    )
    paired = lax.axis_size("lat") == 2 and levels == devices and rows % 2 == 0
    tabled = species == 128 and reactions == 4 * species and rows * columns % 16 == 0
    if paired and tabled and devices % 2 == 0 and longitudes <= 128:
        moved = react_and_advect((*operands, eastward_wind_ratio, northward_wind_ratio))
        return moved.reshape(species_amounts.shape)
    settled_columns = react(operands).reshape(species_amounts.shape)
    lat_rows = species_amounts.shape[0]
    row_ids = lax.axis_index("lat") * lat_rows + lax.broadcasted_iota(
        jnp.int32, (lat_rows, 1, 1, 1), 0
    )
    carried_quantity = lax.all_to_all(
        settled_columns, "lon", split_axis=2, concat_axis=1, tiled=True
    )
    east_faces = jnp.transpose(eastward_wind_ratio, (1, 2, 0))[..., None]
    south_faces = jnp.where(
        row_ids > 0, jnp.transpose(northward_wind_ratio, (1, 2, 0))[..., None], 0.0
    )
    east_pad = wrap_pad(east_faces, 1)
    for sweep_index in range(ADV_STEPS):
        carried_quantity = flux_sweep(
            wrap_pad(carried_quantity, 1), east_pad, 1, carried_quantity.shape[1]
        )
        rimmed, south_pad = (
            with_halo(carried_quantity, (("lat", 0),), 3),
            with_halo(south_faces, (("lat", 0),), 3),
        )
        carried_quantity = flux_sweep(rimmed, south_pad, 0, lat_rows)
    return lax.all_to_all(carried_quantity, "lon", split_axis=1, concat_axis=2, tiled=True)


def solution(mesh):
    return jax.shard_map(
        per_device,
        mesh=mesh,
        in_specs=(
            P("lat", "lon", None, None),
            P("lat", "lon", None),
            P("lat", "lon"),
            P("lat", "lon"),
            P(),
            P(),
            P(),
            P(),
            P("lon", "lat", None),
            P("lon", "lat", None),
        ),
        out_specs=P("lat", "lon", None, None),
        check_vma=False,
    )
```

```python
import functools
import jax
import jax.numpy as jnp
from jax import lax
from jax.experimental import pallas as pl
from jax.experimental.pallas import tpu as pltpu
from jax.sharding import PartitionSpec as P

ADV_STEPS = 2
FAST_LEAST = 1e-12
FAST_MOST = 1e8
HIGHEST = lax.Precision.HIGHEST
MOST_SUBSTEPS = 36
SEGMENT = 4
FLOOR = 1e-20
FLOOR_LOG = -66.43856


def with_halo(block, sides, width):
    for axis, dim in sides:
        count = lax.axis_size(axis)
        forward = [(i, i + 1) for i in range(count - 1)]
        backward = [(target, source) for source, target in forward]
        low = lax.ppermute(
            lax.slice_in_dim(block, block.shape[dim] - width, None, axis=dim), axis, forward
        )
        high = lax.ppermute(lax.slice_in_dim(block, 0, width, axis=dim), axis, backward)
        block = jnp.concatenate([low, block, high], axis=dim)
    return block


def slice_axis(array, start, count, along):
    return lax.slice_in_dim(array, start, start + count, axis=along)


def flux_sweep(padded, courant_pad, along, length):
    far_left = slice_axis(padded, 0, length + 3, along)
    near_left = slice_axis(padded, 1, length + 3, along)
    near_right = slice_axis(padded, 2, length + 3, along)
    far_right = slice_axis(padded, 3, length + 3, along)
    edges = 7.0 / 12.0 * (near_left + near_right) - 1.0 / 12.0 * (far_left + far_right)
    edges = jnp.minimum(
        jnp.maximum(edges, jnp.minimum(near_left, near_right)), jnp.maximum(near_left, near_right)
    )
    cell_means = slice_axis(padded, 2, length + 2, along)
    left_edge = slice_axis(edges, 0, length + 2, along)
    right_edge = slice_axis(edges, 1, length + 2, along)
    edge_jump = right_edge - left_edge
    curvature = 6.0 * cell_means - 3.0 * (left_edge + right_edge)
    courant = slice_axis(courant_pad, 3, length + 1, along)
    magnitude = jnp.abs(courant)
    from_left = slice_axis(right_edge, 0, length + 1, along) - 0.5 * courant * (
        slice_axis(edge_jump, 0, length + 1, along)
        - (1.0 - 2.0 / 3.0 * courant) * slice_axis(curvature, 0, length + 1, along)
    )
    from_right = slice_axis(left_edge, 1, length + 1, along) + 0.5 * magnitude * (
        slice_axis(edge_jump, 1, length + 1, along)
        + (1.0 - 2.0 / 3.0 * magnitude) * slice_axis(curvature, 1, length + 1, along)
    )
    face_flux = courant * jnp.where(courant >= 0.0, from_left, from_right)
    interior = slice_axis(padded, 3, length, along)
    return interior - (
        slice_axis(face_flux, 1, length, along) - slice_axis(face_flux, 0, length, along)
    )


def wrap_pad(array, along):
    extent = array.shape[along]
    return jnp.concatenate(
        [slice_axis(array, extent - 3, 3, along), array, slice_axis(array, 0, 3, along)], axis=along
    )


def two_halves(values):
    high = values.astype(jnp.bfloat16)
    low = (values - high.astype(jnp.float32)).astype(jnp.bfloat16)
    return jnp.concatenate([high, low], axis=1)


def dot32(left, right, dims=((1,), (0,)), precision=None):
    return lax.dot_general(
        left, right, (dims, ((), ())), precision=precision, preferred_element_type=jnp.float32
    )


def chem_kernel(*refs):
    sources, (out, rates, pick, spread, state, least, most, warmth) = refs[:8], refs[8:16]
    amounts, anomaly, solar, counts, speed, response, photo, recipe = held = refs[16:24]
    copies = [
        pltpu.make_async_copy(source, here, refs[24].at[index])
        for index, (source, here) in enumerate(zip(sources, held))
    ]
    for copy in copies:
        copy.start()
    for copy in copies:
        copy.wait()
    rows, columns, levels = anomaly.shape
    cells, species = state.shape
    width = rows * columns
    chunks = rates.shape[0]
    for row in range(rows):
        warmth[row * columns : (row + 1) * columns, :] = anomaly[row]
    place = lax.broadcasted_iota(jnp.int32, (width, species), 0)
    sunlight = jnp.zeros((width, species), jnp.float32)
    count = jnp.zeros((width, species), jnp.int32)
    longest = jnp.int32(0)
    for column in range(width):
        here = place == column
        spot = (column // columns, column % columns)
        sunlight = jnp.where(here, solar[spot], sunlight)
        count = jnp.where(here, counts[spot], count)
        longest = jnp.maximum(longest, counts[spot])
    ids = lax.broadcasted_iota(jnp.int32, (species, species), 0)
    for chunk in range(chunks):
        part = pl.ds(chunk * species, species)
        hits = [
            (recipe[row : row + 1, part] == ids).astype(jnp.float32) for row in range(4)
        ]
        taking = jnp.concatenate([hits[0], hits[1]], axis=1).astype(jnp.bfloat16)
        pick[chunk] = jnp.concatenate([taking, taking], axis=0)
        giving = jnp.concatenate(
            [jnp.transpose(hits[2] + hits[3]), jnp.transpose(hits[0] + hits[1])], axis=1
        ).astype(jnp.bfloat16)
        spread[chunk] = jnp.concatenate([giving, giving], axis=0)
    for level in range(levels):
        block = pl.ds(level * width, width)
        heat = jnp.broadcast_to(warmth[:, level : level + 1], (width, species))
        for chunk in range(chunks):
            part = pl.ds(chunk * species, species)
            rates[chunk, block, :] = (
                speed[:, part] * jnp.exp(response[:, part] * heat) + photo[:, part] * sunlight
            )

    def start():
        for level in range(levels):
            state[pl.ds(level * width, width), :] = amounts[pl.ds(level, width, stride=levels), :]

    def tiled(values):
        return jnp.concatenate([values] * levels, axis=0)

    start()
    substep = 1.0 / count.astype(jnp.float32)
    least[...] = state[...]
    most[...] = state[...]

    def advance(step, carry):
        current = state[...]
        least[...] = jnp.minimum(least[...], current)
        most[...] = jnp.maximum(most[...], current)
        pair = two_halves(current)
        flows = []
        for chunk in range(chunks):
            taken = dot32(pair, pick[chunk])
            flows.append(two_halves(rates[chunk] * taken[:, :species] * taken[:, species:]))
        total = dot32(jnp.concatenate(flows, axis=1), spread[...].reshape(-1, 2 * species))
        produced = total[:, :species]
        consumed = total[:, species:]
        size = tiled(substep)
        updated = (current + size * produced) / (current + size * consumed) * current
        state[...] = jnp.where(tiled(count) > step, updated, current)
        return carry

    lax.fori_loop(0, longest, advance, 0)
    usual = (jnp.min(least[...]) >= FAST_LEAST) & (jnp.max(most[...]) <= FAST_MOST)

    @pl.when(jnp.logical_not(usual))
    def _():
        start()

        def advance_fully(step, carry):
            current = state[...]
            produced = jnp.zeros((cells, species), jnp.float32)
            lost = jnp.zeros((cells, species), jnp.float32)
            for chunk in range(chunks):
                first_hit = pick[chunk, :species, :species].astype(jnp.float32)
                second_hit = pick[chunk, :species, species:].astype(jnp.float32)
                making = spread[chunk, :species, :species].astype(jnp.float32)
                first = dot32(current, first_hit, precision=HIGHEST)
                second = dot32(current, second_hit, precision=HIGHEST)
                rate = rates[chunk]
                produced += dot32(rate * first * second, making, precision=HIGHEST)
                lost += dot32(rate * second, first_hit, ((1,), (1,)), HIGHEST)
                lost += dot32(rate * first, second_hit, ((1,), (1,)), HIGHEST)
            size = tiled(substep)
            updated = (current + size * produced) / (1.0 + size * lost)
            state[...] = jnp.where(tiled(count) > step, updated, current)
            return carry

        lax.fori_loop(0, longest, advance_fully, 0)

    for level in range(levels):
        out[pl.ds(level, width, stride=levels), :] = state[pl.ds(level * width, width), :]


def react(operands):
    cells, species = operands[0].shape
    rows, columns, levels = operands[1].shape
    chunks = operands[7].shape[1] // species
    in_vmem = pl.BlockSpec(memory_space=pltpu.VMEM)
    held = [
        (pltpu.SMEM if index in (2, 3) else pltpu.VMEM)(operand.shape, operand.dtype)
        for index, operand in enumerate(operands)
    ]
    table = pltpu.VMEM((chunks, 2 * species, 2 * species), jnp.bfloat16)
    field = pltpu.VMEM((cells, species), jnp.float32)
    return pl.pallas_call(
        chem_kernel,
        out_shape=jax.ShapeDtypeStruct((cells, species), jnp.float32),
        in_specs=[pl.BlockSpec(memory_space=pltpu.HBM)] * len(operands),
        out_specs=in_vmem,
        scratch_shapes=[
            pltpu.VMEM((chunks, cells, species), jnp.float32), table, table,
            field, field, field, pltpu.VMEM((rows * columns, levels), jnp.float32),
            *held, pltpu.SemaphoreType.DMA((len(operands),)),
        ],
        compiler_params=pltpu.CompilerParams(vmem_limit_bytes=67043328),
    )(*operands)


def others(bands, devices):
    return [(dy, dl) for dl in range(devices) for dy in range(bands) if (dy, dl) != (0, 0)]


def peer(bands, devices, dy, dl):
    band, block = lax.axis_index("lat"), lax.axis_index("lon")
    return (lax.rem(band + dy, bands), lax.rem(block + dl, devices))


def signal_peers(bands, devices):
    barrier = pltpu.get_barrier_semaphore()
    for dy, dl in others(bands, devices):
        pl.semaphore_signal(
            barrier, inc=1, device_id=peer(bands, devices, dy, dl),
            device_id_type=pl.DeviceIdType.MESH,
        )


def clipped_edge(far_left, near_left, near_right, far_right):
    edge = 7.0 / 12.0 * (near_left + near_right) - 1.0 / 12.0 * (far_left + far_right)
    return jnp.minimum(
        jnp.maximum(edge, jnp.minimum(near_left, near_right)), jnp.maximum(near_left, near_right)
    )


def face_flow(courant, before, edge, after, left_mean, right_mean):
    magnitude = jnp.abs(courant)
    rightward = courant >= 0.0
    other = jnp.where(rightward, before, after)
    mean = jnp.where(rightward, left_mean, right_mean)
    bend = 6.0 * mean - 3.0 * (other + edge)
    return courant * (
        edge + 0.5 * magnitude * ((other - edge) + (1.0 - 2.0 / 3.0 * magnitude) * bend)
    )


def halves(values):
    high = values.astype(jnp.bfloat16)
    return high, (values - high.astype(jnp.float32)).astype(jnp.bfloat16)


def substeps(groups, midway, state, number, log_rates, pick, spread, *results):
    sides = range(2)
    gathered = [results[side * groups : (side + 1) * groups] for side in sides]
    scattered = [results[(2 + side) * groups : (3 + side) * groups] for side in sides]
    tall = state.shape[0] // groups
    species = state.shape[1]

    def load_pick():
        for side in sides:
            pltpu.matmul_push_rhs(pick[side], 0, side)

    def load_spread():
        for side in sides:
            pltpu.matmul_push_rhs(spread[side], 1, side)

    def gather(group, logs):
        pair = jnp.concatenate(halves(jnp.maximum(logs, FLOOR_LOG)), axis=1)
        for side in sides:
            pltpu.matmul_acc_lhs(
                gathered[side][group], pair, load_staged_rhs=None if group else 0
            )

    load_pick()
    for group in range(groups):
        gather(group, jnp.log2(state[group * tall : (group + 1) * tall, :]))
    load_spread()

    def advance(step, carry):
        for group in range(groups):
            block = slice(group * tall, (group + 1) * tall)
            for side in sides:
                logs = pltpu.matmul_pop(gathered[side][group]) + log_rates[side, block, :]
                high, low = halves(jnp.exp2(logs))
                pltpu.matmul_acc_lhs(
                    scattered[side][group], high, load_staged_rhs=None if group else 1
                )
                pltpu.matmul_acc_lhs(scattered[side][group], low)
            if group == 0:
                load_spread()
        load_pick()
        for group in range(groups):
            block = slice(group * tall, (group + 1) * tall)
            total = pltpu.matmul_pop(scattered[0][group]) + pltpu.matmul_pop(scattered[1][group])
            current, count = state[block, :], number[block, :]
            above = count * current + total[:, :species]
            below = count + total[:, species:] * (1.0 / jnp.maximum(current, FLOOR))
            gather(group, jnp.log2(above) - jnp.log2(below))
            state[block, :] = jnp.where(count > step.astype(jnp.float32), above / below, current)
        return carry

    lax.fori_loop(0, MOST_SUBSTEPS // 2, advance, 0)
    midway()
    lax.fori_loop(MOST_SUBSTEPS // 2, MOST_SUBSTEPS, advance, 0)
    for side in sides:
        for group in range(groups):
            pltpu.matmul_pop(gathered[side][group])
        pltpu.matmul_acc_lhs(
            scattered[side][0], jnp.zeros((tall, 2 * species), jnp.bfloat16), load_staged_rhs=1
        )
        pltpu.matmul_pop(scattered[side][0])


def remote(source, target, send_sem, recv_sem, device):
    return pltpu.make_async_remote_copy(
        src_ref=source, dst_ref=target, send_sem=send_sem, recv_sem=recv_sem,
        device_id=device, device_id_type=pl.DeviceIdType.MESH,
    )


def wait_for_blocks(box, count, semaphore):
    most = box.at[pl.ds(0, count)]
    pltpu.make_async_copy(most, most, semaphore).wait()


def whole_kernel(bands, devices, *refs):
    sources, out = refs[:10], refs[10]
    amounts, anomaly, solar, counts, speed, response, photo, recipe, east, north = held = refs[11:21]
    log_rates, pick, spread, state, number, warmth, arrived = refs[21:28]
    inbox, outbox, back, wind_out, wind_in, turned, courants, grid, edges = refs[28:37]
    send_there, recv_there, send_wind, recv_wind, send_back, recv_back = refs[37:]
    width, levels = warmth.shape
    cells, species = state.shape
    longitudes = east.shape[2]
    members, segments = bands * SEGMENT, devices // SEGMENT
    per = levels // members
    tall = per * width
    band, home = lax.axis_index("lat"), lax.axis_index("lon")
    segment, corner = lax.div(home, SEGMENT), lax.rem(home, SEGMENT)
    member = band * SEGMENT + corner

    def holder(target, place):
        return (lax.div(target, SEGMENT), place * SEGMENT + lax.rem(target, SEGMENT))

    copies = [
        pltpu.make_async_copy(source, here, arrived.at[index])
        for index, (source, here) in enumerate(zip(sources, held))
    ]
    for copy in copies:
        copy.start()
    signal_peers(bands, devices)
    for copy in copies:
        copy.wait()
    rows, columns, _ = anomaly.shape
    for row in range(rows):
        warmth[row * columns : (row + 1) * columns, :] = anomaly[row]
    place = lax.broadcasted_iota(jnp.int32, (width, species), 0)
    sunlight = jnp.zeros((width, species), jnp.float32)
    count = jnp.zeros((width, species), jnp.int32)
    for column in range(width):
        here = place == column
        spot = (column // columns, column % columns)
        sunlight = jnp.where(here, solar[spot], sunlight)
        count = jnp.where(here, counts[spot], count)
    count = count.astype(jnp.float32)
    ids = lax.broadcasted_iota(jnp.int32, (species, species), 0)
    for chunk in range(4):
        part = pl.ds(chunk * species, species)
        hits = [(recipe[row : row + 1, part] == ids).astype(jnp.float32) for row in range(4)]
        taking, giving = hits[0] + hits[1], hits[2] + hits[3]
        side, spot = chunk // 2, chunk % 2 * species
        for copy in range(2):
            pick[side, copy * species : (copy + 1) * species, spot : spot + species] = (
                taking.astype(jnp.bfloat16)
            )
        spread[side, spot : spot + species, :] = jnp.concatenate(
            [jnp.transpose(giving), jnp.transpose(taking)], axis=1
        ).astype(jnp.bfloat16)
    for level in range(levels):
        block = pl.ds(level * width, width)
        heat = jnp.broadcast_to(warmth[:, level : level + 1], (width, species))
        for chunk in range(4):
            part = pl.ds(chunk * species, species)
            log_rates[chunk // 2, block, chunk % 2 * species : (chunk % 2 + 1) * species] = jnp.log2(
                speed[:, part] * jnp.exp(response[:, part] * heat) + photo[:, part] * sunlight
            )
        state[block, :] = amounts[pl.ds(level, width, stride=levels), :]
        number[block, :] = count

    wind_out[...] = jnp.zeros_like(wind_out)
    wind_out[0:rows, 0:longitudes] = east[0]
    wind_out[rows : 2 * rows, 0:longitudes] = north[0]
    wind_member = lax.div(home, per)
    wind_slot = lax.rem(home, per) * bands + band
    stays = wind_member == member

    def wind_copy(step):
        return remote(
            wind_out, wind_in.at[wind_slot], send_wind.at[step], recv_wind.at[wind_slot],
            holder(wind_member, lax.rem(segment + step, segments)),
        )

    def send_winds():
        pl.semaphore_wait(pltpu.get_barrier_semaphore(), bands * devices - 1)
        for step in range(1, segments):
            wind_copy(step).start()

        @pl.when(stays)
        def _():
            pltpu.make_async_copy(wind_out, wind_in.at[wind_slot], recv_wind.at[wind_slot]).start()

        @pl.when(jnp.logical_not(stays))
        def _():
            wind_copy(0).start()

    groups = cells // 32
    pl.run_scoped(
        functools.partial(substeps, groups, send_winds, state, number, log_rates, pick, spread),
        *[
            pltpu.ACC(side)((32, 2 * species), jnp.float32)
            for use in range(2)
            for side in range(2)
            for group in range(groups)
        ],
    )

    lower = corner < SEGMENT // 2
    beside = lax.rem(segment + jnp.where(lower, segments - 1, 1), segments)
    beside_slot = band * 2 * SEGMENT + lax.rem(corner + 3 * SEGMENT // 2, 2 * SEGMENT)
    own_slot = band * 2 * SEGMENT + corner + SEGMENT // 2

    def rows_for(target):
        return pl.ds(pl.multiple_of(target * tall, tall), tall)

    for place, slot, first in ((beside, beside_slot, 0), (segment, own_slot, 1)):
        for step in range(first, members):
            target = lax.rem(member + step, members)
            remote(
                state.at[rows_for(target)], inbox.at[slot], send_there.at[0], recv_there.at[0],
                holder(target, place),
            ).start()
    inbox[own_slot] = state[rows_for(member), :]

    for step in range(1, segments):
        wind_copy(step).wait_send()

    @pl.when(jnp.logical_not(stays))
    def _():
        wind_copy(0).wait_send()

    for slot in range(per * bands):
        pltpu.make_async_copy(wind_out, wind_in.at[slot], recv_wind.at[slot]).wait()
    wide = wind_out.shape[1]
    winds = [wind_in[slot] for slot in range(per * bands)]
    winds.append(jnp.zeros((wide - per * bands * 2 * rows, wide), jnp.float32))
    upright = jnp.transpose(jnp.concatenate(winds, axis=0))[0:longitudes]
    turned[0:longitudes, :] = upright
    turned[longitudes : 2 * longitudes, :] = upright
    halo = SEGMENT // 2 * columns
    window = 4 * halo
    lats = bands * rows
    start = lax.rem(segment * 2 * halo + longitudes - halo, longitudes)
    view = turned[pl.ds(pl.multiple_of(start, 8), window), :]
    for lat in range(lats):
        for kind in range(2):
            for level in range(per):
                lane = (level * bands + lat // rows) * 2 * rows + kind * rows + lat % rows
                courants[kind, lat, level * window : (level + 1) * window, :] = jnp.broadcast_to(
                    view[:, lane : lane + 1], (window, species)
                )
    wait_for_blocks(inbox, 2 * members - 1, send_there.at[0])
    wait_for_blocks(inbox, 2 * members - 1, recv_there.at[0])

    extent = per * window
    for lat in range(lats):
        for level in range(per):
            for piece in range(2 * SEGMENT):
                to = 8 + level * window + piece * columns
                at = level * width + lat % rows * columns
                grid[lat, to : to + columns, :] = inbox[
                    lat // rows * 2 * SEGMENT + piece, at : at + columns, :
                ]
    planes = [grid[lat, 8 : 8 + extent, :] for lat in range(lats)]
    empty = jnp.zeros((extent, species), jnp.float32)
    for sweep_index in range(ADV_STEPS):
        swept = []
        for lat in range(lats):
            mean = planes[lat]
            grid[lat, 8 : 8 + extent, :] = mean

            def shifted(buffer, shift):
                return buffer[lat, 8 + shift : 8 + shift + extent, :]

            left_mean = shifted(grid, -1)
            edge = clipped_edge(shifted(grid, -2), left_mean, mean, shifted(grid, 1))
            edges[lat, 8 : 8 + extent, :] = edge
            flow = face_flow(
                courants[0, lat], shifted(edges, -1), edge, shifted(edges, 1), left_mean, mean
            )
            grid[lat, 8 : 8 + extent, :] = flow
            swept.append(mean - (shifted(grid, 1) - flow))
        padded = [empty, empty] + swept + [empty, empty]
        rims = [clipped_edge(*padded[lat : lat + 4]) for lat in range(lats + 1)]
        flows = [
            face_flow(
                courants[1, lat], rims[lat - 1], rims[lat], rims[lat + 1],
                swept[lat - 1], swept[lat],
            )
            for lat in range(1, lats)
        ]
        flows = [empty] + flows + [empty]
        planes = [swept[lat] - (flows[lat + 1] - flows[lat]) for lat in range(lats)]
    for lat in range(lats):
        grid[lat, 8 : 8 + extent, :] = planes[lat]
        for level in range(per):
            for piece in range(SEGMENT):
                at = 8 + level * window + halo + piece * columns
                to = level * width + lat % rows * columns
                outbox[lat // rows * SEGMENT + piece, to : to + columns, :] = grid[
                    lat, at : at + columns, :
                ]
    for step in range(1, members):
        target = lax.rem(member + step, members)
        remote(
            outbox.at[target], back.at[member], send_back.at[0], recv_back.at[0],
            holder(target, segment),
        ).start()
    back[member] = outbox[member]
    wait_for_blocks(outbox, members - 1, send_back.at[0])
    wait_for_blocks(back, members - 1, recv_back.at[0])
    for level in range(levels):
        at = level % per * width
        out[pl.ds(level, width, stride=levels), :] = back[level // per, at : at + width, :]


def react_and_advect(operands):
    bands, devices = lax.axis_size("lat"), lax.axis_size("lon")
    cells, species = operands[0].shape
    rows, columns, levels = operands[1].shape
    longitudes = operands[8].shape[2]
    members, segments = bands * SEGMENT, devices // SEGMENT
    per = levels // members
    lats, extent, tall = bands * rows, per * 2 * SEGMENT * columns, per * rows * columns
    wide = -(-longitudes // 128) * 128
    held = [
        (pltpu.SMEM if index in (2, 3) else pltpu.VMEM)(operand.shape, operand.dtype)
        for index, operand in enumerate(operands)
    ]
    one_semaphore = pltpu.SemaphoreType.DMA((1,))
    box = pltpu.VMEM((members, tall, species), jnp.float32)
    padded = pltpu.VMEM((lats, extent + 16, species), jnp.float32)
    table = pltpu.VMEM((2, 2 * species, 2 * species), jnp.bfloat16)
    field = pltpu.VMEM((cells, species), jnp.float32)
    return pl.pallas_call(
        functools.partial(whole_kernel, bands, devices),
        out_shape=jax.ShapeDtypeStruct((cells, species), jnp.float32),
        in_specs=[pl.BlockSpec(memory_space=pltpu.HBM)] * len(operands),
        out_specs=pl.BlockSpec(memory_space=pltpu.VMEM),
        scratch_shapes=[
            *held,
            pltpu.VMEM((2, cells, 2 * species), jnp.float32), table, table, field, field,
            pltpu.VMEM((rows * columns, levels), jnp.float32),
            pltpu.SemaphoreType.DMA((len(operands),)),
            pltpu.VMEM((2 * members, tall, species), jnp.float32), box, box,
            pltpu.VMEM((2 * rows, wide), jnp.float32),
            pltpu.VMEM((per * bands, 2 * rows, wide), jnp.float32),
            pltpu.VMEM((2 * longitudes, wide), jnp.float32),
            pltpu.VMEM((2, lats, extent, species), jnp.float32), padded, padded,
            one_semaphore, one_semaphore, pltpu.SemaphoreType.DMA((segments,)),
            pltpu.SemaphoreType.DMA((per * bands,)), one_semaphore, one_semaphore,
        ],
        compiler_params=pltpu.CompilerParams(
            collective_id=0, has_side_effects=True, vmem_limit_bytes=32 << 20,
        ),
    )(*[pltpu.with_memory_space_constraint(operand, pltpu.HBM) for operand in operands])


def per_device(
    species_amounts,
    thermal_anomaly,
    solar_flux_factor,
    inner_iterations,
    reference_speed,
    thermal_response,
    photo_breakup,
    reaction_recipe,
    eastward_wind_ratio,
    northward_wind_ratio,
):
    rows, columns, levels, species = species_amounts.shape
    devices = lax.axis_size("lon")
    longitudes = eastward_wind_ratio.shape[2]
    reactions = reaction_recipe.shape[1]
    operands = (
        species_amounts.reshape(-1, species), thermal_anomaly, solar_flux_factor,
        inner_iterations, reference_speed.reshape(1, -1), thermal_response.reshape(1, -1),
        photo_breakup.reshape(1, -1), reaction_recipe,
    )
    bands = lax.axis_size("lat")
    halo = SEGMENT // 2 * columns
    tabled = species == 128 and reactions == 4 * species and rows * columns * levels <= 2 * species
    split = levels == devices and levels % (bands * SEGMENT) == 0 and devices % (2 * SEGMENT) == 0
    aligned = rows * columns % 16 == 0 and halo % 8 == 0 and longitudes <= 128
    if tabled and split and aligned and halo >= 3 * ADV_STEPS:
        moved = react_and_advect((*operands, eastward_wind_ratio, northward_wind_ratio))
        return moved.reshape(species_amounts.shape)
    settled_columns = react(operands).reshape(species_amounts.shape)
    lat_rows = species_amounts.shape[0]
    row_ids = lax.axis_index("lat") * lat_rows + lax.broadcasted_iota(
        jnp.int32, (lat_rows, 1, 1, 1), 0
    )
    carried_quantity = lax.all_to_all(
        settled_columns, "lon", split_axis=2, concat_axis=1, tiled=True
    )
    east_faces = jnp.transpose(eastward_wind_ratio, (1, 2, 0))[..., None]
    south_faces = jnp.where(
        row_ids > 0, jnp.transpose(northward_wind_ratio, (1, 2, 0))[..., None], 0.0
    )
    east_pad = wrap_pad(east_faces, 1)
    for sweep_index in range(ADV_STEPS):
        carried_quantity = flux_sweep(
            wrap_pad(carried_quantity, 1), east_pad, 1, carried_quantity.shape[1]
        )
        rimmed, south_pad = (
            with_halo(carried_quantity, (("lat", 0),), 3),
            with_halo(south_faces, (("lat", 0),), 3),
        )
        carried_quantity = flux_sweep(rimmed, south_pad, 0, lat_rows)
    return lax.all_to_all(carried_quantity, "lon", split_axis=1, concat_axis=2, tiled=True)


def solution(mesh):
    return jax.shard_map(
        per_device,
        mesh=mesh,
        in_specs=(
            P("lat", "lon", None, None),
            P("lat", "lon", None),
            P("lat", "lon"),
            P("lat", "lon"),
            P(),
            P(),
            P(),
            P(),
            P("lon", "lat", None),
            P("lon", "lat", None),
        ),
        out_specs=P("lat", "lon", None, None),
        check_vma=False,
    )
```

```python
import functools
import jax
import jax.numpy as jnp
from jax import lax
from jax.experimental import pallas as pl
from jax.experimental.pallas import tpu as pltpu
from jax.sharding import PartitionSpec as P

ADV_STEPS = 2
FAST_LEAST = 1e-12
FAST_MOST = 1e8
HIGHEST = lax.Precision.HIGHEST
MOST_SUBSTEPS = 36
FLOOR = 1e-20
FLOOR_LOG = -66.43856


def with_halo(block, sides, width):
    for axis, dim in sides:
        count = lax.axis_size(axis)
        forward = [(i, i + 1) for i in range(count - 1)]
        backward = [(target, source) for source, target in forward]
        low = lax.ppermute(
            lax.slice_in_dim(block, block.shape[dim] - width, None, axis=dim), axis, forward
        )
        high = lax.ppermute(lax.slice_in_dim(block, 0, width, axis=dim), axis, backward)
        block = jnp.concatenate([low, block, high], axis=dim)
    return block


def slice_axis(array, start, count, along):
    return lax.slice_in_dim(array, start, start + count, axis=along)


def flux_sweep(padded, courant_pad, along, length):
    far_left = slice_axis(padded, 0, length + 3, along)
    near_left = slice_axis(padded, 1, length + 3, along)
    near_right = slice_axis(padded, 2, length + 3, along)
    far_right = slice_axis(padded, 3, length + 3, along)
    edges = 7.0 / 12.0 * (near_left + near_right) - 1.0 / 12.0 * (far_left + far_right)
    edges = jnp.minimum(
        jnp.maximum(edges, jnp.minimum(near_left, near_right)), jnp.maximum(near_left, near_right)
    )
    cell_means = slice_axis(padded, 2, length + 2, along)
    left_edge = slice_axis(edges, 0, length + 2, along)
    right_edge = slice_axis(edges, 1, length + 2, along)
    edge_jump = right_edge - left_edge
    curvature = 6.0 * cell_means - 3.0 * (left_edge + right_edge)
    courant = slice_axis(courant_pad, 3, length + 1, along)
    magnitude = jnp.abs(courant)
    from_left = slice_axis(right_edge, 0, length + 1, along) - 0.5 * courant * (
        slice_axis(edge_jump, 0, length + 1, along)
        - (1.0 - 2.0 / 3.0 * courant) * slice_axis(curvature, 0, length + 1, along)
    )
    from_right = slice_axis(left_edge, 1, length + 1, along) + 0.5 * magnitude * (
        slice_axis(edge_jump, 1, length + 1, along)
        + (1.0 - 2.0 / 3.0 * magnitude) * slice_axis(curvature, 1, length + 1, along)
    )
    face_flux = courant * jnp.where(courant >= 0.0, from_left, from_right)
    interior = slice_axis(padded, 3, length, along)
    return interior - (
        slice_axis(face_flux, 1, length, along) - slice_axis(face_flux, 0, length, along)
    )


def wrap_pad(array, along):
    extent = array.shape[along]
    return jnp.concatenate(
        [slice_axis(array, extent - 3, 3, along), array, slice_axis(array, 0, 3, along)], axis=along
    )


def two_halves(values):
    high = values.astype(jnp.bfloat16)
    low = (values - high.astype(jnp.float32)).astype(jnp.bfloat16)
    return jnp.concatenate([high, low], axis=1)


def dot32(left, right, dims=((1,), (0,)), precision=None):
    return lax.dot_general(
        left, right, (dims, ((), ())), precision=precision, preferred_element_type=jnp.float32
    )


def chem_kernel(*refs):
    sources, (out, rates, pick, spread, state, least, most, warmth) = refs[:8], refs[8:16]
    amounts, anomaly, solar, counts, speed, response, photo, recipe = held = refs[16:24]
    copies = [
        pltpu.make_async_copy(source, here, refs[24].at[index])
        for index, (source, here) in enumerate(zip(sources, held))
    ]
    for copy in copies:
        copy.start()
    for copy in copies:
        copy.wait()
    rows, columns, levels = anomaly.shape
    cells, species = state.shape
    width = rows * columns
    chunks = rates.shape[0]
    for row in range(rows):
        warmth[row * columns : (row + 1) * columns, :] = anomaly[row]
    place = lax.broadcasted_iota(jnp.int32, (width, species), 0)
    sunlight = jnp.zeros((width, species), jnp.float32)
    count = jnp.zeros((width, species), jnp.int32)
    longest = jnp.int32(0)
    for column in range(width):
        here = place == column
        spot = (column // columns, column % columns)
        sunlight = jnp.where(here, solar[spot], sunlight)
        count = jnp.where(here, counts[spot], count)
        longest = jnp.maximum(longest, counts[spot])
    ids = lax.broadcasted_iota(jnp.int32, (species, species), 0)
    for chunk in range(chunks):
        part = pl.ds(chunk * species, species)
        hits = [
            (recipe[row : row + 1, part] == ids).astype(jnp.float32) for row in range(4)
        ]
        taking = jnp.concatenate([hits[0], hits[1]], axis=1).astype(jnp.bfloat16)
        pick[chunk] = jnp.concatenate([taking, taking], axis=0)
        giving = jnp.concatenate(
            [jnp.transpose(hits[2] + hits[3]), jnp.transpose(hits[0] + hits[1])], axis=1
        ).astype(jnp.bfloat16)
        spread[chunk] = jnp.concatenate([giving, giving], axis=0)
    for level in range(levels):
        block = pl.ds(level * width, width)
        heat = jnp.broadcast_to(warmth[:, level : level + 1], (width, species))
        for chunk in range(chunks):
            part = pl.ds(chunk * species, species)
            rates[chunk, block, :] = (
                speed[:, part] * jnp.exp(response[:, part] * heat) + photo[:, part] * sunlight
            )

    def start():
        for level in range(levels):
            state[pl.ds(level * width, width), :] = amounts[pl.ds(level, width, stride=levels), :]

    def tiled(values):
        return jnp.concatenate([values] * levels, axis=0)

    start()
    substep = 1.0 / count.astype(jnp.float32)
    least[...] = state[...]
    most[...] = state[...]

    def advance(step, carry):
        current = state[...]
        least[...] = jnp.minimum(least[...], current)
        most[...] = jnp.maximum(most[...], current)
        pair = two_halves(current)
        flows = []
        for chunk in range(chunks):
            taken = dot32(pair, pick[chunk])
            flows.append(two_halves(rates[chunk] * taken[:, :species] * taken[:, species:]))
        total = dot32(jnp.concatenate(flows, axis=1), spread[...].reshape(-1, 2 * species))
        produced = total[:, :species]
        consumed = total[:, species:]
        size = tiled(substep)
        updated = (current + size * produced) / (current + size * consumed) * current
        state[...] = jnp.where(tiled(count) > step, updated, current)
        return carry

    lax.fori_loop(0, longest, advance, 0)
    usual = (jnp.min(least[...]) >= FAST_LEAST) & (jnp.max(most[...]) <= FAST_MOST)

    @pl.when(jnp.logical_not(usual))
    def _():
        start()

        def advance_fully(step, carry):
            current = state[...]
            produced = jnp.zeros((cells, species), jnp.float32)
            lost = jnp.zeros((cells, species), jnp.float32)
            for chunk in range(chunks):
                first_hit = pick[chunk, :species, :species].astype(jnp.float32)
                second_hit = pick[chunk, :species, species:].astype(jnp.float32)
                making = spread[chunk, :species, :species].astype(jnp.float32)
                first = dot32(current, first_hit, precision=HIGHEST)
                second = dot32(current, second_hit, precision=HIGHEST)
                rate = rates[chunk]
                produced += dot32(rate * first * second, making, precision=HIGHEST)
                lost += dot32(rate * second, first_hit, ((1,), (1,)), HIGHEST)
                lost += dot32(rate * first, second_hit, ((1,), (1,)), HIGHEST)
            size = tiled(substep)
            updated = (current + size * produced) / (1.0 + size * lost)
            state[...] = jnp.where(tiled(count) > step, updated, current)
            return carry

        lax.fori_loop(0, longest, advance_fully, 0)

    for level in range(levels):
        out[pl.ds(level, width, stride=levels), :] = state[pl.ds(level * width, width), :]


def react(operands):
    cells, species = operands[0].shape
    rows, columns, levels = operands[1].shape
    chunks = operands[7].shape[1] // species
    in_vmem = pl.BlockSpec(memory_space=pltpu.VMEM)
    held = [
        (pltpu.SMEM if index in (2, 3) else pltpu.VMEM)(operand.shape, operand.dtype)
        for index, operand in enumerate(operands)
    ]
    table = pltpu.VMEM((chunks, 2 * species, 2 * species), jnp.bfloat16)
    field = pltpu.VMEM((cells, species), jnp.float32)
    return pl.pallas_call(
        chem_kernel,
        out_shape=jax.ShapeDtypeStruct((cells, species), jnp.float32),
        in_specs=[pl.BlockSpec(memory_space=pltpu.HBM)] * len(operands),
        out_specs=in_vmem,
        scratch_shapes=[
            pltpu.VMEM((chunks, cells, species), jnp.float32), table, table,
            field, field, field, pltpu.VMEM((rows * columns, levels), jnp.float32),
            *held, pltpu.SemaphoreType.DMA((len(operands),)),
        ],
        compiler_params=pltpu.CompilerParams(vmem_limit_bytes=67043328),
    )(*operands)


def others(bands, devices):
    return [(dy, dl) for dl in range(devices) for dy in range(bands) if (dy, dl) != (0, 0)]


def peer(bands, devices, dy, dl):
    band, block = lax.axis_index("lat"), lax.axis_index("lon")
    return (lax.rem(band + dy, bands), lax.rem(block + dl, devices))


def flipped(position, mask, count):
    bits = [1 << bit for bit in range(count.bit_length() - 1)]
    return sum(lax.rem(position // bit + mask // bit, 2) * bit for bit in bits)


def mirror(bands, devices, dy, dl):
    band, block = lax.axis_index("lat"), lax.axis_index("lon")
    return (flipped(band, dy, bands), flipped(block, dl, devices))


def mirrored(bands, devices):
    pairs = [(dy, dl) for dl in range(devices) for dy in range(bands)]
    quarter = devices // 4

    def turn(pair):
        return (-pair[0], -(pair[1] % quarter), (3, 1, 2, 0).index(pair[1] // quarter))

    pairs.sort(key=turn)
    return [p for p in pairs if p != (0, 0)]


def signal_peers(bands, devices):
    barrier = pltpu.get_barrier_semaphore()
    for dy, dl in others(bands, devices):
        pl.semaphore_signal(
            barrier, inc=1, device_id=peer(bands, devices, dy, dl),
            device_id_type=pl.DeviceIdType.MESH,
        )


def wrap_rows(buffer, slot, values, half):
    extent = values.shape[0]
    buffer[slot, 8 : 8 + extent, :] = values
    buffer[slot, 0:8, :] = pltpu.roll(values[extent - 8 :], half, 1)
    buffer[slot, 8 + extent : 16 + extent, :] = pltpu.roll(values[:8], half, 1)


def clipped_edge(far_left, near_left, near_right, far_right):
    edge = 7.0 / 12.0 * (near_left + near_right) - 1.0 / 12.0 * (far_left + far_right)
    return jnp.minimum(
        jnp.maximum(edge, jnp.minimum(near_left, near_right)), jnp.maximum(near_left, near_right)
    )


def face_weights(courant):
    magnitude = jnp.abs(courant)
    slope = 1.0 - 2.0 / 3.0 * magnitude
    half = 0.5 * magnitude * courant
    return courant - half * (1.0 + 3.0 * slope), half * (1.0 - 3.0 * slope), 6.0 * slope * half


def face_flow(weights, before, edge, after, left_mean, right_mean):
    on_edge, on_other, on_mean = weights
    rightward = on_mean >= 0.0
    other = jnp.where(rightward, before, after)
    mean = jnp.where(rightward, left_mean, right_mean)
    return on_edge * edge + on_other * other + on_mean * mean


def move_kernel(
    bands, devices, packed, east, north, out,
    inbox, outbox, back, wind_out, wind_in, courants, grid, edges,
    send_there, recv_there, send_wind, recv_wind, send_back, recv_back,
):
    band, block = lax.axis_index("lat"), lax.axis_index("lon")
    _, rows, longitudes = east.shape
    species = packed.shape[2]
    levels = packed.shape[0] // bands
    half = species // 2
    columns = longitudes // devices
    extent = longitudes // 2
    lats = bands * rows
    low_rows = rows // 2
    offsets = others(bands, devices)

    def remote(source, target, send_sem, recv_sem, device):
        return pltpu.make_async_remote_copy(
            src_ref=source, dst_ref=target, send_sem=send_sem, recv_sem=recv_sem,
            device_id=device, device_id_type=pl.DeviceIdType.MESH,
        )

    wind_out[...] = jnp.zeros_like(wind_out)
    wind_out[0:rows, 0:longitudes] = east[0]
    wind_out[rows : 2 * rows, 0:longitudes] = north[0]
    wind_in[band] = wind_out[...]
    inbox[band * devices + block] = packed[block * bands + band]
    pl.semaphore_wait(pltpu.get_barrier_semaphore(), len(offsets))

    winds = []
    for dy in range(1, bands):
        copy = remote(
            wind_out, wind_in.at[band], send_wind.at[dy], recv_wind.at[dy],
            peer(bands, devices, dy, 0),
        )
        copy.start()
        winds.append(copy)
    def wait_for_all(box, semaphore):
        most = box.at[pl.ds(0, len(offsets))]
        pltpu.make_async_copy(most, most, semaphore.at[0]).wait()

    for dy, dl in mirrored(bands, devices):
        device = mirror(bands, devices, dy, dl)
        remote(
            packed.at[device[1] * bands + device[0]], inbox.at[band * devices + block],
            send_there.at[0], recv_there.at[0], device,
        ).start()

    for copy in winds:
        copy.wait()
    near_tall = lax.broadcasted_iota(jnp.int32, (extent, species), 1) < half
    wide = wind_out.shape[1]
    tall = [wind_in[y] for y in range(bands)]
    tall.append(jnp.zeros((wide - bands * 2 * rows, wide), jnp.float32))
    weights = face_weights(jnp.transpose(jnp.concatenate(tall, axis=0))[0 : 2 * extent])
    for lat in range(lats):
        for kind in range(2):
            lane = lat // rows * 2 * rows + kind * rows + lat % rows
            columns_of = [weight[:, lane : lane + 1] for weight in weights]
            for index, column in enumerate(columns_of):
                courants[kind, lat, index] = jnp.where(
                    near_tall,
                    jnp.broadcast_to(column[0:extent], (extent, species)),
                    jnp.broadcast_to(column[extent : 2 * extent], (extent, species)),
                )
    wait_for_all(packed, send_there)
    wait_for_all(inbox, recv_there)

    near = lax.broadcasted_iota(jnp.int32, (low_rows * columns, species), 1) < half

    def swap_pair(first, second):
        return (
            jnp.where(near, first, pltpu.roll(second, half, 1)),
            jnp.where(near, pltpu.roll(first, half, 1), second),
        )

    for y in range(bands):
        for spot in range(devices // 2):
            pair = swap_pair(
                inbox[y * devices + spot], inbox[y * devices + spot + devices // 2]
            )
            for high in range(2):
                for low in range(low_rows):
                    lat = y * rows + high * low_rows + low
                    grid[lat, 8 + spot * columns : 8 + (spot + 1) * columns, :] = pair[high][
                        low * columns : (low + 1) * columns
                    ]
    planes = [grid[lat, 8 : 8 + extent, :] for lat in range(lats)]
    empty = jnp.zeros((extent, species), jnp.float32)
    for sweep_index in range(ADV_STEPS):
        swept = []
        for lat in range(lats):
            mean = planes[lat]
            wrap_rows(grid, lat, mean, half)

            def shifted(buffer, shift):
                return buffer[lat, 8 + shift : 8 + shift + extent, :]

            left_mean = shifted(grid, -1)
            edge = clipped_edge(shifted(grid, -2), left_mean, mean, shifted(grid, 1))
            wrap_rows(edges, lat, edge, half)
            flow = face_flow(
                [courants[0, lat, index] for index in range(3)], shifted(edges, -1), edge, shifted(edges, 1), left_mean, mean
            )
            wrap_rows(grid, lat, flow, half)
            swept.append(mean - (shifted(grid, 1) - flow))
        padded = [empty, empty] + swept + [empty, empty]
        rims = [clipped_edge(*padded[lat : lat + 4]) for lat in range(lats + 1)]
        flows = [
            face_flow(
                [courants[1, lat, index] for index in range(3)], rims[lat - 1], rims[lat], rims[lat + 1],
                swept[lat - 1], swept[lat],
            )
            for lat in range(1, lats)
        ]
        flows = [empty] + flows + [empty]
        planes = [swept[lat] - (flows[lat + 1] - flows[lat]) for lat in range(lats)]
    for lat in range(lats):
        grid[lat, 8 : 8 + extent, :] = planes[lat]
    for y in range(bands):
        for spot in range(devices // 2):
            sides = [
                jnp.concatenate(
                    [
                        grid[
                            y * rows + high * low_rows + low,
                            8 + spot * columns : 8 + (spot + 1) * columns,
                            :,
                        ]
                        for low in range(low_rows)
                    ],
                    axis=0,
                )
                for high in range(2)
            ]
            place = y * devices + spot
            outbox[place], outbox[place + devices // 2] = swap_pair(*sides)
    back[block * bands + band] = outbox[band * devices + block]
    for dy, dl in offsets:
        device = peer(bands, devices, dy, dl)
        remote(
            outbox.at[device[0] * devices + device[1]], back.at[block * bands + band],
            send_back.at[0], recv_back.at[0], device,
        ).start()
    wait_for_all(outbox, send_back)
    wait_for_all(back, recv_back)
    count = low_rows * columns
    for level in range(levels):
        front, behind = swap_pair(back[level * bands], back[level * bands + 1])
        out[pl.ds(level, count, stride=levels), :] = front
        out[pl.ds(count * levels + level, count, stride=levels), :] = behind


def halves(values):
    high = values.astype(jnp.bfloat16)
    return high, (values - high.astype(jnp.float32)).astype(jnp.bfloat16)


def substeps(groups, state, number, log_rates, pick, spread, *results):
    sides = range(2)
    gathered = [results[side * groups : (side + 1) * groups] for side in sides]
    scattered = [results[(2 + side) * groups : (3 + side) * groups] for side in sides]
    tall = state.shape[0] // groups
    species = state.shape[1]

    def load_pick():
        for side in sides:
            pltpu.matmul_push_rhs(pick[side], 0, side)

    def load_spread():
        for side in sides:
            pltpu.matmul_push_rhs(spread[side], 1, side)

    def gather(group, logs):
        pair = jnp.concatenate(halves(jnp.maximum(logs, FLOOR_LOG)), axis=1)
        for side in sides:
            pltpu.matmul_acc_lhs(
                gathered[side][group], pair, load_staged_rhs=None if group else 0
            )

    load_pick()
    for group in range(groups):
        gather(group, jnp.log2(state[group * tall : (group + 1) * tall, :]))
    load_spread()

    def advance(step, carry):
        for group in range(groups):
            block = slice(group * tall, (group + 1) * tall)
            for side in sides:
                logs = pltpu.matmul_pop(gathered[side][group]) + log_rates[side, block, :]
                high, low = halves(jnp.exp2(logs))
                pltpu.matmul_acc_lhs(
                    scattered[side][group], high, load_staged_rhs=None if group else 1
                )
                pltpu.matmul_acc_lhs(scattered[side][group], low)
            if group == 0:
                load_spread()
        load_pick()
        for group in range(groups):
            block = slice(group * tall, (group + 1) * tall)
            total = pltpu.matmul_pop(scattered[0][group]) + pltpu.matmul_pop(scattered[1][group])
            current, count = state[block, :], number[block, :]
            above = count * current + total[:, :species]
            below = count + total[:, species:] * (1.0 / jnp.maximum(current, FLOOR))
            gather(group, jnp.log2(above) - jnp.log2(below))
            state[block, :] = jnp.where(count > step.astype(jnp.float32), above / below, current)
        return carry

    lax.fori_loop(0, MOST_SUBSTEPS, advance, 0)
    for side in sides:
        for group in range(groups):
            pltpu.matmul_pop(gathered[side][group])
        pltpu.matmul_acc_lhs(
            scattered[side][0], jnp.zeros((tall, 2 * species), jnp.bfloat16), load_staged_rhs=1
        )
        pltpu.matmul_pop(scattered[side][0])


def whole_kernel(bands, devices, *refs):
    sources, out = refs[:10], refs[10]
    amounts, anomaly, solar, counts, speed, response, photo, recipe, east, north = held = refs[11:21]
    log_rates, pick, spread, state, number, warmth, arrived, packed = refs[21:29]
    move_refs = refs[29:]
    width = warmth.shape[0]
    cells, species = state.shape
    levels = cells // width

    copies = [
        pltpu.make_async_copy(source, here, arrived.at[index])
        for index, (source, here) in enumerate(zip(sources, held))
    ]
    for copy in copies[7:] + copies[:7]:
        copy.start()
    signal_peers(bands, devices)
    copies[7].wait()
    ids = lax.broadcasted_iota(jnp.int32, (species, species), 0)
    for chunk in range(4):
        part = pl.ds(chunk * species, species)
        hits = [(recipe[row : row + 1, part] == ids).astype(jnp.float32) for row in range(4)]
        taking, giving = hits[0] + hits[1], hits[2] + hits[3]
        side, spot = chunk // 2, chunk % 2 * species
        for copy in range(2):
            pick[side, copy * species : (copy + 1) * species, spot : spot + species] = (
                taking.astype(jnp.bfloat16)
            )
        spread[side, spot : spot + species, :] = jnp.concatenate(
            [jnp.transpose(giving), jnp.transpose(taking)], axis=1
        ).astype(jnp.bfloat16)
    for copy in copies[1:7] + copies[8:]:
        copy.wait()
    rows, columns, _ = anomaly.shape
    for row in range(rows):
        warmth[row * columns : (row + 1) * columns, :] = anomaly[row]
    place = lax.broadcasted_iota(jnp.int32, (width, species), 0)
    sunlight = jnp.zeros((width, species), jnp.float32)
    count = jnp.zeros((width, species), jnp.int32)
    for column in range(width):
        here = place == column
        spot = (column // columns, column % columns)
        sunlight = jnp.where(here, solar[spot], sunlight)
        count = jnp.where(here, counts[spot], count)
    count = count.astype(jnp.float32)
    for level in range(levels):
        block = pl.ds(level * width, width)
        heat = jnp.broadcast_to(warmth[:, level : level + 1], (width, species))
        for chunk in range(4):
            part = pl.ds(chunk * species, species)
            log_rates[chunk // 2, block, chunk % 2 * species : (chunk % 2 + 1) * species] = jnp.log2(
                speed[:, part] * jnp.exp(response[:, part] * heat) + photo[:, part] * sunlight
            )
        number[block, :] = count
    copies[0].wait()
    for level in range(levels):
        state[pl.ds(level * width, width), :] = amounts[pl.ds(level, width, stride=levels), :]

    groups = cells // 32
    pl.run_scoped(
        functools.partial(substeps, groups, state, number, log_rates, pick, spread),
        *[
            pltpu.ACC(side)((32, 2 * species), jnp.float32)
            for use in range(2)
            for side in range(2)
            for group in range(groups)
        ],
    )

    half = species // 2
    near = lax.broadcasted_iota(jnp.int32, (width // 2, species), 1) < half
    for level in range(levels):
        front = state[pl.ds(level * width, width // 2), :]
        behind = state[pl.ds(level * width + width // 2, width // 2), :]
        packed[2 * level] = jnp.where(near, front, pltpu.roll(behind, half, 1))
        packed[2 * level + 1] = jnp.where(near, pltpu.roll(front, half, 1), behind)
    move_kernel(bands, devices, packed, east, north, out, *move_refs)


def react_and_advect(operands):
    bands, devices = lax.axis_size("lat"), lax.axis_size("lon")
    cells, species = operands[0].shape
    rows, columns, levels = operands[1].shape
    longitudes = operands[8].shape[2]
    lats, extent, count = bands * rows, longitudes // 2, rows * columns // 2
    wide = -(-longitudes // 128) * 128
    held = [
        (pltpu.SMEM if index in (2, 3) else pltpu.VMEM)(operand.shape, operand.dtype)
        for index, operand in enumerate(operands)
    ]
    semaphores = pltpu.SemaphoreType.DMA((1,))
    wind_semaphores = pltpu.SemaphoreType.DMA((bands,))
    box = pltpu.VMEM((bands * devices, count, species), jnp.float32)
    exchanged = pltpu.VMEM((levels * bands, count, species), jnp.float32)
    wrapped = pltpu.VMEM((lats, extent + 16, species), jnp.float32)
    table = pltpu.VMEM((2, 2 * species, 2 * species), jnp.bfloat16)
    field = pltpu.VMEM((cells, species), jnp.float32)
    return pl.pallas_call(
        functools.partial(whole_kernel, bands, devices),
        out_shape=jax.ShapeDtypeStruct((cells, species), jnp.float32),
        in_specs=[pl.BlockSpec(memory_space=pltpu.HBM)] * len(operands),
        out_specs=pl.BlockSpec(memory_space=pltpu.VMEM),
        scratch_shapes=[
            *held,
            pltpu.VMEM((2, cells, 2 * species), jnp.float32), table, table, field, field,
            pltpu.VMEM((rows * columns, levels), jnp.float32),
            pltpu.SemaphoreType.DMA((len(operands),)), exchanged,
            box, box, exchanged,
            pltpu.VMEM((2 * rows, wide), jnp.float32),
            pltpu.VMEM((bands, 2 * rows, wide), jnp.float32),
            pltpu.VMEM((2, lats, 3, extent, species), jnp.float32), wrapped, wrapped,
            semaphores, semaphores, wind_semaphores, wind_semaphores, semaphores, semaphores,
        ],
        compiler_params=pltpu.CompilerParams(
            collective_id=0, has_side_effects=True, vmem_limit_bytes=32 << 20,
        ),
    )(*[pltpu.with_memory_space_constraint(operand, pltpu.HBM) for operand in operands])


def per_device(
    species_amounts,
    thermal_anomaly,
    solar_flux_factor,
    inner_iterations,
    reference_speed,
    thermal_response,
    photo_breakup,
    reaction_recipe,
    eastward_wind_ratio,
    northward_wind_ratio,
):
    rows, columns, levels, species = species_amounts.shape
    devices = lax.axis_size("lon")
    longitudes = eastward_wind_ratio.shape[2]
    reactions = reaction_recipe.shape[1]
    operands = (
        species_amounts.reshape(-1, species), thermal_anomaly, solar_flux_factor,
        inner_iterations, reference_speed.reshape(1, -1), thermal_response.reshape(1, -1),
        photo_breakup.reshape(1, -1), reaction_recipe,
    )
    paired = lax.axis_size("lat") == 2 and levels == devices and rows % 2 == 0
    tabled = species == 128 and reactions == 4 * species and rows * columns % 16 == 0
    if paired and tabled and devices % 2 == 0 and longitudes <= 128:
        moved = react_and_advect((*operands, eastward_wind_ratio, northward_wind_ratio))
        return moved.reshape(species_amounts.shape)
    settled_columns = react(operands).reshape(species_amounts.shape)
    lat_rows = species_amounts.shape[0]
    row_ids = lax.axis_index("lat") * lat_rows + lax.broadcasted_iota(
        jnp.int32, (lat_rows, 1, 1, 1), 0
    )
    carried_quantity = lax.all_to_all(
        settled_columns, "lon", split_axis=2, concat_axis=1, tiled=True
    )
    east_faces = jnp.transpose(eastward_wind_ratio, (1, 2, 0))[..., None]
    south_faces = jnp.where(
        row_ids > 0, jnp.transpose(northward_wind_ratio, (1, 2, 0))[..., None], 0.0
    )
    east_pad = wrap_pad(east_faces, 1)
    for sweep_index in range(ADV_STEPS):
        carried_quantity = flux_sweep(
            wrap_pad(carried_quantity, 1), east_pad, 1, carried_quantity.shape[1]
        )
        rimmed, south_pad = (
            with_halo(carried_quantity, (("lat", 0),), 3),
            with_halo(south_faces, (("lat", 0),), 3),
        )
        carried_quantity = flux_sweep(rimmed, south_pad, 0, lat_rows)
    return lax.all_to_all(carried_quantity, "lon", split_axis=1, concat_axis=2, tiled=True)


def solution(mesh):
    return jax.shard_map(
        per_device,
        mesh=mesh,
        in_specs=(
            P("lat", "lon", None, None),
            P("lat", "lon", None),
            P("lat", "lon"),
            P("lat", "lon"),
            P(),
            P(),
            P(),
            P(),
            P("lon", "lat", None),
            P("lon", "lat", None),
        ),
        out_specs=P("lat", "lon", None, None),
        check_vma=False,
    )
```

```python
import functools
import jax
import jax.numpy as jnp
from jax import lax
from jax.experimental import pallas as pl
from jax.experimental.pallas import tpu as pltpu
from jax.sharding import PartitionSpec as P

ADV_STEPS = 2
FAST_LEAST = 1e-12
FAST_MOST = 1e8
HIGHEST = lax.Precision.HIGHEST
MOST_SUBSTEPS = 36
FLOOR = 1e-20
FLOOR_LOG = -66.43856


def with_halo(block, sides, width):
    for axis, dim in sides:
        count = lax.axis_size(axis)
        forward = [(i, i + 1) for i in range(count - 1)]
        backward = [(target, source) for source, target in forward]
        low = lax.ppermute(
            lax.slice_in_dim(block, block.shape[dim] - width, None, axis=dim), axis, forward
        )
        high = lax.ppermute(lax.slice_in_dim(block, 0, width, axis=dim), axis, backward)
        block = jnp.concatenate([low, block, high], axis=dim)
    return block


def slice_axis(array, start, count, along):
    return lax.slice_in_dim(array, start, start + count, axis=along)


def flux_sweep(padded, courant_pad, along, length):
    far_left = slice_axis(padded, 0, length + 3, along)
    near_left = slice_axis(padded, 1, length + 3, along)
    near_right = slice_axis(padded, 2, length + 3, along)
    far_right = slice_axis(padded, 3, length + 3, along)
    edges = 7.0 / 12.0 * (near_left + near_right) - 1.0 / 12.0 * (far_left + far_right)
    edges = jnp.minimum(
        jnp.maximum(edges, jnp.minimum(near_left, near_right)), jnp.maximum(near_left, near_right)
    )
    cell_means = slice_axis(padded, 2, length + 2, along)
    left_edge = slice_axis(edges, 0, length + 2, along)
    right_edge = slice_axis(edges, 1, length + 2, along)
    edge_jump = right_edge - left_edge
    curvature = 6.0 * cell_means - 3.0 * (left_edge + right_edge)
    courant = slice_axis(courant_pad, 3, length + 1, along)
    magnitude = jnp.abs(courant)
    from_left = slice_axis(right_edge, 0, length + 1, along) - 0.5 * courant * (
        slice_axis(edge_jump, 0, length + 1, along)
        - (1.0 - 2.0 / 3.0 * courant) * slice_axis(curvature, 0, length + 1, along)
    )
    from_right = slice_axis(left_edge, 1, length + 1, along) + 0.5 * magnitude * (
        slice_axis(edge_jump, 1, length + 1, along)
        + (1.0 - 2.0 / 3.0 * magnitude) * slice_axis(curvature, 1, length + 1, along)
    )
    face_flux = courant * jnp.where(courant >= 0.0, from_left, from_right)
    interior = slice_axis(padded, 3, length, along)
    return interior - (
        slice_axis(face_flux, 1, length, along) - slice_axis(face_flux, 0, length, along)
    )


def wrap_pad(array, along):
    extent = array.shape[along]
    return jnp.concatenate(
        [slice_axis(array, extent - 3, 3, along), array, slice_axis(array, 0, 3, along)], axis=along
    )


def two_halves(values):
    high = values.astype(jnp.bfloat16)
    low = (values - high.astype(jnp.float32)).astype(jnp.bfloat16)
    return jnp.concatenate([high, low], axis=1)


def dot32(left, right, dims=((1,), (0,)), precision=None):
    return lax.dot_general(
        left, right, (dims, ((), ())), precision=precision, preferred_element_type=jnp.float32
    )


def chem_kernel(*refs):
    sources, (out, rates, pick, spread, state, least, most, warmth) = refs[:8], refs[8:16]
    amounts, anomaly, solar, counts, speed, response, photo, recipe = held = refs[16:24]
    copies = [
        pltpu.make_async_copy(source, here, refs[24].at[index])
        for index, (source, here) in enumerate(zip(sources, held))
    ]
    for copy in copies:
        copy.start()
    for copy in copies:
        copy.wait()
    rows, columns, levels = anomaly.shape
    cells, species = state.shape
    width = rows * columns
    chunks = rates.shape[0]
    for row in range(rows):
        warmth[row * columns : (row + 1) * columns, :] = anomaly[row]
    place = lax.broadcasted_iota(jnp.int32, (width, species), 0)
    sunlight = jnp.zeros((width, species), jnp.float32)
    count = jnp.zeros((width, species), jnp.int32)
    longest = jnp.int32(0)
    for column in range(width):
        here = place == column
        spot = (column // columns, column % columns)
        sunlight = jnp.where(here, solar[spot], sunlight)
        count = jnp.where(here, counts[spot], count)
        longest = jnp.maximum(longest, counts[spot])
    ids = lax.broadcasted_iota(jnp.int32, (species, species), 0)
    for chunk in range(chunks):
        part = pl.ds(chunk * species, species)
        hits = [
            (recipe[row : row + 1, part] == ids).astype(jnp.float32) for row in range(4)
        ]
        taking = jnp.concatenate([hits[0], hits[1]], axis=1).astype(jnp.bfloat16)
        pick[chunk] = jnp.concatenate([taking, taking], axis=0)
        giving = jnp.concatenate(
            [jnp.transpose(hits[2] + hits[3]), jnp.transpose(hits[0] + hits[1])], axis=1
        ).astype(jnp.bfloat16)
        spread[chunk] = jnp.concatenate([giving, giving], axis=0)
    for level in range(levels):
        block = pl.ds(level * width, width)
        heat = jnp.broadcast_to(warmth[:, level : level + 1], (width, species))
        for chunk in range(chunks):
            part = pl.ds(chunk * species, species)
            rates[chunk, block, :] = (
                speed[:, part] * jnp.exp(response[:, part] * heat) + photo[:, part] * sunlight
            )

    def start():
        for level in range(levels):
            state[pl.ds(level * width, width), :] = amounts[pl.ds(level, width, stride=levels), :]

    def tiled(values):
        return jnp.concatenate([values] * levels, axis=0)

    start()
    substep = 1.0 / count.astype(jnp.float32)
    least[...] = state[...]
    most[...] = state[...]

    def advance(step, carry):
        current = state[...]
        least[...] = jnp.minimum(least[...], current)
        most[...] = jnp.maximum(most[...], current)
        pair = two_halves(current)
        flows = []
        for chunk in range(chunks):
            taken = dot32(pair, pick[chunk])
            flows.append(two_halves(rates[chunk] * taken[:, :species] * taken[:, species:]))
        total = dot32(jnp.concatenate(flows, axis=1), spread[...].reshape(-1, 2 * species))
        produced = total[:, :species]
        consumed = total[:, species:]
        size = tiled(substep)
        updated = (current + size * produced) / (current + size * consumed) * current
        state[...] = jnp.where(tiled(count) > step, updated, current)
        return carry

    lax.fori_loop(0, longest, advance, 0)
    usual = (jnp.min(least[...]) >= FAST_LEAST) & (jnp.max(most[...]) <= FAST_MOST)

    @pl.when(jnp.logical_not(usual))
    def _():
        start()

        def advance_fully(step, carry):
            current = state[...]
            produced = jnp.zeros((cells, species), jnp.float32)
            lost = jnp.zeros((cells, species), jnp.float32)
            for chunk in range(chunks):
                first_hit = pick[chunk, :species, :species].astype(jnp.float32)
                second_hit = pick[chunk, :species, species:].astype(jnp.float32)
                making = spread[chunk, :species, :species].astype(jnp.float32)
                first = dot32(current, first_hit, precision=HIGHEST)
                second = dot32(current, second_hit, precision=HIGHEST)
                rate = rates[chunk]
                produced += dot32(rate * first * second, making, precision=HIGHEST)
                lost += dot32(rate * second, first_hit, ((1,), (1,)), HIGHEST)
                lost += dot32(rate * first, second_hit, ((1,), (1,)), HIGHEST)
            size = tiled(substep)
            updated = (current + size * produced) / (1.0 + size * lost)
            state[...] = jnp.where(tiled(count) > step, updated, current)
            return carry

        lax.fori_loop(0, longest, advance_fully, 0)

    for level in range(levels):
        out[pl.ds(level, width, stride=levels), :] = state[pl.ds(level * width, width), :]


def react(operands):
    cells, species = operands[0].shape
    rows, columns, levels = operands[1].shape
    chunks = operands[7].shape[1] // species
    in_vmem = pl.BlockSpec(memory_space=pltpu.VMEM)
    held = [
        (pltpu.SMEM if index in (2, 3) else pltpu.VMEM)(operand.shape, operand.dtype)
        for index, operand in enumerate(operands)
    ]
    table = pltpu.VMEM((chunks, 2 * species, 2 * species), jnp.bfloat16)
    field = pltpu.VMEM((cells, species), jnp.float32)
    return pl.pallas_call(
        chem_kernel,
        out_shape=jax.ShapeDtypeStruct((cells, species), jnp.float32),
        in_specs=[pl.BlockSpec(memory_space=pltpu.HBM)] * len(operands),
        out_specs=in_vmem,
        scratch_shapes=[
            pltpu.VMEM((chunks, cells, species), jnp.float32), table, table,
            field, field, field, pltpu.VMEM((rows * columns, levels), jnp.float32),
            *held, pltpu.SemaphoreType.DMA((len(operands),)),
        ],
        compiler_params=pltpu.CompilerParams(vmem_limit_bytes=67043328),
    )(*operands)


def others(bands, devices, order):
    pairs = [(dy, dl) for dl in order for dy in reversed(range(bands))]
    return [pair for pair in pairs if pair != (0, 0)]


def peer(bands, devices, dy, dl):
    band, block = lax.axis_index("lat"), lax.axis_index("lon")
    return (lax.rem(band + dy, bands), lax.rem(block + dl, devices))


def signal_peers(bands, devices):
    barrier = pltpu.get_barrier_semaphore()
    for dy, dl in others(bands, devices, range(devices)):
        pl.semaphore_signal(
            barrier, inc=1, device_id=peer(bands, devices, dy, dl),
            device_id_type=pl.DeviceIdType.MESH,
        )


def wrap_rows(buffer, slot, values, half):
    extent = values.shape[0]
    buffer[slot, 8 : 8 + extent, :] = values
    buffer[slot, 0:8, :] = pltpu.roll(values[extent - 8 :], half, 1)
    buffer[slot, 8 + extent : 16 + extent, :] = pltpu.roll(values[:8], half, 1)


def clipped_edge(far_left, near_left, near_right, far_right):
    edge = 7.0 / 12.0 * (near_left + near_right) - 1.0 / 12.0 * (far_left + far_right)
    return jnp.minimum(
        jnp.maximum(edge, jnp.minimum(near_left, near_right)), jnp.maximum(near_left, near_right)
    )


def face_weights(courant):
    magnitude = jnp.abs(courant)
    slope = 1.0 - 2.0 / 3.0 * magnitude
    half = 0.5 * magnitude * courant
    return courant - half * (1.0 + 3.0 * slope), half * (1.0 - 3.0 * slope), 6.0 * slope * half


def face_flow(weights, before, edge, after, left_mean, right_mean):
    on_edge, on_other, on_mean = weights
    rightward = on_mean >= 0.0
    other = jnp.where(rightward, before, after)
    mean = jnp.where(rightward, left_mean, right_mean)
    return on_edge * edge + on_other * other + on_mean * mean


def move_kernel(
    bands, devices, packed, east, north, out,
    inbox, outbox, back, wind_out, wind_in, courants, grid, edges,
    send_there, recv_there, send_wind, recv_wind, send_back, recv_back,
):
    band, block = lax.axis_index("lat"), lax.axis_index("lon")
    _, rows, longitudes = east.shape
    species = packed.shape[2]
    levels = packed.shape[0] // bands
    half = species // 2
    columns = longitudes // devices
    extent = longitudes // 2
    lats = bands * rows
    low_rows = rows // 2
    first = 3 * devices // 4
    falling = [step % devices for step in range(first + devices, first, -1)]
    offsets = others(bands, devices, range(devices))

    def remote(source, target, send_sem, recv_sem, device):
        return pltpu.make_async_remote_copy(
            src_ref=source, dst_ref=target, send_sem=send_sem, recv_sem=recv_sem,
            device_id=device, device_id_type=pl.DeviceIdType.MESH,
        )

    wind_out[...] = jnp.zeros_like(wind_out)
    wind_out[0:rows, 0:longitudes] = east[0]
    wind_out[rows : 2 * rows, 0:longitudes] = north[0]
    wind_in[band] = wind_out[...]
    inbox[band * devices + block] = packed[block * bands + band]
    pl.semaphore_wait(pltpu.get_barrier_semaphore(), len(offsets))

    winds = []
    for dy in range(1, bands):
        copy = remote(
            wind_out, wind_in.at[band], send_wind.at[dy], recv_wind.at[dy],
            peer(bands, devices, dy, 0),
        )
        copy.start()
        winds.append(copy)
    def wait_for_all(box, semaphore):
        most = box.at[pl.ds(0, len(offsets))]
        pltpu.make_async_copy(most, most, semaphore.at[0]).wait()

    for dy, dl in others(bands, devices, falling):
        device = peer(bands, devices, dy, dl)
        remote(
            packed.at[device[1] * bands + device[0]], inbox.at[band * devices + block],
            send_there.at[0], recv_there.at[0], device,
        ).start()

    for copy in winds:
        copy.wait()
    near_tall = lax.broadcasted_iota(jnp.int32, (extent, species), 1) < half
    wide = wind_out.shape[1]
    tall = [wind_in[y] for y in range(bands)]
    tall.append(jnp.zeros((wide - bands * 2 * rows, wide), jnp.float32))
    weights = face_weights(jnp.transpose(jnp.concatenate(tall, axis=0))[0 : 2 * extent])
    for lat in range(lats):
        for kind in range(2):
            lane = lat // rows * 2 * rows + kind * rows + lat % rows
            columns_of = [weight[:, lane : lane + 1] for weight in weights]
            for index, column in enumerate(columns_of):
                courants[kind, lat, index] = jnp.where(
                    near_tall,
                    jnp.broadcast_to(column[0:extent], (extent, species)),
                    jnp.broadcast_to(column[extent : 2 * extent], (extent, species)),
                )
    wait_for_all(packed, send_there)
    wait_for_all(inbox, recv_there)

    near = lax.broadcasted_iota(jnp.int32, (low_rows * columns, species), 1) < half

    def swap_pair(first, second):
        return (
            jnp.where(near, first, pltpu.roll(second, half, 1)),
            jnp.where(near, pltpu.roll(first, half, 1), second),
        )

    for y in range(bands):
        for spot in range(devices // 2):
            pair = swap_pair(
                inbox[y * devices + spot], inbox[y * devices + spot + devices // 2]
            )
            for high in range(2):
                for low in range(low_rows):
                    lat = y * rows + high * low_rows + low
                    grid[lat, 8 + spot * columns : 8 + (spot + 1) * columns, :] = pair[high][
                        low * columns : (low + 1) * columns
                    ]
    planes = [grid[lat, 8 : 8 + extent, :] for lat in range(lats)]
    empty = jnp.zeros((extent, species), jnp.float32)
    for sweep_index in range(ADV_STEPS):
        swept = []
        for lat in range(lats):
            mean = planes[lat]
            wrap_rows(grid, lat, mean, half)

            def shifted(buffer, shift):
                return buffer[lat, 8 + shift : 8 + shift + extent, :]

            left_mean = shifted(grid, -1)
            edge = clipped_edge(shifted(grid, -2), left_mean, mean, shifted(grid, 1))
            wrap_rows(edges, lat, edge, half)
            flow = face_flow(
                [courants[0, lat, index] for index in range(3)], shifted(edges, -1), edge, shifted(edges, 1), left_mean, mean
            )
            wrap_rows(grid, lat, flow, half)
            swept.append(mean - (shifted(grid, 1) - flow))
        padded = [empty, empty] + swept + [empty, empty]
        rims = [clipped_edge(*padded[lat : lat + 4]) for lat in range(lats + 1)]
        flows = [
            face_flow(
                [courants[1, lat, index] for index in range(3)], rims[lat - 1], rims[lat], rims[lat + 1],
                swept[lat - 1], swept[lat],
            )
            for lat in range(1, lats)
        ]
        flows = [empty] + flows + [empty]
        planes = [swept[lat] - (flows[lat + 1] - flows[lat]) for lat in range(lats)]
    for lat in range(lats):
        grid[lat, 8 : 8 + extent, :] = planes[lat]
    for y in range(bands):
        for spot in range(devices // 2):
            sides = [
                jnp.concatenate(
                    [
                        grid[
                            y * rows + high * low_rows + low,
                            8 + spot * columns : 8 + (spot + 1) * columns,
                            :,
                        ]
                        for low in range(low_rows)
                    ],
                    axis=0,
                )
                for high in range(2)
            ]
            place = y * devices + spot
            outbox[place], outbox[place + devices // 2] = swap_pair(*sides)
    back[block * bands + band] = outbox[band * devices + block]
    for dy, dl in offsets:
        device = peer(bands, devices, dy, dl)
        remote(
            outbox.at[device[0] * devices + device[1]], back.at[block * bands + band],
            send_back.at[0], recv_back.at[0], device,
        ).start()
    wait_for_all(outbox, send_back)
    wait_for_all(back, recv_back)
    count = low_rows * columns
    for level in range(levels):
        front, behind = swap_pair(back[level * bands], back[level * bands + 1])
        out[pl.ds(level, count, stride=levels), :] = front
        out[pl.ds(count * levels + level, count, stride=levels), :] = behind


def halves(values):
    high = values.astype(jnp.bfloat16)
    return high, (values - high.astype(jnp.float32)).astype(jnp.bfloat16)


def substeps(groups, state, number, log_rates, pick, spread, *results):
    sides = range(2)
    gathered = [results[side * groups : (side + 1) * groups] for side in sides]
    scattered = [results[(2 + side) * groups : (3 + side) * groups] for side in sides]
    tall = state.shape[0] // groups
    species = state.shape[1]

    def load_pick():
        for side in sides:
            pltpu.matmul_push_rhs(pick[side], 0, side)

    def load_spread():
        for side in sides:
            pltpu.matmul_push_rhs(spread[side], 1, side)

    def gather(group, logs):
        pair = jnp.concatenate(halves(jnp.maximum(logs, FLOOR_LOG)), axis=1)
        for side in sides:
            pltpu.matmul_acc_lhs(
                gathered[side][group], pair, load_staged_rhs=None if group else 0
            )

    load_pick()
    for group in range(groups):
        gather(group, jnp.log2(state[group * tall : (group + 1) * tall, :]))
    load_spread()

    def advance(step, carry):
        for group in range(groups):
            block = slice(group * tall, (group + 1) * tall)
            for side in sides:
                logs = pltpu.matmul_pop(gathered[side][group]) + log_rates[side, block, :]
                high, low = halves(jnp.exp2(logs))
                pltpu.matmul_acc_lhs(
                    scattered[side][group], high, load_staged_rhs=None if group else 1
                )
                pltpu.matmul_acc_lhs(scattered[side][group], low)
            if group == 0:
                load_spread()
        load_pick()
        for group in range(groups):
            block = slice(group * tall, (group + 1) * tall)
            total = pltpu.matmul_pop(scattered[0][group]) + pltpu.matmul_pop(scattered[1][group])
            current, count = state[block, :], number[block, :]
            above = count * current + total[:, :species]
            below = count + total[:, species:] * (1.0 / jnp.maximum(current, FLOOR))
            gather(group, jnp.log2(above) - jnp.log2(below))
            state[block, :] = jnp.where(count > step.astype(jnp.float32), above / below, current)
        return carry

    lax.fori_loop(0, MOST_SUBSTEPS, advance, 0)
    for side in sides:
        for group in range(groups):
            pltpu.matmul_pop(gathered[side][group])
        pltpu.matmul_acc_lhs(
            scattered[side][0], jnp.zeros((tall, 2 * species), jnp.bfloat16), load_staged_rhs=1
        )
        pltpu.matmul_pop(scattered[side][0])


def whole_kernel(bands, devices, *refs):
    sources, out = refs[:10], refs[10]
    amounts, anomaly, solar, counts, speed, response, photo, recipe, east, north = held = refs[11:21]
    log_rates, pick, spread, state, number, warmth, arrived, packed = refs[21:29]
    move_refs = refs[29:]
    width = warmth.shape[0]
    cells, species = state.shape
    levels = cells // width

    copies = [
        pltpu.make_async_copy(source, here, arrived.at[index])
        for index, (source, here) in enumerate(zip(sources, held))
    ]
    for copy in copies[7:] + copies[:7]:
        copy.start()
    signal_peers(bands, devices)
    copies[7].wait()
    ids = lax.broadcasted_iota(jnp.int32, (species, species), 0)
    for chunk in range(4):
        part = pl.ds(chunk * species, species)
        hits = [(recipe[row : row + 1, part] == ids).astype(jnp.float32) for row in range(4)]
        taking, giving = hits[0] + hits[1], hits[2] + hits[3]
        side, spot = chunk // 2, chunk % 2 * species
        for copy in range(2):
            pick[side, copy * species : (copy + 1) * species, spot : spot + species] = (
                taking.astype(jnp.bfloat16)
            )
        spread[side, spot : spot + species, :] = jnp.concatenate(
            [jnp.transpose(giving), jnp.transpose(taking)], axis=1
        ).astype(jnp.bfloat16)
    for copy in copies[1:7] + copies[8:]:
        copy.wait()
    rows, columns, _ = anomaly.shape
    for row in range(rows):
        warmth[row * columns : (row + 1) * columns, :] = anomaly[row]
    place = lax.broadcasted_iota(jnp.int32, (width, species), 0)
    sunlight = jnp.zeros((width, species), jnp.float32)
    count = jnp.zeros((width, species), jnp.int32)
    for column in range(width):
        here = place == column
        spot = (column // columns, column % columns)
        sunlight = jnp.where(here, solar[spot], sunlight)
        count = jnp.where(here, counts[spot], count)
    count = count.astype(jnp.float32)
    for level in range(levels):
        block = pl.ds(level * width, width)
        heat = jnp.broadcast_to(warmth[:, level : level + 1], (width, species))
        for chunk in range(4):
            part = pl.ds(chunk * species, species)
            log_rates[chunk // 2, block, chunk % 2 * species : (chunk % 2 + 1) * species] = jnp.log2(
                speed[:, part] * jnp.exp(response[:, part] * heat) + photo[:, part] * sunlight
            )
        number[block, :] = count
    copies[0].wait()
    for level in range(levels):
        state[pl.ds(level * width, width), :] = amounts[pl.ds(level, width, stride=levels), :]

    groups = cells // 32
    pl.run_scoped(
        functools.partial(substeps, groups, state, number, log_rates, pick, spread),
        *[
            pltpu.ACC(side)((32, 2 * species), jnp.float32)
            for use in range(2)
            for side in range(2)
            for group in range(groups)
        ],
    )

    half = species // 2
    near = lax.broadcasted_iota(jnp.int32, (width // 2, species), 1) < half
    for level in range(levels):
        front = state[pl.ds(level * width, width // 2), :]
        behind = state[pl.ds(level * width + width // 2, width // 2), :]
        packed[2 * level] = jnp.where(near, front, pltpu.roll(behind, half, 1))
        packed[2 * level + 1] = jnp.where(near, pltpu.roll(front, half, 1), behind)
    move_kernel(bands, devices, packed, east, north, out, *move_refs)


def react_and_advect(operands):
    bands, devices = lax.axis_size("lat"), lax.axis_size("lon")
    cells, species = operands[0].shape
    rows, columns, levels = operands[1].shape
    longitudes = operands[8].shape[2]
    lats, extent, count = bands * rows, longitudes // 2, rows * columns // 2
    wide = -(-longitudes // 128) * 128
    held = [
        (pltpu.SMEM if index in (2, 3) else pltpu.VMEM)(operand.shape, operand.dtype)
        for index, operand in enumerate(operands)
    ]
    semaphores = pltpu.SemaphoreType.DMA((1,))
    wind_semaphores = pltpu.SemaphoreType.DMA((bands,))
    box = pltpu.VMEM((bands * devices, count, species), jnp.float32)
    exchanged = pltpu.VMEM((levels * bands, count, species), jnp.float32)
    wrapped = pltpu.VMEM((lats, extent + 16, species), jnp.float32)
    table = pltpu.VMEM((2, 2 * species, 2 * species), jnp.bfloat16)
    field = pltpu.VMEM((cells, species), jnp.float32)
    return pl.pallas_call(
        functools.partial(whole_kernel, bands, devices),
        out_shape=jax.ShapeDtypeStruct((cells, species), jnp.float32),
        in_specs=[pl.BlockSpec(memory_space=pltpu.HBM)] * len(operands),
        out_specs=pl.BlockSpec(memory_space=pltpu.VMEM),
        scratch_shapes=[
            *held,
            pltpu.VMEM((2, cells, 2 * species), jnp.float32), table, table, field, field,
            pltpu.VMEM((rows * columns, levels), jnp.float32),
            pltpu.SemaphoreType.DMA((len(operands),)), exchanged,
            box, box, exchanged,
            pltpu.VMEM((2 * rows, wide), jnp.float32),
            pltpu.VMEM((bands, 2 * rows, wide), jnp.float32),
            pltpu.VMEM((2, lats, 3, extent, species), jnp.float32), wrapped, wrapped,
            semaphores, semaphores, wind_semaphores, wind_semaphores, semaphores, semaphores,
        ],
        compiler_params=pltpu.CompilerParams(
            collective_id=0, has_side_effects=True, vmem_limit_bytes=32 << 20,
        ),
    )(*[pltpu.with_memory_space_constraint(operand, pltpu.HBM) for operand in operands])


def per_device(
    species_amounts,
    thermal_anomaly,
    solar_flux_factor,
    inner_iterations,
    reference_speed,
    thermal_response,
    photo_breakup,
    reaction_recipe,
    eastward_wind_ratio,
    northward_wind_ratio,
):
    rows, columns, levels, species = species_amounts.shape
    devices = lax.axis_size("lon")
    longitudes = eastward_wind_ratio.shape[2]
    reactions = reaction_recipe.shape[1]
    operands = (
        species_amounts.reshape(-1, species), thermal_anomaly, solar_flux_factor,
        inner_iterations, reference_speed.reshape(1, -1), thermal_response.reshape(1, -1),
        photo_breakup.reshape(1, -1), reaction_recipe,
    )
    paired = lax.axis_size("lat") == 2 and levels == devices and rows % 2 == 0
    tabled = species == 128 and reactions == 4 * species and rows * columns % 16 == 0
    if paired and tabled and devices % 2 == 0 and longitudes <= 128:
        moved = react_and_advect((*operands, eastward_wind_ratio, northward_wind_ratio))
        return moved.reshape(species_amounts.shape)
    settled_columns = react(operands).reshape(species_amounts.shape)
    lat_rows = species_amounts.shape[0]
    row_ids = lax.axis_index("lat") * lat_rows + lax.broadcasted_iota(
        jnp.int32, (lat_rows, 1, 1, 1), 0
    )
    carried_quantity = lax.all_to_all(
        settled_columns, "lon", split_axis=2, concat_axis=1, tiled=True
    )
    east_faces = jnp.transpose(eastward_wind_ratio, (1, 2, 0))[..., None]
    south_faces = jnp.where(
        row_ids > 0, jnp.transpose(northward_wind_ratio, (1, 2, 0))[..., None], 0.0
    )
    east_pad = wrap_pad(east_faces, 1)
    for sweep_index in range(ADV_STEPS):
        carried_quantity = flux_sweep(
            wrap_pad(carried_quantity, 1), east_pad, 1, carried_quantity.shape[1]
        )
        rimmed, south_pad = (
            with_halo(carried_quantity, (("lat", 0),), 3),
            with_halo(south_faces, (("lat", 0),), 3),
        )
        carried_quantity = flux_sweep(rimmed, south_pad, 0, lat_rows)
    return lax.all_to_all(carried_quantity, "lon", split_axis=1, concat_axis=2, tiled=True)


def solution(mesh):
    return jax.shard_map(
        per_device,
        mesh=mesh,
        in_specs=(
            P("lat", "lon", None, None),
            P("lat", "lon", None),
            P("lat", "lon"),
            P("lat", "lon"),
            P(),
            P(),
            P(),
            P(),
            P("lon", "lat", None),
            P("lon", "lat", None),
        ),
        out_specs=P("lat", "lon", None, None),
        check_vma=False,
    )
```

```python
import functools
import jax
import jax.numpy as jnp
from jax import lax
from jax.experimental import pallas as pl
from jax.experimental.pallas import tpu as pltpu
from jax.sharding import PartitionSpec as P

ADV_STEPS = 2
FAST_LEAST = 1e-12
FAST_MOST = 1e8
HIGHEST = lax.Precision.HIGHEST
MOST_SUBSTEPS = 36
FLOOR = 1e-20
FLOOR_LOG = -66.43856


def with_halo(block, sides, width):
    for axis, dim in sides:
        count = lax.axis_size(axis)
        forward = [(i, i + 1) for i in range(count - 1)]
        backward = [(target, source) for source, target in forward]
        low = lax.ppermute(
            lax.slice_in_dim(block, block.shape[dim] - width, None, axis=dim), axis, forward
        )
        high = lax.ppermute(lax.slice_in_dim(block, 0, width, axis=dim), axis, backward)
        block = jnp.concatenate([low, block, high], axis=dim)
    return block


def slice_axis(array, start, count, along):
    return lax.slice_in_dim(array, start, start + count, axis=along)


def flux_sweep(padded, courant_pad, along, length):
    far_left = slice_axis(padded, 0, length + 3, along)
    near_left = slice_axis(padded, 1, length + 3, along)
    near_right = slice_axis(padded, 2, length + 3, along)
    far_right = slice_axis(padded, 3, length + 3, along)
    edges = 7.0 / 12.0 * (near_left + near_right) - 1.0 / 12.0 * (far_left + far_right)
    edges = jnp.minimum(
        jnp.maximum(edges, jnp.minimum(near_left, near_right)), jnp.maximum(near_left, near_right)
    )
    cell_means = slice_axis(padded, 2, length + 2, along)
    left_edge = slice_axis(edges, 0, length + 2, along)
    right_edge = slice_axis(edges, 1, length + 2, along)
    edge_jump = right_edge - left_edge
    curvature = 6.0 * cell_means - 3.0 * (left_edge + right_edge)
    courant = slice_axis(courant_pad, 3, length + 1, along)
    magnitude = jnp.abs(courant)
    from_left = slice_axis(right_edge, 0, length + 1, along) - 0.5 * courant * (
        slice_axis(edge_jump, 0, length + 1, along)
        - (1.0 - 2.0 / 3.0 * courant) * slice_axis(curvature, 0, length + 1, along)
    )
    from_right = slice_axis(left_edge, 1, length + 1, along) + 0.5 * magnitude * (
        slice_axis(edge_jump, 1, length + 1, along)
        + (1.0 - 2.0 / 3.0 * magnitude) * slice_axis(curvature, 1, length + 1, along)
    )
    face_flux = courant * jnp.where(courant >= 0.0, from_left, from_right)
    interior = slice_axis(padded, 3, length, along)
    return interior - (
        slice_axis(face_flux, 1, length, along) - slice_axis(face_flux, 0, length, along)
    )


def wrap_pad(array, along):
    extent = array.shape[along]
    return jnp.concatenate(
        [slice_axis(array, extent - 3, 3, along), array, slice_axis(array, 0, 3, along)], axis=along
    )


def two_halves(values):
    high = values.astype(jnp.bfloat16)
    low = (values - high.astype(jnp.float32)).astype(jnp.bfloat16)
    return jnp.concatenate([high, low], axis=1)


def dot32(left, right, dims=((1,), (0,)), precision=None):
    return lax.dot_general(
        left, right, (dims, ((), ())), precision=precision, preferred_element_type=jnp.float32
    )


def chem_kernel(*refs):
    sources, (out, rates, pick, spread, state, least, most, warmth) = refs[:8], refs[8:16]
    amounts, anomaly, solar, counts, speed, response, photo, recipe = held = refs[16:24]
    copies = [
        pltpu.make_async_copy(source, here, refs[24].at[index])
        for index, (source, here) in enumerate(zip(sources, held))
    ]
    for copy in copies:
        copy.start()
    for copy in copies:
        copy.wait()
    rows, columns, levels = anomaly.shape
    cells, species = state.shape
    width = rows * columns
    chunks = rates.shape[0]
    for row in range(rows):
        warmth[row * columns : (row + 1) * columns, :] = anomaly[row]
    place = lax.broadcasted_iota(jnp.int32, (width, species), 0)
    sunlight = jnp.zeros((width, species), jnp.float32)
    count = jnp.zeros((width, species), jnp.int32)
    longest = jnp.int32(0)
    for column in range(width):
        here = place == column
        spot = (column // columns, column % columns)
        sunlight = jnp.where(here, solar[spot], sunlight)
        count = jnp.where(here, counts[spot], count)
        longest = jnp.maximum(longest, counts[spot])
    ids = lax.broadcasted_iota(jnp.int32, (species, species), 0)
    for chunk in range(chunks):
        part = pl.ds(chunk * species, species)
        hits = [
            (recipe[row : row + 1, part] == ids).astype(jnp.float32) for row in range(4)
        ]
        taking = jnp.concatenate([hits[0], hits[1]], axis=1).astype(jnp.bfloat16)
        pick[chunk] = jnp.concatenate([taking, taking], axis=0)
        giving = jnp.concatenate(
            [jnp.transpose(hits[2] + hits[3]), jnp.transpose(hits[0] + hits[1])], axis=1
        ).astype(jnp.bfloat16)
        spread[chunk] = jnp.concatenate([giving, giving], axis=0)
    for level in range(levels):
        block = pl.ds(level * width, width)
        heat = jnp.broadcast_to(warmth[:, level : level + 1], (width, species))
        for chunk in range(chunks):
            part = pl.ds(chunk * species, species)
            rates[chunk, block, :] = (
                speed[:, part] * jnp.exp(response[:, part] * heat) + photo[:, part] * sunlight
            )

    def start():
        for level in range(levels):
            state[pl.ds(level * width, width), :] = amounts[pl.ds(level, width, stride=levels), :]

    def tiled(values):
        return jnp.concatenate([values] * levels, axis=0)

    start()
    substep = 1.0 / count.astype(jnp.float32)
    least[...] = state[...]
    most[...] = state[...]

    def advance(step, carry):
        current = state[...]
        least[...] = jnp.minimum(least[...], current)
        most[...] = jnp.maximum(most[...], current)
        pair = two_halves(current)
        flows = []
        for chunk in range(chunks):
            taken = dot32(pair, pick[chunk])
            flows.append(two_halves(rates[chunk] * taken[:, :species] * taken[:, species:]))
        total = dot32(jnp.concatenate(flows, axis=1), spread[...].reshape(-1, 2 * species))
        produced = total[:, :species]
        consumed = total[:, species:]
        size = tiled(substep)
        updated = (current + size * produced) / (current + size * consumed) * current
        state[...] = jnp.where(tiled(count) > step, updated, current)
        return carry

    lax.fori_loop(0, longest, advance, 0)
    usual = (jnp.min(least[...]) >= FAST_LEAST) & (jnp.max(most[...]) <= FAST_MOST)

    @pl.when(jnp.logical_not(usual))
    def _():
        start()

        def advance_fully(step, carry):
            current = state[...]
            produced = jnp.zeros((cells, species), jnp.float32)
            lost = jnp.zeros((cells, species), jnp.float32)
            for chunk in range(chunks):
                first_hit = pick[chunk, :species, :species].astype(jnp.float32)
                second_hit = pick[chunk, :species, species:].astype(jnp.float32)
                making = spread[chunk, :species, :species].astype(jnp.float32)
                first = dot32(current, first_hit, precision=HIGHEST)
                second = dot32(current, second_hit, precision=HIGHEST)
                rate = rates[chunk]
                produced += dot32(rate * first * second, making, precision=HIGHEST)
                lost += dot32(rate * second, first_hit, ((1,), (1,)), HIGHEST)
                lost += dot32(rate * first, second_hit, ((1,), (1,)), HIGHEST)
            size = tiled(substep)
            updated = (current + size * produced) / (1.0 + size * lost)
            state[...] = jnp.where(tiled(count) > step, updated, current)
            return carry

        lax.fori_loop(0, longest, advance_fully, 0)

    for level in range(levels):
        out[pl.ds(level, width, stride=levels), :] = state[pl.ds(level * width, width), :]


def react(operands):
    cells, species = operands[0].shape
    rows, columns, levels = operands[1].shape
    chunks = operands[7].shape[1] // species
    in_vmem = pl.BlockSpec(memory_space=pltpu.VMEM)
    held = [
        (pltpu.SMEM if index in (2, 3) else pltpu.VMEM)(operand.shape, operand.dtype)
        for index, operand in enumerate(operands)
    ]
    table = pltpu.VMEM((chunks, 2 * species, 2 * species), jnp.bfloat16)
    field = pltpu.VMEM((cells, species), jnp.float32)
    return pl.pallas_call(
        chem_kernel,
        out_shape=jax.ShapeDtypeStruct((cells, species), jnp.float32),
        in_specs=[pl.BlockSpec(memory_space=pltpu.HBM)] * len(operands),
        out_specs=in_vmem,
        scratch_shapes=[
            pltpu.VMEM((chunks, cells, species), jnp.float32), table, table,
            field, field, field, pltpu.VMEM((rows * columns, levels), jnp.float32),
            *held, pltpu.SemaphoreType.DMA((len(operands),)),
        ],
        compiler_params=pltpu.CompilerParams(vmem_limit_bytes=67043328),
    )(*operands)


def others(bands, devices, order):
    pairs = [(dy, dl) for dl in order for dy in reversed(range(bands))]
    return [pair for pair in pairs if pair != (0, 0)]


def peer(bands, devices, dy, dl):
    band, block = lax.axis_index("lat"), lax.axis_index("lon")
    return (lax.rem(band + dy, bands), lax.rem(block + dl, devices))


def signal_peers(bands, devices):
    barrier = pltpu.get_barrier_semaphore()
    for dy, dl in others(bands, devices, range(devices)):
        pl.semaphore_signal(
            barrier, inc=1, device_id=peer(bands, devices, dy, dl),
            device_id_type=pl.DeviceIdType.MESH,
        )


def wrap_rows(buffer, slot, values, half):
    extent = values.shape[0]
    buffer[slot, 8 : 8 + extent, :] = values
    buffer[slot, 0:8, :] = pltpu.roll(values[extent - 8 :], half, 1)
    buffer[slot, 8 + extent : 16 + extent, :] = pltpu.roll(values[:8], half, 1)


def clipped_edge(far_left, near_left, near_right, far_right):
    edge = 7.0 / 12.0 * (near_left + near_right) - 1.0 / 12.0 * (far_left + far_right)
    return jnp.minimum(
        jnp.maximum(edge, jnp.minimum(near_left, near_right)), jnp.maximum(near_left, near_right)
    )


def face_weights(courant):
    magnitude = jnp.abs(courant)
    slope = 1.0 - 2.0 / 3.0 * magnitude
    half = 0.5 * magnitude * courant
    return courant - half * (1.0 + 3.0 * slope), half * (1.0 - 3.0 * slope), 6.0 * slope * half


def face_flow(weights, before, edge, after, left_mean, right_mean):
    on_edge, on_other, on_mean = weights
    rightward = on_mean >= 0.0
    other = jnp.where(rightward, before, after)
    mean = jnp.where(rightward, left_mean, right_mean)
    return on_edge * edge + on_other * other + on_mean * mean


def remote(source, target, send_sem, recv_sem, device):
    return pltpu.make_async_remote_copy(
        src_ref=source, dst_ref=target, send_sem=send_sem, recv_sem=recv_sem,
        device_id=device, device_id_type=pl.DeviceIdType.MESH,
    )


def wind_copies(bands, devices, wind_out, wind_in, send_wind, recv_wind):
    band = lax.axis_index("lat")
    return [
        remote(
            wind_out, wind_in.at[band], send_wind.at[dy], recv_wind.at[dy],
            peer(bands, devices, dy, 0),
        )
        for dy in range(1, bands)
    ]


def move_kernel(
    bands, devices, rows, longitudes, packed, out,
    inbox, outbox, back, wind_out, wind_in, courants, grid, edges,
    send_there, recv_there, send_wind, recv_wind, send_back, recv_back,
):
    band, block = lax.axis_index("lat"), lax.axis_index("lon")
    species = packed.shape[2]
    levels = packed.shape[0] // bands
    half = species // 2
    columns = longitudes // devices
    extent = longitudes // 2
    lats = bands * rows
    low_rows = rows // 2
    offsets = others(bands, devices, range(devices))

    def wait_for_all(box, semaphore):
        most = box.at[pl.ds(0, len(offsets))]
        pltpu.make_async_copy(most, most, semaphore.at[0]).wait()

    for copy in wind_copies(bands, devices, wind_out, wind_in, send_wind, recv_wind):
        copy.wait()
    near_tall = lax.broadcasted_iota(jnp.int32, (extent, species), 1) < half
    wide = wind_out.shape[1]
    tall = [wind_in[y] for y in range(bands)]
    tall.append(jnp.zeros((wide - bands * 2 * rows, wide), jnp.float32))
    weights = face_weights(jnp.transpose(jnp.concatenate(tall, axis=0))[0 : 2 * extent])
    for lat in range(lats):
        for kind in range(2):
            lane = lat // rows * 2 * rows + kind * rows + lat % rows
            columns_of = [weight[:, lane : lane + 1] for weight in weights]
            for index, column in enumerate(columns_of):
                courants[kind, lat, index] = jnp.where(
                    near_tall,
                    jnp.broadcast_to(column[0:extent], (extent, species)),
                    jnp.broadcast_to(column[extent : 2 * extent], (extent, species)),
                )
    wait_for_all(packed, send_there)
    wait_for_all(inbox, recv_there)

    near = lax.broadcasted_iota(jnp.int32, (low_rows * columns, species), 1) < half

    def swap_pair(first, second):
        return (
            jnp.where(near, first, pltpu.roll(second, half, 1)),
            jnp.where(near, pltpu.roll(first, half, 1), second),
        )

    for y in range(bands):
        for spot in range(devices // 2):
            pair = swap_pair(
                inbox[y * devices + spot], inbox[y * devices + spot + devices // 2]
            )
            for high in range(2):
                for low in range(low_rows):
                    lat = y * rows + high * low_rows + low
                    grid[lat, 8 + spot * columns : 8 + (spot + 1) * columns, :] = pair[high][
                        low * columns : (low + 1) * columns
                    ]
    planes = [grid[lat, 8 : 8 + extent, :] for lat in range(lats)]
    empty = jnp.zeros((extent, species), jnp.float32)
    for sweep_index in range(ADV_STEPS):
        swept = []
        for lat in range(lats):
            mean = planes[lat]
            wrap_rows(grid, lat, mean, half)

            def shifted(buffer, shift):
                return buffer[lat, 8 + shift : 8 + shift + extent, :]

            left_mean = shifted(grid, -1)
            edge = clipped_edge(shifted(grid, -2), left_mean, mean, shifted(grid, 1))
            wrap_rows(edges, lat, edge, half)
            flow = face_flow(
                [courants[0, lat, index] for index in range(3)], shifted(edges, -1), edge, shifted(edges, 1), left_mean, mean
            )
            wrap_rows(grid, lat, flow, half)
            swept.append(mean - (shifted(grid, 1) - flow))
        padded = [empty, empty] + swept + [empty, empty]
        rims = [clipped_edge(*padded[lat : lat + 4]) for lat in range(lats + 1)]
        flows = [
            face_flow(
                [courants[1, lat, index] for index in range(3)], rims[lat - 1], rims[lat], rims[lat + 1],
                swept[lat - 1], swept[lat],
            )
            for lat in range(1, lats)
        ]
        flows = [empty] + flows + [empty]
        planes = [swept[lat] - (flows[lat + 1] - flows[lat]) for lat in range(lats)]
    for lat in range(lats):
        grid[lat, 8 : 8 + extent, :] = planes[lat]
    for y in range(bands):
        for spot in range(devices // 2):
            sides = [
                jnp.concatenate(
                    [
                        grid[
                            y * rows + high * low_rows + low,
                            8 + spot * columns : 8 + (spot + 1) * columns,
                            :,
                        ]
                        for low in range(low_rows)
                    ],
                    axis=0,
                )
                for high in range(2)
            ]
            place = y * devices + spot
            outbox[place], outbox[place + devices // 2] = swap_pair(*sides)
    back[block * bands + band] = outbox[band * devices + block]
    for dy, dl in offsets:
        device = peer(bands, devices, dy, dl)
        remote(
            outbox.at[device[0] * devices + device[1]], back.at[block * bands + band],
            send_back.at[0], recv_back.at[0], device,
        ).start()
    wait_for_all(outbox, send_back)
    wait_for_all(back, recv_back)
    count = low_rows * columns
    for level in range(levels):
        front, behind = swap_pair(back[level * bands], back[level * bands + 1])
        out[pl.ds(level, count, stride=levels), :] = front
        out[pl.ds(count * levels + level, count, stride=levels), :] = behind


def halves(values):
    high = values.astype(jnp.bfloat16)
    return high, (values - high.astype(jnp.float32)).astype(jnp.bfloat16)


def substeps(groups, depart, state, number, log_rates, pick, spread, *results):
    sides = range(2)
    gathered = [results[side * groups : (side + 1) * groups] for side in sides]
    scattered = [results[(2 + side) * groups : (3 + side) * groups] for side in sides]
    tall = state.shape[0] // groups
    species = state.shape[1]

    def load_pick():
        for side in sides:
            pltpu.matmul_push_rhs(pick[side], 0, side)

    def load_spread():
        for side in sides:
            pltpu.matmul_push_rhs(spread[side], 1, side)

    def gather(group, logs):
        pair = jnp.concatenate(halves(jnp.maximum(logs, FLOOR_LOG)), axis=1)
        for side in sides:
            pltpu.matmul_acc_lhs(
                gathered[side][group], pair, load_staged_rhs=None if group else 0
            )

    load_pick()
    for group in range(groups):
        gather(group, jnp.log2(state[group * tall : (group + 1) * tall, :]))
    load_spread()

    def advance(step, carry):
        for group in range(groups):
            block = slice(group * tall, (group + 1) * tall)
            for side in sides:
                logs = pltpu.matmul_pop(gathered[side][group]) + log_rates[side, block, :]
                high, low = halves(jnp.exp2(logs))
                pltpu.matmul_acc_lhs(
                    scattered[side][group], high, load_staged_rhs=None if group else 1
                )
                pltpu.matmul_acc_lhs(scattered[side][group], low)
            if group == 0:
                load_spread()
        load_pick()
        for group in range(groups):
            block = slice(group * tall, (group + 1) * tall)
            total = pltpu.matmul_pop(scattered[0][group]) + pltpu.matmul_pop(scattered[1][group])
            current, count = state[block, :], number[block, :]
            above = count * current + total[:, :species]
            below = count + total[:, species:] * (1.0 / jnp.maximum(current, FLOOR))
            gather(group, jnp.log2(above) - jnp.log2(below))
            state[block, :] = jnp.where(count > step.astype(jnp.float32), above / below, current)
        return carry

    lax.fori_loop(0, MOST_SUBSTEPS, advance, 0)
    depart()
    for side in sides:
        for group in range(groups):
            pltpu.matmul_pop(gathered[side][group])
        pltpu.matmul_acc_lhs(
            scattered[side][0], jnp.zeros((tall, 2 * species), jnp.bfloat16), load_staged_rhs=1
        )
        pltpu.matmul_pop(scattered[side][0])


def whole_kernel(bands, devices, *refs):
    sources, out = refs[:10], refs[10]
    amounts, anomaly, solar, counts, speed, response, photo, recipe, east, north = held = refs[11:21]
    log_rates, pick, spread, state, number, warmth, arrived, packed = refs[21:29]
    move_refs = refs[29:]
    width = warmth.shape[0]
    cells, species = state.shape
    levels = cells // width

    copies = [
        pltpu.make_async_copy(source, here, arrived.at[index])
        for index, (source, here) in enumerate(zip(sources, held))
    ]
    for copy in copies[7:] + copies[:7]:
        copy.start()
    signal_peers(bands, devices)
    copies[7].wait()
    ids = lax.broadcasted_iota(jnp.int32, (species, species), 0)
    for chunk in range(4):
        part = pl.ds(chunk * species, species)
        hits = [(recipe[row : row + 1, part] == ids).astype(jnp.float32) for row in range(4)]
        taking, giving = hits[0] + hits[1], hits[2] + hits[3]
        side, spot = chunk // 2, chunk % 2 * species
        for copy in range(2):
            pick[side, copy * species : (copy + 1) * species, spot : spot + species] = (
                taking.astype(jnp.bfloat16)
            )
        spread[side, spot : spot + species, :] = jnp.concatenate(
            [jnp.transpose(giving), jnp.transpose(taking)], axis=1
        ).astype(jnp.bfloat16)
    for copy in copies[1:7] + copies[8:]:
        copy.wait()
    rows, columns, _ = anomaly.shape
    for row in range(rows):
        warmth[row * columns : (row + 1) * columns, :] = anomaly[row]
    place = lax.broadcasted_iota(jnp.int32, (width, species), 0)
    sunlight = jnp.zeros((width, species), jnp.float32)
    count = jnp.zeros((width, species), jnp.int32)
    for column in range(width):
        here = place == column
        spot = (column // columns, column % columns)
        sunlight = jnp.where(here, solar[spot], sunlight)
        count = jnp.where(here, counts[spot], count)
    count = count.astype(jnp.float32)
    for level in range(levels):
        block = pl.ds(level * width, width)
        heat = jnp.broadcast_to(warmth[:, level : level + 1], (width, species))
        for chunk in range(4):
            part = pl.ds(chunk * species, species)
            log_rates[chunk // 2, block, chunk % 2 * species : (chunk % 2 + 1) * species] = jnp.log2(
                speed[:, part] * jnp.exp(response[:, part] * heat) + photo[:, part] * sunlight
            )
        number[block, :] = count
    copies[0].wait()
    for level in range(levels):
        state[pl.ds(level * width, width), :] = amounts[pl.ds(level, width, stride=levels), :]

    wind_out, wind_in, send_wind, recv_wind = move_refs[3], move_refs[4], move_refs[10], move_refs[11]
    longitudes = east.shape[2]
    wind_out[...] = jnp.zeros_like(wind_out)
    wind_out[0:rows, 0:longitudes] = east[0]
    wind_out[rows : 2 * rows, 0:longitudes] = north[0]
    wind_in[lax.axis_index("lat")] = wind_out[...]

    inbox, send_there, recv_there = move_refs[0], move_refs[8], move_refs[9]
    band, home = lax.axis_index("lat"), lax.axis_index("lon")
    first = 3 * devices // 4
    falling = [step % devices for step in range(first + devices, first, -1)]

    def depart():
        half = species // 2
        near = lax.broadcasted_iota(jnp.int32, (width // 2, species), 1) < half
        for level in range(levels):
            front = state[pl.ds(level * width, width // 2), :]
            behind = state[pl.ds(level * width + width // 2, width // 2), :]
            packed[2 * level] = jnp.where(near, front, pltpu.roll(behind, half, 1))
            packed[2 * level + 1] = jnp.where(near, pltpu.roll(front, half, 1), behind)
        pl.semaphore_wait(pltpu.get_barrier_semaphore(), bands * devices - 1)
        for copy in wind_copies(bands, devices, wind_out, wind_in, send_wind, recv_wind):
            copy.start()
        for dy, dl in others(bands, devices, falling):
            device = peer(bands, devices, dy, dl)
            remote(
                packed.at[device[1] * bands + device[0]], inbox.at[band * devices + home],
                send_there.at[0], recv_there.at[0], device,
            ).start()
        inbox[band * devices + home] = packed[home * bands + band]

    groups = cells // 32
    pl.run_scoped(
        functools.partial(substeps, groups, depart, state, number, log_rates, pick, spread),
        *[
            pltpu.ACC(side)((32, 2 * species), jnp.float32)
            for use in range(2)
            for side in range(2)
            for group in range(groups)
        ],
    )

    move_kernel(bands, devices, rows, longitudes, packed, out, *move_refs)


def react_and_advect(operands):
    bands, devices = lax.axis_size("lat"), lax.axis_size("lon")
    cells, species = operands[0].shape
    rows, columns, levels = operands[1].shape
    longitudes = operands[8].shape[2]
    lats, extent, count = bands * rows, longitudes // 2, rows * columns // 2
    wide = -(-longitudes // 128) * 128
    held = [
        (pltpu.SMEM if index in (2, 3) else pltpu.VMEM)(operand.shape, operand.dtype)
        for index, operand in enumerate(operands)
    ]
    semaphores = pltpu.SemaphoreType.DMA((1,))
    wind_semaphores = pltpu.SemaphoreType.DMA((bands,))
    box = pltpu.VMEM((bands * devices, count, species), jnp.float32)
    exchanged = pltpu.VMEM((levels * bands, count, species), jnp.float32)
    wrapped = pltpu.VMEM((lats, extent + 16, species), jnp.float32)
    table = pltpu.VMEM((2, 2 * species, 2 * species), jnp.bfloat16)
    field = pltpu.VMEM((cells, species), jnp.float32)
    return pl.pallas_call(
        functools.partial(whole_kernel, bands, devices),
        out_shape=jax.ShapeDtypeStruct((cells, species), jnp.float32),
        in_specs=[pl.BlockSpec(memory_space=pltpu.HBM)] * len(operands),
        out_specs=pl.BlockSpec(memory_space=pltpu.VMEM),
        scratch_shapes=[
            *held,
            pltpu.VMEM((2, cells, 2 * species), jnp.float32), table, table, field, field,
            pltpu.VMEM((rows * columns, levels), jnp.float32),
            pltpu.SemaphoreType.DMA((len(operands),)), exchanged,
            box, box, exchanged,
            pltpu.VMEM((2 * rows, wide), jnp.float32),
            pltpu.VMEM((bands, 2 * rows, wide), jnp.float32),
            pltpu.VMEM((2, lats, 3, extent, species), jnp.float32), wrapped, wrapped,
            semaphores, semaphores, wind_semaphores, wind_semaphores, semaphores, semaphores,
        ],
        compiler_params=pltpu.CompilerParams(
            collective_id=0, has_side_effects=True, vmem_limit_bytes=32 << 20,
        ),
    )(*[pltpu.with_memory_space_constraint(operand, pltpu.HBM) for operand in operands])


def per_device(
    species_amounts,
    thermal_anomaly,
    solar_flux_factor,
    inner_iterations,
    reference_speed,
    thermal_response,
    photo_breakup,
    reaction_recipe,
    eastward_wind_ratio,
    northward_wind_ratio,
):
    rows, columns, levels, species = species_amounts.shape
    devices = lax.axis_size("lon")
    longitudes = eastward_wind_ratio.shape[2]
    reactions = reaction_recipe.shape[1]
    operands = (
        species_amounts.reshape(-1, species), thermal_anomaly, solar_flux_factor,
        inner_iterations, reference_speed.reshape(1, -1), thermal_response.reshape(1, -1),
        photo_breakup.reshape(1, -1), reaction_recipe,
    )
    paired = lax.axis_size("lat") == 2 and levels == devices and rows % 2 == 0
    tabled = species == 128 and reactions == 4 * species and rows * columns % 16 == 0
    if paired and tabled and devices % 2 == 0 and longitudes <= 128:
        moved = react_and_advect((*operands, eastward_wind_ratio, northward_wind_ratio))
        return moved.reshape(species_amounts.shape)
    settled_columns = react(operands).reshape(species_amounts.shape)
    lat_rows = species_amounts.shape[0]
    row_ids = lax.axis_index("lat") * lat_rows + lax.broadcasted_iota(
        jnp.int32, (lat_rows, 1, 1, 1), 0
    )
    carried_quantity = lax.all_to_all(
        settled_columns, "lon", split_axis=2, concat_axis=1, tiled=True
    )
    east_faces = jnp.transpose(eastward_wind_ratio, (1, 2, 0))[..., None]
    south_faces = jnp.where(
        row_ids > 0, jnp.transpose(northward_wind_ratio, (1, 2, 0))[..., None], 0.0
    )
    east_pad = wrap_pad(east_faces, 1)
    for sweep_index in range(ADV_STEPS):
        carried_quantity = flux_sweep(
            wrap_pad(carried_quantity, 1), east_pad, 1, carried_quantity.shape[1]
        )
        rimmed, south_pad = (
            with_halo(carried_quantity, (("lat", 0),), 3),
            with_halo(south_faces, (("lat", 0),), 3),
        )
        carried_quantity = flux_sweep(rimmed, south_pad, 0, lat_rows)
    return lax.all_to_all(carried_quantity, "lon", split_axis=1, concat_axis=2, tiled=True)


def solution(mesh):
    return jax.shard_map(
        per_device,
        mesh=mesh,
        in_specs=(
            P("lat", "lon", None, None),
            P("lat", "lon", None),
            P("lat", "lon"),
            P("lat", "lon"),
            P(),
            P(),
            P(),
            P(),
            P("lon", "lat", None),
            P("lon", "lat", None),
        ),
        out_specs=P("lat", "lon", None, None),
        check_vma=False,
    )
```
